32 devices in a mesh: grp: 4 (over z), seq: 8 (over y, x, core).
Axes of the slice: x: 2, y: 2, z: 4, core: 2. Of those that a mesh axis runs over, the one named last changes fastest.
Arguments:
- tokens: bfloat16 [16, 1024, 512], P('grp', 'seq'), may hold values from -6 to 6
- segments: int32 [16, 1024], P('grp', 'seq'), may hold values from 0 to 7, never falling along the last dimension, each value on 1 to 256 neighbouring positions
- cotangent: float32 [16, 1024, 512], P('grp', 'seq'), may hold values from -6 to 6
- first_gain: bfloat16 [512], P('seq'), may hold values from 0.099609375 to 1.8984375
- value_weight: bfloat16 [512, 1024], P('seq'), may hold values from -0.25 to 0.25
- value_bias: bfloat16 [1024], P('seq'), may hold values from -3 to 3
- decay_alpha: bfloat16 [512, 16], P('seq'), may hold values from -5 to -1
- decay_delta: bfloat16 [512, 16], P('seq'), may hold values from -4 to -1
- decay_beta: bfloat16 [512, 16], P('seq'), may hold values from -4 to 4
- decay_eta: bfloat16 [512, 16], P('seq'), may hold values from -1.5 to 1.5
- skip_omega: bfloat16 [512], P('seq'), may hold values from -4 to 4
- mix_weight: bfloat16 [512, 2176], P('seq'), may hold values from -0.25 to 0.25
- mix_bias: bfloat16 [2176], P('seq'), may hold values from -3 to 3
- latent_gains: bfloat16 [2, 128], P(None, 'seq'), may hold values from -3 to 3
- query_offset: bfloat16 [128], P('seq'), may hold values from -4 to 4
- position_bias: bfloat16 [128], P('seq'), may hold values from -4 to 4
- attend_weight: bfloat16 [1024, 512], P('seq'), may hold values from -0.75 to 0.75
- second_gain: bfloat16 [512], P('seq'), may hold values from 0.099609375 to 1.8984375
- up_weight: bfloat16 [512, 1024], P('seq'), may hold values from -0.25 to 0.25
- up_bias: bfloat16 [1024], P('seq'), may hold values from -3 to 3
- down_weight: bfloat16 [1024, 512], P('seq'), may hold values from -0.1875 to 0.1875
- down_bias: bfloat16 [512], P('seq'), may hold values from -3 to 3
Outputs:
- layer_output: float32 [16, 1024, 512], P('grp', 'seq')
- tokens_grad: float32 [16, 1024, 512], P('grp', 'seq')
- first_gain_grad: float32 [512], P('seq')
- value_weight_grad: float32 [512, 1024], P('seq')
- value_bias_grad: float32 [1024], P('seq')
- decay_alpha_grad: float32 [512, 16], P('seq')
- decay_delta_grad: float32 [512, 16], P('seq')
- decay_beta_grad: float32 [512, 16], P('seq')
- decay_eta_grad: float32 [512, 16], P('seq')
- skip_omega_grad: float32 [512], P('seq')
- mix_weight_grad: float32 [512, 2176], P('seq')
- mix_bias_grad: float32 [2176], P('seq')
- latent_gains_grad: float32 [2, 128], P(None, 'seq')
- query_offset_grad: float32 [128], P('seq')
- position_bias_grad: float32 [128], P('seq')
- attend_weight_grad: float32 [1024, 512], P('seq')
- second_gain_grad: float32 [512], P('seq')
- up_weight_grad: float32 [512, 1024], P('seq')
- up_bias_grad: float32 [1024], P('seq')
- down_weight_grad: float32 [1024, 512], P('seq')
- down_bias_grad: float32 [512], P('seq')
The draws below stay inside these ranges and needn't reach their ends.
Inputs may be any that keep to these rules, and one draw needn't show every extreme that they name: `segments`: along each sequence the segment numbers never fall; each number covers 1 to 256 consecutive tokens, and one covers exactly 256.
All inputs are finite; a program needn't handle non-finite values.
Results may differ from the reference program's by a relative error of at most 0.028.
Values may be sent and summed in bfloat16 or wider, within the bound.
No kernel may reach another device: no remote copies, remote signals or barrier semaphores. Data moves between devices by JAX's collectives and lax.ppermute only.
A program may use at most 192 MiB of HBM per device.

```python
import math
import jax
import jax.numpy as jnp
import numpy as np
from jax import lax

D = 512
Z = 128
V = 1024
H = 16
FF = 1024
SPAN = 128
SEQS = 4
LEN = 1024
ROWS = 16
N_GRP = 4
N_SEQ = 8


def block_scale(own_key, dims, shards, smallest, largest):
    loudness, own = 1.0, jax.random.fold_in(own_key, 6)
    for position, blocks in shards:
        steps = jnp.exp(jax.random.uniform(jax.random.fold_in(own, position), (blocks,), jnp.float32, smallest / len(shards), largest / len(shards)))
        loudness = loudness * jnp.repeat(steps, dims[position] // blocks).reshape([-1 if axis == position else 1 for axis in range(len(dims))])
    return loudness


def split_up(count, total, most, slope):
    weights = [(1 << 20) // math.isqrt(standing ** slope) + 1 for standing in range(2, count + 1)]
    rest, holding = total - most - (count - 1), [1] * (count - 1)
    while rest > 0:
        candidates = [i for i in range(count - 1) if holding[i] < most]
        mass, remaining = sum([weights[i] for i in candidates]), rest
        for i in candidates:
            more = min(most - holding[i], max(1, remaining * weights[i] // mass), rest)
            holding[i] = holding[i] + more
            rest = rest - more
    return np.array([most] + holding)


def uneven_parts(rng, count, total, most, lean):
    if count == 2:
        one = jax.random.randint(rng, (), max(1, total - most), min(most, total - 1) + 1)
        return jnp.stack([one, total - one])
    tallies = jnp.asarray(split_up(count, total, most, lean), jnp.int32)
    pairs = (count - 1) // 2
    donor, receiver = tallies[1:1 + 2 * pairs:2], tallies[2:2 + 2 * pairs:2]
    margin = jnp.minimum(donor - 1, most - receiver)
    shifted = jax.random.randint(jax.random.fold_in(rng, 1), (pairs,), 0, 1 << 20) % (margin + 1)
    tallies = tallies.at[1:1 + 2 * pairs:2].set(donor - shifted).at[2:2 + 2 * pairs:2].set(receiver + shifted)
    return tallies[jax.random.permutation(jax.random.fold_in(rng, 2), count)]


def normal_values(key, extent, spread, limit, pieces=(), kind=jnp.bfloat16):
    values = jax.random.normal(key, extent, jnp.float32) * spread
    if len(pieces) > 0:
        values = block_scale(key, extent, pieces, -0.22, 0.18) * values
    return jnp.clip(values, min=-limit, max=limit).astype(kind)


def setup_inputs(seed: int = 0) -> dict:
    streams_of = jax.random.split(jax.random.key(seed), 23)
    return {
        "tokens": normal_values(streams_of[0], (ROWS, LEN, D), 1.0, 6.0, ((0, 4), (1, 8))),
        "segments": jax.vmap(lambda own: jnp.searchsorted(jnp.cumsum(uneven_parts(own, N_SEQ, LEN, LEN // 4, 2)), jnp.arange(LEN), side="right"))(jax.random.split(streams_of[1], ROWS)).reshape((ROWS, LEN)).astype(jnp.int32),
        "cotangent": normal_values(streams_of[2], (ROWS, LEN, D), 1.0, 6.0, ((0, 4), (1, 8)), jnp.float32),
        "first_gain": jnp.clip(1.0 + 0.18 * jax.random.normal(streams_of[3], (D,), jnp.float32), 0.099609375, 1.8984375).astype(jnp.bfloat16),
        "value_weight": normal_values(streams_of[4], (D, V), D ** -0.5, 0.25, ((0, 8),)),
        "value_bias": normal_values(streams_of[5], (V,), 0.5, 3.0, ((0, 8),)),
        "decay_alpha": jnp.clip(-5.0 + 4.0 * jax.random.uniform(streams_of[6], (D, H), jnp.float32) ** block_scale(streams_of[6], (D, H), ((0, 8),), -0.2, 0.2), -5.0, -1.0).astype(jnp.bfloat16),
        "decay_delta": jnp.clip(-4.0 + 3.0 * jax.random.uniform(streams_of[7], (D, H), jnp.float32) ** block_scale(streams_of[7], (D, H), ((0, 8),), -0.2, 0.2), -4.0, -1.0).astype(jnp.bfloat16),
        "decay_beta": normal_values(streams_of[8], (D, H), 1.0, 4.0, ((0, 8),)),
        "decay_eta": normal_values(streams_of[9], (D, H), H ** -0.5, 1.5, ((0, 8),)),
        "skip_omega": normal_values(streams_of[10], (D,), 1.0, 4.0, ((0, 8),)),
        "mix_weight": normal_values(streams_of[11], (D, 2 * D + Z + V), D ** -0.5, 0.25, ((0, 8),)),
        "mix_bias": normal_values(streams_of[12], (2 * D + Z + V,), 0.5, 3.0, ((0, 8),)),
        "latent_gains": normal_values(streams_of[13], (2, Z), 1.0, 3.0, ((1, 8),)),
        "query_offset": normal_values(streams_of[14], (Z,), 1.0, 4.0, ((0, 8),)),
        "position_bias": normal_values(streams_of[15], (SPAN,), 1.0, 4.0, ((0, 8),)),
        "attend_weight": normal_values(streams_of[16], (V, D), (V // 16) ** -0.5, 0.75, ((0, 8),)),
        "second_gain": jnp.clip(1.0 + 0.18 * jax.random.normal(streams_of[17], (D,), jnp.float32), 0.099609375, 1.8984375).astype(jnp.bfloat16),
        "up_weight": normal_values(streams_of[18], (D, FF), D ** -0.5, 0.25, ((0, 8),)),
        "up_bias": normal_values(streams_of[19], (FF,), 0.5, 3.0, ((0, 8),)),
        "down_weight": normal_values(streams_of[20], (FF, D), FF ** -0.5, 0.1875, ((0, 8),)),
        "down_bias": normal_values(streams_of[21], (D,), 0.5, 3.0, ((0, 8),)),
    }


@jax.custom_vjp
def low(v):
    return lax.optimization_barrier(v.astype(jnp.bfloat16)).astype(jnp.float32)

@jax.custom_vjp
def low_back(v):
    return v

def low_keep(v):
    return (low(v), None)

def low_pass(kept, grad):
    return (grad,)

def back_keep(v):
    return (v, None)

def back_low(kept, grad):
    return (low(grad),)
low.defvjp(low_keep, low_pass)
low_back.defvjp(back_keep, back_low)
EPSILON = 1e-06
HIGH = lax.Precision.HIGHEST

def matmul(left, right):
    return jnp.einsum('...k,kn->...n', left, right, precision=HIGH, preferred_element_type=jnp.float32)

def rms_norm(values, gain):
    return values * lax.rsqrt(lax.optimization_barrier(jnp.mean(values * values, axis=-1, keepdims=True)) + EPSILON) * gain

def smooth_layer(normed, segment, alpha, delta, beta, eta):
    rate = jax.nn.sigmoid(alpha)
    decay = 1.0 - rate * jax.nn.sigmoid(delta)
    inflow = rate * beta
    continued = (segment[:, 1:] == segment[:, :-1]).astype(jnp.float32)
    continued = jnp.concatenate([jnp.zeros((segment.shape[0], 1), jnp.float32), continued], axis=1)

    def advance(state, inputs):
        column, flag = inputs
        state = state * decay * flag[:, None, None] + column[:, :, None] * inflow
        return (state, lax.optimization_barrier(jnp.sum(state * eta, axis=-1)))
    start = jnp.zeros((normed.shape[0], normed.shape[2], alpha.shape[1]), jnp.float32)
    _, series = lax.scan(advance, start, (jnp.swapaxes(normed, 0, 1), jnp.swapaxes(continued, 0, 1)))
    return jnp.swapaxes(series, 0, 1)

def block_attention(query, key, value, segment, position_bias):
    rows, length, _ = query.shape
    count = length // SPAN
    query = query.reshape(rows, count, SPAN, -1)
    key = key.reshape(rows, count, SPAN, -1)
    value = value.reshape(rows, count, SPAN, -1)
    scores = low_back(jnp.einsum('rnid,rnjd->rnij', query, key, precision=HIGH))
    places = jnp.arange(SPAN).astype(jnp.int32)
    offset = places[:, None] - places[None, :]
    table = position_bias[jnp.clip(offset, 0, SPAN - 1).astype(jnp.int32)]
    labels = segment.reshape(rows, count, SPAN)
    allowed = (offset >= 0)[None, None] & (labels[:, :, :, None] == labels[:, :, None, :])
    scores = jnp.where(allowed, scores + table, -1e+30)
    probs = low(jax.nn.softmax(scores, axis=-1))
    attended = low_back(jnp.einsum('rnij,rnjd->rnid', probs, value, precision=HIGH))
    return attended.reshape(rows, length, -1)

def layer_forward(tokens, segment, first_gain, value_weight, value_bias, decay_alpha, decay_delta, decay_beta, decay_eta, skip_omega, mix_weight, mix_bias, latent_gains, query_offset, position_bias, attend_weight, second_gain, up_weight, up_bias, down_weight, down_bias):
    normed = rms_norm(tokens, first_gain)
    value = low(jax.nn.silu(low_back(matmul(low(normed), value_weight)) + value_bias))
    smoothed = smooth_layer(normed, segment, decay_alpha, decay_delta, decay_beta, decay_eta)
    mixed = low(jax.nn.silu(smoothed + skip_omega * normed))
    base = low_back(matmul(mixed, mix_weight)) + mix_bias
    update = jax.nn.sigmoid(base[:, :, :D])
    latent = jax.nn.silu(base[:, :, D:D + Z])
    reset = jax.nn.silu(base[:, :, D + Z:D + Z + V])
    extra = base[:, :, D + Z + V:]
    query = low((latent * latent_gains[0] + query_offset) * Z ** (-0.5))
    key = low(latent * latent_gains[1])
    attended = block_attention(query, key, value, segment, position_bias)
    candidate = jax.nn.silu(extra + low_back(matmul(low(attended * reset), attend_weight)))
    middle = tokens + update * (candidate - tokens)
    second = low(rms_norm(middle, second_gain))
    hidden = low(jax.nn.silu(low_back(matmul(second, up_weight)) + up_bias))
    return middle + low_back(matmul(hidden, down_weight)) + down_bias

def reference(tokens, segments, cotangent, first_gain, value_weight, value_bias, decay_alpha, decay_delta, decay_beta, decay_eta, skip_omega, mix_weight, mix_bias, latent_gains, query_offset, position_bias, attend_weight, second_gain, up_weight, up_bias, down_weight, down_bias):
    weights = (first_gain, value_weight, value_bias, decay_alpha, decay_delta, decay_beta, decay_eta, skip_omega, mix_weight, mix_bias, latent_gains, query_offset, position_bias, attend_weight, second_gain, up_weight, up_bias, down_weight, down_bias)
    weights = tuple((piece.astype(jnp.float32) for piece in weights))
    inputs = tokens.astype(jnp.float32).reshape(N_GRP, SEQS, LEN, D)
    labels = segments.reshape(N_GRP, SEQS, LEN)
    incoming = cotangent.astype(jnp.float32).reshape(N_GRP, SEQS, LEN, D)

    def one_group(totals, item):
        block, segment, upstream = item

        def forward(values, *params):
            return layer_forward(values, segment, *params)
        output, backward = jax.vjp(forward, block, *weights)
        grads = backward(upstream)
        totals = tuple((total + grad for total, grad in zip(totals, grads[1:])))
        return (totals, (output, grads[0]))
    zeros = tuple((jnp.zeros_like(piece) for piece in weights))
    totals, (outputs, token_grads) = lax.scan(one_group, zeros, (inputs, labels, incoming))
    return (outputs.reshape(ROWS, LEN, D), token_grads.reshape(ROWS, LEN, D), totals[0], totals[1], totals[2], totals[3], totals[4], totals[5], totals[6], totals[7], totals[8], totals[9], totals[10], totals[11], totals[12], totals[13], totals[14], totals[15], totals[16], totals[17], totals[18])
```

```python
from functools import partial

import jax
import jax.numpy as jnp
from jax import lax
from jax.experimental import pallas as pl
from jax.experimental.pallas import tpu as pltpu
from jax.sharding import PartitionSpec as P

EPSILON = 1e-06
F32 = jnp.float32
BF = jnp.bfloat16
TILE = 128
SUBS = 8
ROWS_SMALL = 88
NN = (((1,), (0,)), ((), ()))
NT = (((1,), (1,)), ((), ()))
TN = (((0,), (0,)), ((), ()))


def dot(a, b, dims=NN):
    return lax.dot_general(a, b, dims, preferred_element_type=F32)


def sig(v):
    return 0.5 * jnp.tanh(0.5 * v) + 0.5


def struct(shape, dtype):
    return jax.ShapeDtypeStruct(shape, dtype)


VM = pl.BlockSpec(memory_space=pltpu.VMEM)
HB = pl.BlockSpec(memory_space=pl.ANY)
PARAMS = pltpu.CompilerParams(vmem_limit_bytes=56 << 20)


def whole(body, outs, scratch=(), in_specs=None, n_in=None, name=None):
    return pl.pallas_call(
        body,
        out_shape=outs,
        in_specs=in_specs if in_specs is not None else [VM] * n_in,
        out_specs=jax.tree.map(lambda _: VM, outs),
        scratch_shapes=list(scratch),
        compiler_params=PARAMS,
        name=name,
    )


def tiles(m_size, n_size, tm, tn, fn):
    nm, nn = m_size // tm, n_size // tn

    def body(i, _):
        fn(pl.multiple_of((i % nm) * tm, tm), pl.multiple_of((i // nm) * tn, tn))
        return 0

    lax.fori_loop(0, nm * nn, body, 0)


def rows_loop(total, step, fn):
    def body(i, _):
        fn(pl.multiple_of(i * step, step))
        return 0

    lax.fori_loop(0, total // step, body, 0)


def ceil_div(a, b):
    return -(-a // b)


def spread(n, devices):
    return max(ceil_div((d * n) % TILE + n, TILE) for d in range(devices))


def place_kernel(flat_ref, dec_ref, out_ref, *, plan):
    me = lax.axis_index("seq")
    out_ref[...] = jnp.zeros_like(out_ref)
    held = dec_ref.shape[0]
    row = lax.broadcasted_iota(jnp.int32, (held, TILE), 0)
    lane = lax.broadcasted_iota(jnp.int32, (held, TILE), 1)
    pick = jnp.where(lane == row + (me * held) % TILE, 1.0, 0.0).astype(BF)
    out_ref[0 : dec_ref.shape[1], :] = dot(dec_ref[...], pick, TN)
    for at, off, n, nt in plan:
        low, high = off // TILE * TILE, ceil_div(off + n, TILE) * TILE
        values = jnp.broadcast_to(flat_ref[:, low:high].astype(F32), (SUBS, high - low)).astype(BF)
        row = lax.broadcasted_iota(jnp.int32, (high - low, nt * TILE), 0) - (off - low)
        lane = lax.broadcasted_iota(jnp.int32, (high - low, nt * TILE), 1)
        hit = (lane == row + (me * n) % TILE) & (row >= 0) & (row < n)
        moved = dot(values, jnp.where(hit, 1.0, 0.0).astype(BF))
        for j in range(nt):
            out_ref[at + j : at + j + 1, :] = moved[0:1, j * TILE : (j + 1) * TILE]


def assemble(src, low, high, n, total, devices):
    parts = [None] * ceil_div(total, TILE)
    for d in range(devices):
        t = d * n // TILE
        block = src[d, low:high, :]
        parts[t] = block if parts[t] is None else parts[t] + block
    return parts


def chunk_labels(lab_ref, steps):
    return lab_ref[pl.ds(0, SUBS, stride=steps), :], lab_ref[pl.ds(steps - 1, SUBS, stride=steps), :]


def lanes_of(t):
    return slice(t * TILE, (t + 1) * TILE)


def one_way(src_ref, lab_ref, ref_label, dk_ref, out_ref, dims, steps, width, reverse, unroll=8):
    for lt in range(width // TILE):
        lanes = lanes_of(lt)
        decay = [jnp.broadcast_to(dk_ref[h : h + 1, lanes], (SUBS, TILE)) for h in range(dims)]

        def step(i, state, lt=lt, decay=decay):
            state = list(state)
            for u in range(unroll):
                t = i * unroll + u
                if reverse:
                    t = steps - 1 - t
                x = src_ref[lt, pl.ds(t, SUBS, stride=steps), :]
                l = lab_ref[pl.ds(t, SUBS, stride=steps), :]
                x = jnp.where(l == ref_label, x, 0.0)
                state = [decay[h] * state[h] + x for h in range(dims)]
            return tuple(state)

        zero = jnp.zeros((SUBS, TILE), F32)
        final = lax.fori_loop(0, steps // unroll, step, (zero,) * dims)
        for h in range(dims):
            out_ref[h * SUBS : (h + 1) * SUBS, lanes] = final[h]


def norm_scale(x):
    return lax.rsqrt(jnp.mean(x * x, axis=-1, keepdims=True) + EPSILON)


def head_kernel(
    small_ref, tok_ref, seg_ref, pd_ref, pv_ref, pz_ref, pm_ref, dk_ref, nrm_ref, low_ref, lab_ref,
    fin_ref, msg_ref, scr_ref, *, devices, dims, nv, nm,
):
    tokens, width = tok_ref.shape
    seqs, length = seg_ref.shape
    steps = tokens // SUBS
    for t, part in enumerate(assemble(small_ref, 0, 72, width // devices, width, devices)):
        pd_ref[:, lanes_of(t)] = part
    for t, part in enumerate(assemble(small_ref, 72, 80, nv // devices, nv, devices)):
        pv_ref[:, lanes_of(t)] = part
    z = small_ref[0, 72:80, :]
    for d in range(1, devices):
        z = z + small_ref[d, 72:80, :]
    pz_ref[...] = z
    n = nm // devices
    cells = [None] * (nm // TILE)
    for d in range(devices):
        first, lane = divmod(d * n, TILE)
        for j in range(ceil_div(lane + n, TILE)):
            piece = small_ref[d, 80 + j : 81 + j, :]
            cells[first + j] = piece if cells[first + j] is None else cells[first + j] + piece
    for t, piece in enumerate(cells):
        pm_ref[:, lanes_of(t)] = jnp.broadcast_to(piece, (SUBS, TILE))

    rate = 1.0 / (1.0 + jnp.exp(-pd_ref[0:dims, :]))
    damping = 1.0 / (1.0 + jnp.exp(-pd_ref[dims : 2 * dims, :]))
    decay = 1.0 - rate * damping
    dk_ref[0:dims, :] = decay
    dk_ref[dims : 2 * dims, :] = pd_ref[3 * dims : 4 * dims, :] * rate * pd_ref[2 * dims : 3 * dims, :]
    power, k = decay, 1
    while k < steps:
        power, k = power * power, k * 2
    dk_ref[2 * dims : 3 * dims, :] = power

    gain = pd_ref[4 * dims : 4 * dims + 1, :]

    def norm(r):
        x = tok_ref[pl.ds(r, 64), :].astype(F32)
        y = x * norm_scale(x) * gain
        for t in range(width // TILE):
            nrm_ref[t, pl.ds(r, 64), :] = y[:, lanes_of(t)]
        low_ref[pl.ds(r, 64), :] = y.astype(BF)

    rows_loop(tokens, 64, norm)

    labels = seg_ref[...].astype(F32)
    row = lax.broadcasted_iota(jnp.int32, (length, length), 0)
    col = lax.broadcasted_iota(jnp.int32, (length, length), 1)
    for s in range(seqs):
        diagonal = jnp.where(row == col, labels[s : s + 1, :], 0.0).astype(BF)
        lab_ref[s * length : (s + 1) * length, :] = dot(diagonal, jnp.ones((length, TILE), BF))

    first, last = chunk_labels(lab_ref, steps)
    one_way(nrm_ref, lab_ref, last, dk_ref, fin_ref, dims, steps, width, False)
    through = (first == last) & (first == pltpu.roll(last, 1, 0))
    for lt in range(width // TILE):
        lanes = lanes_of(lt)
        for h in range(dims):
            own = fin_ref[h * SUBS : (h + 1) * SUBS, lanes]
            before = pltpu.roll(own, 1, 0) * power[h : h + 1, lanes]
            scr_ref[h * SUBS : (h + 1) * SUBS, :] = own + jnp.where(through, before, 0.0)
        half = SUBS // seqs
        msg_ref[0 : dims * seqs, lanes] = scr_ref[
            pl.ds(half - 1, dims * seqs, stride=half), :
        ].astype(BF)
        ends = lab_ref[pl.ds(length - 1, seqs, stride=length), :]
        tail = jnp.concatenate([ends, jnp.zeros((16 - seqs, TILE), F32)], axis=0)
        msg_ref[dims * seqs : dims * seqs + 16, lanes] = tail.astype(BF)


def entering(msgs, own_label, even, scr_refs, lab_scr, start, dims, seqs, power):
    half = SUBS // seqs
    gates = []
    for m, scr in zip(msgs, scr_refs):
        scr[pl.ds(start, dims * seqs, stride=half), :] = m[0 : dims * seqs, :].astype(F32)
        tail = m[dims * seqs : dims * seqs + 16, :].astype(F32)
        lab_scr[pl.ds(start, seqs, stride=half), :] = tail[0:seqs, :]
        gates.append(even & (lab_scr[...] == own_label))
    result = []
    for h in range(dims):
        total, reach = None, None
        for gate, scr in zip(gates, scr_refs):
            part = jnp.where(gate, scr[h * SUBS : (h + 1) * SUBS, :], 0.0)
            if total is None:
                total, reach = part, power[h : h + 1, :] * power[h : h + 1, :]
                far = reach
            else:
                total, far = total + part * far, far * reach
        result.append(total)
    return result


def scan_kernel(*refs, reach, dims, seqs):
    nrm_ref, lab_ref, dk_ref, pd_ref, fin_ref = refs[:5]
    msgs = refs[5 : 5 + reach]
    z_ref, mlow_ref, sp_ref = refs[5 + reach : 8 + reach]
    ent_ref, lab_scr, ys_ref = refs[8 + reach : 11 + reach]
    scr_refs = refs[11 + reach :]
    tokens = nrm_ref.shape[0]
    steps = tokens // SUBS
    half = SUBS // seqs
    first, last = chunk_labels(lab_ref, steps)
    place = lax.broadcasted_iota(jnp.int32, (SUBS, TILE), 0)
    even = place % half == 0
    power = dk_ref[2 * dims : 3 * dims, :]
    arrivals = entering(msgs, first, even, scr_refs, lab_scr, 0, dims, seqs, power)
    inside = first == last
    joined = first == pltpu.roll(last, 1, 0)
    for h in range(dims):
        e = arrivals[h]
        own = fin_ref[h * SUBS : (h + 1) * SUBS, :]
        onward = pltpu.roll(own + jnp.where(inside, e * power[h : h + 1, :], 0.0), 1, 0)
        ent_ref[h * SUBS : (h + 1) * SUBS, :] = jnp.where(even, e, jnp.where(joined, onward, 0.0))
    decay = [jnp.broadcast_to(dk_ref[h : h + 1, :], (SUBS, TILE)) for h in range(dims)]
    weight = [jnp.broadcast_to(dk_ref[dims + h : dims + h + 1, :], (SUBS, TILE)) for h in range(dims)]
    unroll = 4

    def step(i, carry):
        before, state = carry[0], list(carry[1:])
        for u in range(unroll):
            t = i * unroll + u
            x = nrm_ref[pl.ds(t, SUBS, stride=steps), :]
            l = lab_ref[pl.ds(t, SUBS, stride=steps), :]
            same = l == before
            before = l
            sums = [None] * 4
            for h in range(dims):
                kept = jnp.where(same, state[h], 0.0)
                sp_ref[t, h * SUBS : (h + 1) * SUBS, :] = kept
                state[h] = decay[h] * kept + x
                term = weight[h] * state[h]
                sums[h % 4] = term if sums[h % 4] is None else sums[h % 4] + term
            ys_ref[pl.ds(t, SUBS, stride=steps), :] = (sums[0] + sums[1]) + (sums[2] + sums[3])
        return (before,) + tuple(state)

    start = tuple(ent_ref[h * SUBS : (h + 1) * SUBS, :] for h in range(dims))
    lax.fori_loop(0, steps // unroll, step, (first,) + start)
    omega = pd_ref[4 * dims + 1 : 4 * dims + 2, :]

    def gate(r):
        v = ys_ref[pl.ds(r, 64), :] + omega * nrm_ref[pl.ds(r, 64), :]
        z_ref[pl.ds(r, 64), :] = v
        mlow_ref[pl.ds(r, 64), :] = (v * sig(v)).astype(BF)

    rows_loop(tokens, 64, gate)


def load_weights(pieces, dst, sem, rows, start, cols, place):
    me = lax.axis_index("seq")
    copies = []
    for k, piece in enumerate(pieces):
        p = me ^ k
        copies.append(
            pltpu.make_async_copy(
                piece.at[pl.ds(start, rows), pl.ds(0, cols)],
                dst.at[pl.ds(pl.multiple_of(p * rows, rows), rows), pl.ds(0, cols)],
                sem.at[place, k],
            )
        )
    for c in copies:
        c.start()
    return copies


def split_sizes(width, latent, nv):
    return {"u": 0, "l": width, "r": width + latent, "e": width + latent + nv}


def front_kernel(*refs, devices):
    pieces = refs[:devices]
    nlow, mlow, pv, pm, pz, lab, seg = refs[devices : devices + 7]
    vlow, dval, upd, ext, lat, rs, ad, glow, probs, qlow, klow = refs[devices + 7 : devices + 18]
    w, res, sem = refs[devices + 18 :]
    tokens, width = nlow.shape
    nv = vlow.shape[1]
    zw = lat.shape[1]
    seqs, length = seg.shape
    rows = width // devices
    copies = load_weights(pieces, w, sem, rows, 0, w.shape[1], 0)
    for c in copies:
        c.wait()

    def value(m, n):
        v = dot(nlow[pl.ds(m, 256), :], w[:, pl.ds(n, 256)]) + pv[0:1, pl.ds(n, 256)]
        s = sig(v)
        vlow[pl.ds(m, 256), pl.ds(n, 256)] = (v * s).astype(BF)
        dval[pl.ds(m, 256), pl.ds(n, 256)] = (s * (1.0 + v * (1.0 - s))).astype(BF)

    tiles(tokens, nv, 256, 256, value)
    at = split_sizes(width, zw, nv)

    def base(m, n, start, size):
        cols = pl.multiple_of(start + n, TILE)
        wcols = pl.multiple_of(nv + start + n, TILE)
        return dot(mlow[pl.ds(m, 256), :], w[:, pl.ds(wcols, size)]) + pm[0:1, pl.ds(cols, size)]

    def update(m, n):
        upd[pl.ds(m, 256), pl.ds(n, 256)] = sig(base(m, n, at["u"], 256))

    tiles(tokens, width, 256, 256, update)

    def extra(m, n):
        ext[pl.ds(m, 256), pl.ds(n, 256)] = base(m, n, at["e"], 256)

    tiles(tokens, width, 256, 256, extra)

    def reset(m, n):
        res[pl.ds(m, 256), pl.ds(n, 256)] = base(m, n, at["r"], 256)

    tiles(tokens, nv, 256, 256, reset)

    def latent(m, n):
        v = base(m, n, at["l"], zw)
        lat[pl.ds(m, 256), :] = v
        y = v * sig(v)
        qlow[pl.ds(m, 256), :] = ((y * pz[2:3, :] + pz[4:5, :]) * zw ** (-0.5)).astype(BF)
        klow[pl.ds(m, 256), :] = (y * pz[3:4, :]).astype(BF)

    tiles(tokens, zw, 256, zw, latent)

    row = lax.broadcasted_iota(jnp.int32, (length, length), 0)
    col = lax.broadcasted_iota(jnp.int32, (length, length), 1)
    flip = jnp.where((row + col) % length == 0, 1.0, 0.0).astype(BF)
    bias = dot(pz[...].astype(BF), flip)[5:6, :]
    table = pltpu.roll(jnp.broadcast_to(bias, (length, length)), 0, 1, stride=1, stride_axis=0)
    causal = row >= col

    def attend(r):
        here = pl.ds(r, length)
        label_j = seg[pl.ds(r // length, 1), :].astype(F32)
        allowed = causal & (lab[here, :] == label_j)
        scores = dot(qlow[here, :], klow[here, :], NT) + table
        scores = jnp.where(allowed, scores, -1e30)
        weights = jnp.exp(scores - jnp.max(scores, axis=-1, keepdims=True))
        prob = weights / jnp.sum(weights, axis=-1, keepdims=True)
        probs[here, :] = prob
        plow = prob.astype(BF)
        for n in range(nv // 256):
            cols = slice(n * 256, (n + 1) * 256)
            a = dot(plow, vlow[here, cols])
            v = res[here, cols]
            s = sig(v)
            y = v * s
            rs[here, cols] = y.astype(BF)
            ad[here, cols] = (a * (s * (1.0 + v * (1.0 - s)))).astype(BF)
            glow[here, cols] = (a * y).astype(BF)

    rows_loop(tokens, length, attend)


def column_sum(ref, row, cols, values, first):
    total = jnp.sum(values, axis=0, keepdims=True)

    @pl.when(first)
    def _():
        ref[row : row + 1, cols] = total

    @pl.when(jnp.logical_not(first))
    def _():
        ref[row : row + 1, cols] = ref[row : row + 1, cols] + total


def put_pieces(src, own, sib, devices, depth, rows, at, src_cols, cols):
    me = lax.axis_index("seq")
    for p in range(devices):
        k = me ^ p
        kc = k // 2

        def put(dst, p=p, kc=kc):
            for z in range(depth):
                begin = (p * depth + z) * rows
                dst[kc, z, at : at + rows, cols] = src[begin : begin + rows, src_cols].astype(BF)

        pl.when(k % 2 == 0)(partial(put, own))
        pl.when(k % 2 == 1)(partial(put, sib))


def middle_kernel(*refs, devices, depth, dims):
    pieces = refs[:devices]
    tok, cot, upd, ext, rs, ad, glow, pd, pv = refs[devices : devices + 9]
    out, gin, attg, blu, blre, v512, v1024, own, sib = refs[devices + 9 : devices + 18]
    w2, wup, proj, mid, slow, dup, hlow, clow, ulow, elow, gmid, grad, sem = refs[devices + 18 :]
    tokens, width = tok.shape
    nv = rs.shape[1]
    nf = dup.shape[1]
    rows2, rows1 = nv // devices, width // devices
    copies = load_weights(pieces, w2, sem, rows2, 0, 2 * width, 0)
    copies += load_weights(pieces, wup, sem, rows1, rows2, nf, 1)
    for c in copies:
        c.wait()
    down = pl.ds(width, width)

    def project(m, n):
        proj[pl.ds(m, 256), pl.ds(n, 256)] = dot(glow[pl.ds(m, 256), :], w2[:, pl.ds(n, 256)])

    tiles(tokens, width, 256, 256, project)
    gain = pd[4 * dims + 2 : 4 * dims + 3, :]

    def blend(r):
        here = pl.ds(r, 64)
        x = tok[here, :].astype(F32)
        pre = ext[here, :] + proj[here, :]
        s = sig(pre)
        m = x + upd[here, :] * (pre * s - x)
        mid[here, :] = m
        slow[here, :] = (m * norm_scale(m) * gain).astype(BF)

    rows_loop(tokens, 64, blend)

    def up(m, n):
        v = dot(slow[pl.ds(m, 256), :], wup[:, pl.ds(n, 256)]) + pv[1:2, pl.ds(n, 256)]
        s = sig(v)
        hlow[pl.ds(m, 256), pl.ds(n, 256)] = (v * s).astype(BF)
        dup[pl.ds(m, 256), pl.ds(n, 256)] = s * (1.0 + v * (1.0 - s))

    tiles(tokens, nf, 256, 256, up)

    def down_forward(m, n):
        at, cols = pl.ds(m, 256), pl.ds(n, 256)
        y = dot(hlow[at, :], w2[:, pl.ds(pl.multiple_of(width + n, 256), 256)])
        out[at, cols] = mid[at, cols] + y + pd[4 * dims + 3 : 4 * dims + 4, cols]
        c = cot[at, cols]
        clow[at, cols] = c.astype(BF)
        column_sum(v512, 0, cols, c, m == 0)

    tiles(tokens, width, 256, 256, down_forward)

    def up_back(m, n):
        at, cols = pl.ds(m, 256), pl.ds(n, 256)
        g = dot(clow[at, :], w2[cols, down], NT) * dup[at, cols]
        ulow[at, cols] = g.astype(BF)
        column_sum(v1024, 0, cols, g, m == 0)

    tiles(tokens, nf, 256, 256, up_back)

    def down_grad(m, n):
        grad[pl.ds(m, 256), pl.ds(pl.multiple_of(width + n, 256), 256)] = dot(
            hlow[:, pl.ds(m, 256)], clow[:, pl.ds(n, 256)], TN
        ).astype(BF)

    tiles(nf, width, 256, 256, down_grad)

    def second_back(m, n):
        proj[pl.ds(m, 256), pl.ds(n, 256)] += 0.0
        gmid[pl.ds(m, 256), pl.ds(n, 256)] = dot(ulow[pl.ds(m, 256), :], wup[pl.ds(n, 256), :], NT)

    tiles(tokens, width, 256, 256, second_back)
    everything = slice(0, width)

    def middle_back(r):
        here = pl.ds(r, 64)
        start = r == 0
        m = mid[here, :]
        g = gmid[here, :]
        scale = norm_scale(m)
        n = m * scale
        column_sum(v512, 1, everything, g * n, start)
        g = g * gain
        gm = cot[here, :] + scale * (g - n * jnp.mean(g * n, axis=-1, keepdims=True))
        x = tok[here, :].astype(F32)
        pre = ext[here, :] + proj[here, :]
        s = sig(pre)
        u = upd[here, :]
        ge = gm * u * (s * (1.0 + pre * (1.0 - s)))
        gu = gm * (pre * s - x) * (u * (1.0 - u))
        gin[here, :] = gm * (1.0 - u)
        low = ge.astype(BF)
        elow[here, :] = low
        blre[here, pl.ds(nv, width)] = low
        blu[here, :] = gu.astype(BF)
        column_sum(v512, 2, everything, gu, start)
        column_sum(v512, 3, everything, ge, start)

    rows_loop(tokens, 64, middle_back)

    def gated_back(m, n):
        at, cols = pl.ds(m, 256), pl.ds(n, 256)
        g = dot(elow[at, :], w2[cols, pl.ds(0, width)], NT)
        gr = g * ad[at, cols].astype(F32)
        blre[at, cols] = gr.astype(BF)
        attg[at, cols] = (g * rs[at, cols].astype(F32)).astype(BF)
        column_sum(v1024, 1, cols, gr, m == 0)

    tiles(tokens, nv, 256, 256, gated_back)

    def attend_grad(m, n):
        grad[pl.ds(m, 256), pl.ds(n, 256)] = dot(
            glow[:, pl.ds(m, 256)], elow[:, pl.ds(n, 256)], TN
        ).astype(BF)

    tiles(nv, width, 256, 256, attend_grad)
    r2, r1 = rows2 // depth, rows1 // depth
    put_pieces(grad, own, sib, devices, depth, r2, 0, slice(0, 2 * width), slice(0, 2 * width))

    def up_grad(m, n):
        grad[pl.ds(m, 256), pl.ds(n, 256)] = dot(
            slow[:, pl.ds(m, 256)], ulow[:, pl.ds(n, 256)], TN
        ).astype(BF)

    tiles(width, nf, 256, 256, up_grad)
    put_pieces(grad, own, sib, devices, depth, r1, r2, slice(0, nf), slice(0, nf))


def back_kernel(*refs, devices, dims):
    pieces = refs[:devices]
    probs, attg, vlow, dval, qlow, klow, lat, blu, blre, z, nrm, pd, pz, dk, lab = refs[
        devices : devices + 15
    ]
    vgl, bll, gs, gnp, w512, w1024, w128, msg, ach = refs[devices + 15 : devices + 24]
    w, gq, gk, scr, sem = refs[devices + 24 :]
    tokens, width = z.shape
    nv = vlow.shape[1]
    zw = lat.shape[1]
    seqs = tokens // probs.shape[1]
    length = probs.shape[1]
    steps = tokens // SUBS
    rows = width // devices
    copies = load_weights(pieces, w, sem, rows, 0, w.shape[1], 0)
    row = lax.broadcasted_iota(jnp.int32, (length, length), 0)
    col = lax.broadcasted_iota(jnp.int32, (length, length), 1)

    def attend(r, total):
        here = pl.ds(pl.multiple_of(r * length, length), length)
        p = probs[here, :]
        plow = p.astype(BF)
        gp = dot(attg[here, :], vlow[here, :], NT)
        gsc = p * (gp - jnp.sum(p * gp, axis=-1, keepdims=True))
        low = gsc.astype(BF)
        gq[here, :] = dot(low, klow[here, :])
        gk[here, :] = dot(low, qlow[here, :], TN)
        for n in range(nv // 256):
            cols = slice(n * 256, (n + 1) * 256)
            gv = dot(plow, attg[here, cols], TN) * dval[here, cols].astype(F32)
            vgl[here, cols] = gv.astype(BF)
            column_sum(w1024, 0, cols, gv, r == 0)
        return total + gsc

    total = lax.fori_loop(0, seqs, attend, jnp.zeros((length, length), F32))
    flip = jnp.where((row + col) % length == 0, 1.0, 0.0)
    turned = lax.dot_general(
        total, flip, NN, precision=lax.Precision.HIGHEST, preferred_element_type=F32
    )
    turned = pltpu.roll(turned, 0, 1, stride=1, stride_axis=0)
    w128[...] = jnp.zeros_like(w128)
    w128[5:6, :] = jnp.sum(turned, axis=0, keepdims=True)

    def latent_back(r):
        here = pl.ds(r, 128)
        v = lat[here, :]
        s = sig(v)
        y = v * s
        q = gq[here, :] * zw ** (-0.5)
        k = gk[here, :]
        g = (q * pz[2:3, :] + k * pz[3:4, :]) * (s * (1.0 + v * (1.0 - s)))
        bll[here, :] = g.astype(BF)
        start = r == 0
        every = slice(0, zw)
        column_sum(w128, 0, every, g, start)
        column_sum(w128, 2, every, q * y, start)
        column_sum(w128, 3, every, k * y, start)
        column_sum(w128, 4, every, q, start)

    rows_loop(tokens, 128, latent_back)
    for c in copies:
        c.wait()
    at = split_sizes(width, zw, nv)

    def mixed_back(m, n):
        here, cols = pl.ds(m, 256), pl.ds(n, 256)
        g = dot(blu[here, :], w[cols, nv : nv + width], NT)
        g = g + dot(bll[here, :], w[cols, nv + at["l"] : nv + at["r"]], NT)
        g = g + dot(blre[here, :], w[cols, nv + at["r"] :], NT)
        v = z[here, cols]
        s = sig(v)
        g = g * (s * (1.0 + v * (1.0 - s)))
        t = n // TILE
        for j in range(256 // TILE):
            gs[t + j, here, :] = g[:, lanes_of(j)]
        column_sum(w512, 0, cols, g * two(nrm, t, here), m == 0)

    tiles(tokens, width, 256, 256, mixed_back)
    first, last = chunk_labels(lab, steps)
    one_way(gs, lab, first, dk, ach, dims, steps, width, True)
    power = dk[2 * dims : 3 * dims, :]
    through = (first == last) & (last == pltpu.roll(first, SUBS - 1, 0))
    for lt in range(width // TILE):
        lanes = lanes_of(lt)
        for h in range(dims):
            here = slice(h * SUBS, (h + 1) * SUBS)
            after = pltpu.roll(ach[here, lanes], SUBS - 1, 0) * power[h : h + 1, lanes]
            scr[here, :] = ach[here, lanes] + jnp.where(through, after, 0.0)
        half = SUBS // seqs
        msg[0 : dims * seqs, lanes] = scr[pl.ds(0, dims * seqs, stride=half), :].astype(BF)
        starts = lab[pl.ds(0, seqs, stride=length), :]
        tail = jnp.concatenate([starts, jnp.zeros((16 - seqs, TILE), F32)], axis=0)
        msg[dims * seqs : dims * seqs + 16, lanes] = tail.astype(BF)

    def normed_back(m, n):
        here, cols = pl.ds(m, 256), pl.ds(n, 256)
        omega = pd[4 * dims + 1 : 4 * dims + 2, cols]
        gnp[here, cols] = two(gs, n // TILE, here) * omega + dot(vgl[here, :], w[cols, 0:nv], NT)

    tiles(tokens, width, 256, 256, normed_back)


def two(ref, t, here):
    return jnp.concatenate([ref[t + j, here, :] for j in range(256 // TILE)], axis=1)


def weight_kernel(
    nlow, mlow, vgl, blu, bll, blre, own, sib, grad, *, devices, depth
):
    tokens, width = nlow.shape
    nv = vgl.shape[1]
    zw = bll.shape[1]
    at = split_sizes(width, zw, nv)

    def piece(lhs, rhs, start, cols):
        def fn(m, n):
            grad[pl.ds(m, 256), pl.ds(pl.multiple_of(start + n, TILE), cols)] = dot(
                lhs[:, pl.ds(m, 256)], rhs[:, pl.ds(n, cols)], TN
            ).astype(BF)

        tiles(width, rhs.shape[1], 256, cols, fn)

    piece(nlow, vgl, 0, 256)
    piece(mlow, blu, nv, 256)
    piece(mlow, bll, nv + at["l"], zw)
    piece(mlow, blre, nv + at["r"], 256)
    full = slice(0, grad.shape[1])
    put_pieces(grad, own, sib, devices, depth, width // devices // depth, 0, full, full)


def last_kernel(*refs, reach, devices, dims, seqs, nm):
    sp, nrm, gs, gnp, lab, dk, pdb, ach = refs[:8]
    msgs = refs[8 : 8 + reach]
    tok, gin, pd, v512, v1024, w512, w1024, w128 = refs[8 + reach : 16 + reach]
    tg, own, sib = refs[16 + reach : 19 + reach]
    ent, lab_scr, gnb, gnf, sd, sv, sm = refs[19 + reach : 26 + reach]
    scr_refs = refs[26 + reach :]
    tokens = nrm.shape[0]
    width = tok.shape[1]
    steps = tokens // SUBS
    half = SUBS // seqs
    lt = pl.program_id(0)
    first, last = chunk_labels(lab, steps)
    place = lax.broadcasted_iota(jnp.int32, (SUBS, TILE), 0)
    odd = place % half == half - 1
    power = dk[2 * dims : 3 * dims, :]
    arrivals = entering(msgs, last, odd, scr_refs, lab_scr, half - 1, dims, seqs, power)
    inside = first == last
    joined = last == pltpu.roll(first, SUBS - 1, 0)
    for h in range(dims):
        e = arrivals[h]
        here = slice(h * SUBS, (h + 1) * SUBS)
        onward = pltpu.roll(
            ach[here, :] + jnp.where(inside, e * power[h : h + 1, :], 0.0), SUBS - 1, 0
        )
        ent[here, :] = jnp.where(odd, e, jnp.where(joined, onward, 0.0))
    unroll = 4
    group = 8
    zero = jnp.zeros((SUBS, TILE), F32)
    cols = pl.ds(pl.multiple_of(lt * TILE, TILE), TILE)
    for base in range(0, dims, group):
        span = range(base, base + group)
        decay = [jnp.broadcast_to(dk[h : h + 1, :], (SUBS, TILE)) for h in span]
        weight = [jnp.broadcast_to(dk[dims + h : dims + h + 1, :], (SUBS, TILE)) for h in span]

        def step(i, carry, base=base, decay=decay, weight=weight):
            after = carry[0]
            a, g0, g1 = (list(carry[1 + j * group : 1 + (j + 1) * group]) for j in range(3))
            for u in range(unroll):
                t = steps - 1 - (i * unroll + u)
                here = pl.ds(t, SUBS, stride=steps)
                x = nrm[here, :]
                g = gs[here, :]
                l = lab[here, :]
                same = l == after
                after = l
                sums = [gnp[here, :] if base == 0 else gnb[here, :], zero]
                for j in range(group):
                    h = base + j
                    a[j] = decay[j] * jnp.where(same, a[j], 0.0) + g
                    g0[j] = g0[j] + a[j] * x
                    g1[j] = g1[j] + a[j] * sp[t, h * SUBS : (h + 1) * SUBS, :]
                    sums[j % 2] = sums[j % 2] + weight[j] * a[j]
                gnb[here, :] = sums[0] + sums[1]
            return (after,) + tuple(a) + tuple(g0) + tuple(g1)

        start = tuple(ent[h * SUBS : (h + 1) * SUBS, :] for h in span)
        done = lax.fori_loop(0, steps // unroll, step, (last,) + start + (zero,) * (2 * group))
        for j in range(group):
            h = base + j
            g0 = jnp.sum(done[1 + group + j], axis=0, keepdims=True)
            g1 = jnp.sum(done[1 + 2 * group + j], axis=0, keepdims=True)
            rate = 1.0 / (1.0 + jnp.exp(-pdb[h : h + 1, :]))
            damping = 1.0 / (1.0 + jnp.exp(-pdb[dims + h : dims + h + 1, :]))
            beta = pdb[2 * dims + h : 2 * dims + h + 1, :]
            eta = pdb[3 * dims + h : 3 * dims + h + 1, :]
            grad_decay = g1 * eta * rate * beta
            grad_rate = g0 * eta * beta - damping * grad_decay
            sd[h : h + 1, cols] = grad_rate * rate * (1.0 - rate)
            sd[dims + h : dims + h + 1, cols] = -grad_decay * rate * damping * (1.0 - damping)
            sd[2 * dims + h : 2 * dims + h + 1, cols] = g0 * rate * eta
            sd[3 * dims + h : 3 * dims + h + 1, cols] = g0 * rate * beta
    gnf[:, cols] = gnb[...]

    @pl.when(lt == pl.num_programs(0) - 1)
    def _():
        top = 4 * dims
        gain = pd[top : top + 1, :]
        sd[top : top + 8, :] = jnp.zeros((8, width), F32)

        def norm(r):
            here = pl.ds(r, 64)
            x = tok[here, :].astype(F32)
            q = norm_scale(x)
            m = x * q
            gn = gnf[here, :]
            sd[top : top + 1, :] += jnp.sum(gn * m, axis=0, keepdims=True)
            gn = gn * gain
            tg[here, :] = gin[here, :] + q * (gn - m * jnp.mean(gn * m, axis=-1, keepdims=True))

        rows_loop(tokens, 64, norm)
        sd[top + 1 : top + 2, :] = w512[0:1, :]
        sd[top + 2 : top + 3, :] = v512[1:2, :]
        sd[top + 3 : top + 4, :] = v512[0:1, :]
        nv = v1024.shape[1]
        zw = w128.shape[1]
        sv[...] = jnp.zeros_like(sv)
        sv[0:1, :] = w1024[0:1, :]
        sv[1:2, :] = v1024[0:1, :]
        at = split_sizes(width, zw, nv)
        sm[...] = jnp.zeros_like(sm)
        sm[0:1, 0:width] = v512[2:3, :]
        sm[0:1, at["l"] : at["r"]] = w128[0:1, :]
        sm[0:1, at["r"] : at["e"]] = v1024[1:2, :]
        sm[0:1, at["e"] : nm] = v512[3:4, :]
        me = lax.axis_index("seq")
        zrow = lax.broadcasted_iota(jnp.int32, (8, TILE), 0)
        zpart = jnp.where(zrow >= 2, w128[...], 0.0)
        for p in range(devices):
            k = me ^ p
            kc = k // 2

            def put(dst, p=p, kc=kc):
                dst[kc, 0:72, :] = sd[:, lanes_of(p * (width // devices) // TILE)]
                dst[kc, 72:80, :] = sv[:, lanes_of(p * (nv // devices) // TILE)] + zpart
                begin = p * (nm // devices) // TILE
                dst[kc, 80:88, :] = jnp.zeros((8, TILE), F32)
                for j in range(spread(nm // devices, devices)):
                    dst[kc, 80 + j : 81 + j, :] = sm[0:1, lanes_of(begin + j)]

            pl.when(k % 2 == 0)(partial(put, own))
            pl.when(k % 2 == 1)(partial(put, sib))


def hop(x, axis, k):
    length = lax.axis_size(axis)
    return lax.ppermute(x, axis, [(i, i ^ k) for i in range(length)])


def fold_kernel(own, got, *outs):
    for k, out in enumerate(outs):
        out[...] = (own[k].astype(F32) + got[k].astype(F32)).astype(out.dtype)


def fold(own, sib, dtype):
    got = hop(sib, "seq", 1)
    outs = [struct(own.shape[1:], F32)] + [struct(own.shape[1:], dtype)] * (own.shape[0] - 1)
    return whole(fold_kernel, outs, n_in=2, name="fold")(own, got)


def across(parts):
    return [parts[0]] + [hop(part, "seq", 2 * k) for k, part in enumerate(parts) if k]


def deal_kernel(*refs, count, depth):
    ins, outs, scr = refs[:count], refs[count:-1], refs[-1]
    me = lax.axis_index("grp")
    total = ins[0][...]
    for other in ins[1:]:
        total = total + other[...].astype(F32)
    scr[...] = total
    for k in range(depth):
        outs[k][...] = scr[me ^ k].astype(outs[k].dtype)


def deal(parts, depth):
    shape = parts[0].shape
    outs = [struct(shape[1:], F32)] + [struct(shape[1:], BF)] * (depth - 1)
    body = partial(deal_kernel, count=len(parts), depth=depth)
    mine = whole(body, outs, [pltpu.VMEM(shape, F32)], n_in=len(parts), name="deal")(*parts)
    return [mine[0]] + [hop(part, "grp", k) for k, part in enumerate(mine) if k]


def join_kernel(*refs):
    total = refs[0][...]
    for other in refs[1:-1]:
        total = total + other[...].astype(F32)
    refs[-1][...] = total.astype(BF)


def join(parts):
    depth = len(parts)
    mine = whole(join_kernel, struct(parts[0].shape, BF), n_in=depth, name="join")(*parts)
    return [mine] + [hop(mine, "grp", k) for k in range(1, depth)]


def spread_a_kernel(*refs, depth, r2, width):
    ins, (attend, down, up, scr) = refs[:depth], refs[depth:]
    me = lax.axis_index("grp")
    for k in range(depth):
        scr[me ^ k] = ins[k][...].astype(F32)
    r1 = up.shape[0] // depth
    for z in range(depth):
        attend[z * r2 : (z + 1) * r2, :] = scr[z, 0:r2, 0:width]
        down[z * r2 : (z + 1) * r2, :] = scr[z, 0:r2, width:]
        up[z * r1 : (z + 1) * r1, :] = scr[z, r2:, :]


def spread_b_kernel(*refs, depth):
    ins, (value, mix, scr) = refs[:depth], refs[depth:]
    me = lax.axis_index("grp")
    for k in range(depth):
        scr[me ^ k] = ins[k][...].astype(F32)
    r = value.shape[0] // depth
    nv = value.shape[1]
    for z in range(depth):
        value[z * r : (z + 1) * r, :] = scr[z, :, 0:nv]
        mix[z * r : (z + 1) * r, :] = scr[z, :, nv:]


def final_kernel(*refs, depth, plan, held, dims):
    ins, dec, flat, scr = refs[:depth], refs[depth], refs[depth + 1], refs[depth + 2]
    grp, me = lax.axis_index("grp"), lax.axis_index("seq")
    for k in range(depth):
        scr[grp ^ k] = ins[k][...]
    total = scr[0]
    for z in range(1, depth):
        total = total + scr[z]
    row = lax.broadcasted_iota(jnp.int32, (held, TILE), 0)
    lane = lax.broadcasted_iota(jnp.int32, (held, TILE), 1)
    pick = jnp.where(lane == row + (me * held) % TILE, 1.0, 0.0)
    dec[...] = lax.dot_general(
        pick, total[0 : 4 * dims, :], NT, precision=lax.Precision.HIGHEST, preferred_element_type=F32
    )
    flat[...] = jnp.zeros_like(flat)
    for j, (at, _, n, nt) in enumerate(plan):
        values = [total[at + i : at + i + 1, :] for i in range(nt)]
        values = values[0] if nt == 1 else jnp.concatenate(values, axis=1)
        values = jnp.broadcast_to(values, (SUBS, nt * TILE))
        lanes = nt * TILE
        moved = pltpu.roll(values, (lanes - (me * n) % TILE) % lanes, 1)
        flat[j : j + 1, 0:lanes] = moved[0:1, :]


def total_kernel(*refs):
    total = refs[0][...]
    for other in refs[1:-1]:
        total = total + other[...]
    refs[-1][...] = total


def gather_pieces(x, devices):
    near = [x] + [hop(x, "seq", 2 * k) for k in range(1, devices // 2)]
    far = [hop(part, "seq", 1) for part in near]
    return [part for pair in zip(near, far) for part in pair]


def per_device(
    tokens, segments, cotangent, first_gain, value_weight, value_bias, decay_alpha, decay_delta,
    decay_beta, decay_eta, skip_omega, mix_weight, mix_bias, latent_gains, query_offset,
    position_bias, attend_weight, second_gain, up_weight, up_bias, down_weight, down_bias,
):
    devices = lax.axis_size("seq")
    depth = lax.axis_size("grp")
    seqs, length, width = tokens.shape
    count = seqs * length
    steps = count // SUBS
    dims = decay_alpha.shape[1]
    nv = value_weight.shape[1]
    nf = up_weight.shape[1]
    nm = mix_weight.shape[1]
    zw = query_offset.shape[0] * devices
    reach = max(1, devices // 4)
    held = width // devices

    vectors = [
        (72, value_bias), (73, up_bias), (80, mix_bias), (64, first_gain), (65, skip_omega),
        (66, second_gain), (67, down_bias), (74, latent_gains[0]), (75, latent_gains[1]),
        (76, query_offset), (77, position_bias),
    ]
    plan, off = [], 0
    for at, v in vectors:
        plan.append((at, off, v.shape[0], spread(v.shape[0], devices)))
        off += v.shape[0]
    padded = ceil_div(off, TILE) * TILE
    flat = jnp.concatenate([v for _, v in vectors] + [jnp.zeros((padded - off,), BF)])[None]
    decs = jnp.concatenate([decay_alpha, decay_delta, decay_beta, decay_eta], axis=1)
    placed = whole(
        partial(place_kernel, plan=plan), struct((ROWS_SMALL, TILE), F32), n_in=2, name="place"
    )(flat, decs)
    small = lax.all_gather(placed, "seq", axis=0, tiled=False)

    w1 = gather_pieces(jnp.concatenate([value_weight, mix_weight], axis=1), devices)
    w2 = gather_pieces(
        jnp.concatenate([jnp.concatenate([attend_weight, down_weight], axis=1), up_weight], axis=0),
        devices,
    )

    tok = tokens.reshape(count, width)
    cot = cotangent.reshape(count, width)
    blocks = width // TILE
    msg_rows = dims * seqs + 16
    pd, pv, pz, pm, dk, nrm, nlow, lab, fin, msg = whole(
        partial(head_kernel, devices=devices, dims=dims, nv=nv, nm=nm),
        [
            struct((72, width), F32), struct((8, nv), F32), struct((8, TILE), F32),
            struct((8, nm), F32), struct((3 * dims, width), F32), struct((blocks, count, TILE), F32),
            struct((count, width), BF), struct((count, TILE), F32),
            struct((dims * SUBS, width), F32), struct((msg_rows, width), BF),
        ],
        [pltpu.VMEM((dims * SUBS, TILE), F32)],
        n_in=3,
        name="head",
    )(small, tok, segments)

    onward = [
        lax.ppermute(msg, "seq", [(i, i + k) for i in range(devices - k)])
        for k in range(1, reach + 1)
    ]

    def lane_block(rows):
        return pl.BlockSpec((rows, TILE), lambda i: (0, i))

    tile_block = pl.BlockSpec((None, count, TILE), lambda i: (i, 0, 0))

    def fixed(shape):
        return pl.BlockSpec(shape, lambda i: (0,) * len(shape))

    arrivals = [pltpu.VMEM((dims * SUBS, TILE), F32)] * reach
    z, mlow, sp = pl.pallas_call(
        partial(scan_kernel, reach=reach, dims=dims, seqs=seqs),
        grid=(blocks,),
        in_specs=[
            tile_block, fixed((count, TILE)), lane_block(3 * dims), lane_block(72),
            lane_block(dims * SUBS),
        ] + [lane_block(msg_rows)] * reach,
        out_specs=[
            lane_block(count), lane_block(count),
            pl.BlockSpec((steps, dims * SUBS, TILE), lambda i: (0, 0, i)),
        ],
        out_shape=[
            struct((count, width), F32), struct((count, width), BF),
            struct((steps, dims * SUBS, width), F32),
        ],
        scratch_shapes=[
            pltpu.VMEM((dims * SUBS, TILE), F32), pltpu.VMEM((SUBS, TILE), F32),
            pltpu.VMEM((count, TILE), F32),
        ] + arrivals,
        compiler_params=PARAMS,
        name="scan",
    )(nrm, lab, dk, pd, fin, *onward)

    def sems(n):
        return pltpu.SemaphoreType.DMA((n, devices))

    vlow, dval, upd, ext, lat, rs, ad, glow, probs, qlow, klow = whole(
        partial(front_kernel, devices=devices),
        [
            struct((count, nv), BF), struct((count, nv), BF), struct((count, width), F32),
            struct((count, width), F32), struct((count, zw), F32), struct((count, nv), BF),
            struct((count, nv), BF), struct((count, nv), BF), struct((count, length), F32),
            struct((count, zw), BF), struct((count, zw), BF),
        ],
        [pltpu.VMEM((width, nv + nm), BF), pltpu.VMEM((count, nv), F32), sems(1)],
        in_specs=[HB] * devices + [VM] * 7,
        name="front",
    )(*w1, nlow, mlow, pv, pm, pz, lab, segments)

    half = devices // 2
    rows2, rows1 = nv // devices // depth, held // depth
    piece_a = struct((half, depth, rows2 + rows1, 2 * width), BF)
    out, gin, attg, blu, blre, v512, v1024, own_a, sib_a = whole(
        partial(middle_kernel, devices=devices, depth=depth, dims=dims),
        [
            struct((count, width), F32), struct((count, width), F32), struct((count, nv), BF),
            struct((count, width), BF), struct((count, nv + width), BF), struct((8, width), F32),
            struct((8, nv), F32), piece_a, piece_a,
        ],
        [
            pltpu.VMEM((nv, 2 * width), BF), pltpu.VMEM((width, nf), BF),
            pltpu.VMEM((count, width), F32), pltpu.VMEM((count, width), F32),
            pltpu.VMEM((count, width), BF), pltpu.VMEM((count, nf), F32),
            pltpu.VMEM((count, nf), BF), pltpu.VMEM((count, width), BF),
            pltpu.VMEM((count, nf), BF), pltpu.VMEM((count, width), BF),
            pltpu.VMEM((count, width), F32), pltpu.VMEM((nv, 2 * width), BF), sems(2),
        ],
        in_specs=[HB] * devices + [VM] * 9,
        name="middle",
    )(*w2, tok, cot, upd, ext, rs, ad, glow, pd, pv)

    vgl, bll, gs, gnp, w512, w1024, w128, back_msg, ach = whole(
        partial(back_kernel, devices=devices, dims=dims),
        [
            struct((count, nv), BF), struct((count, zw), BF), struct((blocks, count, TILE), F32),
            struct((count, width), F32), struct((8, width), F32), struct((8, nv), F32),
            struct((8, TILE), F32), struct((msg_rows, width), BF),
            struct((dims * SUBS, width), F32),
        ],
        [
            pltpu.VMEM((width, nv + nm), BF), pltpu.VMEM((count, zw), F32),
            pltpu.VMEM((count, zw), F32), pltpu.VMEM((dims * SUBS, TILE), F32), sems(1),
        ],
        in_specs=[HB] * devices + [VM] * 15,
        name="back",
    )(*w1, probs, attg, vlow, dval, qlow, klow, lat, blu, blre, z, nrm, pd, pz, dk, lab)

    backward = [
        lax.ppermute(back_msg, "seq", [(i + k, i) for i in range(devices - k)])
        for k in range(1, reach + 1)
    ]

    piece_b = struct((half, depth, rows1, nv + nm), BF)
    own_b, sib_b = whole(
        partial(weight_kernel, devices=devices, depth=depth),
        [piece_b, piece_b],
        [pltpu.VMEM((width, nv + nm), BF)],
        n_in=6,
        name="weights",
    )(nlow, mlow, vgl, blu, bll, blre)

    piece_c = struct((half, ROWS_SMALL, TILE), F32)
    wide = ceil_div(nm, TILE) + 2
    tokens_grad, own_c, sib_c = pl.pallas_call(
        partial(last_kernel, reach=reach, devices=devices, dims=dims, seqs=seqs, nm=nm),
        grid=(blocks,),
        in_specs=[
            pl.BlockSpec((steps, dims * SUBS, TILE), lambda i: (0, 0, i)), tile_block,
            tile_block, lane_block(count), fixed((count, TILE)), lane_block(3 * dims),
            lane_block(72), lane_block(dims * SUBS),
        ] + [lane_block(msg_rows)] * reach + [
            fixed((count, width)), fixed((count, width)), fixed((72, width)), fixed((8, width)),
            fixed((8, nv)), fixed((8, width)), fixed((8, nv)), fixed((8, TILE)),
        ],
        out_specs=[
            fixed((count, width)), fixed(piece_c.shape), fixed(piece_c.shape),
        ],
        out_shape=[struct((count, width), F32), piece_c, piece_c],
        scratch_shapes=[
            pltpu.VMEM((dims * SUBS, TILE), F32), pltpu.VMEM((SUBS, TILE), F32),
            pltpu.VMEM((count, TILE), F32), pltpu.VMEM((count, width), F32),
            pltpu.VMEM((72, width), F32), pltpu.VMEM((8, nv), F32),
            pltpu.VMEM((8, wide * TILE), F32),
        ] + arrivals,
        compiler_params=PARAMS,
        name="last",
    )(
        sp, nrm, gs, gnp, lab, dk, pd, ach, *backward, tok, gin, pd, v512, v1024, w512, w1024, w128
    )

    sum_a = join(deal(across(fold(own_a, sib_a, BF)), depth))
    attend_grad, down_grad, up_grad = whole(
        partial(spread_a_kernel, depth=depth, r2=rows2, width=width),
        [
            struct((nv // devices, width), F32), struct((nf // devices, width), F32),
            struct((held, nf), F32),
        ],
        [pltpu.VMEM((depth,) + piece_a.shape[2:], F32)],
        n_in=depth,
        name="spread_a",
    )(*sum_a)
    sum_b = join(deal(across(fold(own_b, sib_b, BF)), depth))
    value_grad, mix_grad = whole(
        partial(spread_b_kernel, depth=depth),
        [struct((held, nv), F32), struct((held, nm), F32)],
        [pltpu.VMEM((depth,) + piece_b.shape[2:], F32)],
        n_in=depth,
        name="spread_b",
    )(*sum_b)
    parts_c = across(fold(own_c, sib_c, F32))
    shard_c = whole(total_kernel, struct(piece_c.shape[1:], F32), n_in=half, name="total")(*parts_c)
    all_c = [shard_c] + [hop(shard_c, "grp", k) for k in range(1, depth)]
    most = max(nt for _, _, _, nt in plan)
    dec_grad, flat_grad = whole(
        partial(final_kernel, depth=depth, plan=plan, held=held, dims=dims),
        [struct((held, 4 * dims), F32), struct((16, most * TILE), F32)],
        [pltpu.VMEM((depth,) + piece_c.shape[1:], F32)],
        n_in=depth,
        name="final",
    )(*all_c)
    grads = [flat_grad[j, :n] for j, (_, _, n, _) in enumerate(plan)]
    value_b, up_b, mix_b, first_g, omega, second_g, down_b, g0, g1, qoff, posb = grads
    return (
        out.reshape(tokens.shape),
        tokens_grad.reshape(tokens.shape),
        first_g,
        value_grad,
        value_b,
        dec_grad[:, 0:dims],
        dec_grad[:, dims : 2 * dims],
        dec_grad[:, 2 * dims : 3 * dims],
        dec_grad[:, 3 * dims :],
        omega,
        mix_grad,
        mix_b,
        jnp.stack([g0, g1]),
        qoff,
        posb,
        attend_grad,
        second_g,
        up_grad,
        up_b,
        down_grad,
        down_b,
    )


def solution(mesh):
    vec, mat = P("seq"), P("seq", None)
    data = P("grp", "seq", None)
    params = (
        vec, mat, vec, mat, mat, mat, mat, vec, mat, vec, P(None, "seq"), vec, vec, mat, vec, mat,
        vec, mat, vec,
    )
    return jax.shard_map(
        per_device,
        mesh=mesh,
        in_specs=(data, P("grp", "seq"), data) + params,
        out_specs=(data, data) + params,
        check_vma=False,
    )
```

```python
from functools import partial

import jax
import jax.numpy as jnp
from jax import lax
from jax.experimental import pallas as pl
from jax.experimental.pallas import tpu as pltpu
from jax.sharding import PartitionSpec as P

EPSILON = 1e-06
F32 = jnp.float32
BF = jnp.bfloat16
TILE = 128
SUBS = 8
ROWS_SMALL = 88
NN = (((1,), (0,)), ((), ()))
NT = (((1,), (1,)), ((), ()))
TN = (((0,), (0,)), ((), ()))


def dot(a, b, dims=NN):
    return lax.dot_general(a, b, dims, preferred_element_type=F32)


def sig(v):
    return 0.5 * jnp.tanh(0.5 * v) + 0.5


def struct(shape, dtype):
    return jax.ShapeDtypeStruct(shape, dtype)


VM = pl.BlockSpec(memory_space=pltpu.VMEM)
HB = pl.BlockSpec(memory_space=pl.ANY)


def cost(micros):
    return pl.CostEstimate(flops=0, transcendentals=0, bytes_accessed=int(micros * 3.69e6))


def whole(body, outs, scratch=(), in_specs=None, n_in=None, name=None, micros=2, vmem=26):
    return pl.pallas_call(
        body,
        out_shape=outs,
        in_specs=in_specs if in_specs is not None else [VM] * n_in,
        out_specs=jax.tree.map(lambda _: VM, outs),
        scratch_shapes=list(scratch),
        compiler_params=pltpu.CompilerParams(vmem_limit_bytes=vmem << 20),
        cost_estimate=cost(micros),
        name=name,
    )


def tiles(m_size, n_size, tm, tn, fn):
    for n in range(0, n_size, tn):
        for m in range(0, m_size, tm):
            fn(m, n)


def rows_loop(total, step, fn):
    def body(i, _):
        fn(pl.multiple_of(i * step, step))
        return 0

    lax.fori_loop(0, total // step, body, 0)


def ceil_div(a, b):
    return -(-a // b)


def spread(n, devices):
    return max(ceil_div((d * n) % TILE + n, TILE) for d in range(devices))


def place_kernel(*refs, plan):
    me = lax.axis_index("seq")
    decs, vectors, out_ref = refs[:4], refs[4:-1], refs[-1]
    out_ref[...] = jnp.zeros_like(out_ref)
    dims, held = decs[0].shape
    pick = pick_lanes(me, held, TILE)
    for j, dec in enumerate(decs):
        out_ref[j * dims : (j + 1) * dims, :] = dot(dec[...], pick.astype(BF))
    source = 0
    for at, count, n, nt in plan:
        values = vectors[source][...].astype(F32)
        source += 1
        if count == 1:
            values = values.reshape(1, n)
        values = jnp.broadcast_to(values, (SUBS, n)) if count == 1 else values
        moved = dot(values.astype(BF), pick_lanes(me, n, nt * TILE).astype(BF))
        for i in range(count):
            for j in range(nt):
                out_ref[at + i + j : at + i + j + 1, :] = moved[i : i + 1, j * TILE : (j + 1) * TILE]


def pick_lanes(me, n, lanes):
    row = lax.broadcasted_iota(jnp.int32, (n, lanes), 0)
    lane = lax.broadcasted_iota(jnp.int32, (n, lanes), 1)
    return jnp.where(lane == row + (me * n) % TILE, 1.0, 0.0)


def pack_kernel(value, mix, attend, down, up, w1, w2):
    nv = value.shape[1]
    w1[:, 0:nv] = value[...]
    w1[:, nv:] = mix[...]
    rows, width = attend.shape
    w2[0:rows, 0:width] = attend[...]
    w2[0:rows, width:] = down[...]
    w2[rows:, :] = up[...]


def assemble(src, low, high, n, total, devices):
    parts = [None] * ceil_div(total, TILE)
    for d in range(devices):
        t = d * n // TILE
        block = src[d, low:high, :]
        parts[t] = block if parts[t] is None else parts[t] + block
    return parts


def chunk_labels(lab_ref, steps):
    return lab_ref[pl.ds(0, SUBS, stride=steps), :], lab_ref[pl.ds(steps - 1, SUBS, stride=steps), :]


def lanes_of(t):
    return slice(t * TILE, (t + 1) * TILE)


def one_way(src_ref, lab_ref, ref_label, dk_ref, out_ref, dims, steps, width, reverse, unroll=8):
    for lt in range(width // TILE):
        lanes = lanes_of(lt)
        decay = [jnp.broadcast_to(dk_ref[h : h + 1, lanes], (SUBS, TILE)) for h in range(dims)]

        def step(i, state, lt=lt, decay=decay):
            state = list(state)
            for u in range(unroll):
                t = i * unroll + u
                if reverse:
                    t = steps - 1 - t
                x = src_ref[lt, pl.ds(t, SUBS, stride=steps), :]
                l = lab_ref[pl.ds(t, SUBS, stride=steps), :]
                x = jnp.where(l == ref_label, x, 0.0)
                state = [decay[h] * state[h] + x for h in range(dims)]
            return tuple(state)

        zero = jnp.zeros((SUBS, TILE), F32)
        final = lax.fori_loop(0, steps // unroll, step, (zero,) * dims)
        for h in range(dims):
            out_ref[h * SUBS : (h + 1) * SUBS, lanes] = final[h]


def norm_scale(x):
    return lax.rsqrt(jnp.mean(x * x, axis=-1, keepdims=True) + EPSILON)


def head_kernel(*refs, devices, dims, nv, nm):
    (
        tok_ref, seg_ref, pd_ref, pv_ref, pz_ref, pm_ref, dk_ref, nrm_ref, low_ref, lab_ref,
        fin_ref, msg_ref, scr_ref, small_ref,
    ) = refs[devices:]
    me = lax.axis_index("seq")
    for k in range(devices):
        small_ref[me ^ k] = refs[k][...]
    tokens, width = tok_ref.shape
    seqs, length = seg_ref.shape
    steps = tokens // SUBS
    for t, part in enumerate(assemble(small_ref, 0, 72, width // devices, width, devices)):
        pd_ref[:, lanes_of(t)] = part
    for t, part in enumerate(assemble(small_ref, 72, 80, nv // devices, nv, devices)):
        pv_ref[:, lanes_of(t)] = part
    z = small_ref[0, 72:80, :]
    for d in range(1, devices):
        z = z + small_ref[d, 72:80, :]
    pz_ref[...] = z
    n = nm // devices
    cells = [None] * (nm // TILE)
    for d in range(devices):
        first, lane = divmod(d * n, TILE)
        for j in range(ceil_div(lane + n, TILE)):
            piece = small_ref[d, 80 + j : 81 + j, :]
            cells[first + j] = piece if cells[first + j] is None else cells[first + j] + piece
    for t, piece in enumerate(cells):
        pm_ref[:, lanes_of(t)] = jnp.broadcast_to(piece, (SUBS, TILE))

    rate = 1.0 / (1.0 + jnp.exp(-pd_ref[0:dims, :]))
    damping = 1.0 / (1.0 + jnp.exp(-pd_ref[dims : 2 * dims, :]))
    decay = 1.0 - rate * damping
    dk_ref[0:dims, :] = decay
    dk_ref[dims : 2 * dims, :] = pd_ref[3 * dims : 4 * dims, :] * rate * pd_ref[2 * dims : 3 * dims, :]
    power, k = decay, 1
    while k < steps:
        power, k = power * power, k * 2
    dk_ref[2 * dims : 3 * dims, :] = power

    gain = pd_ref[4 * dims : 4 * dims + 1, :]

    def norm(r):
        x = tok_ref[pl.ds(r, 64), :].astype(F32)
        y = x * norm_scale(x) * gain
        for t in range(width // TILE):
            nrm_ref[t, pl.ds(r, 64), :] = y[:, lanes_of(t)]
        low_ref[pl.ds(r, 64), :] = y.astype(BF)

    rows_loop(tokens, 64, norm)

    labels = seg_ref[...].astype(F32)
    row = lax.broadcasted_iota(jnp.int32, (length, length), 0)
    col = lax.broadcasted_iota(jnp.int32, (length, length), 1)
    for s in range(seqs):
        diagonal = jnp.where(row == col, labels[s : s + 1, :], 0.0).astype(BF)
        lab_ref[s * length : (s + 1) * length, :] = dot(diagonal, jnp.ones((length, TILE), BF))

    first, last = chunk_labels(lab_ref, steps)
    one_way(nrm_ref, lab_ref, last, dk_ref, fin_ref, dims, steps, width, False)
    through = (first == last) & (first == pltpu.roll(last, 1, 0))
    for lt in range(width // TILE):
        lanes = lanes_of(lt)
        for h in range(dims):
            own = fin_ref[h * SUBS : (h + 1) * SUBS, lanes]
            before = pltpu.roll(own, 1, 0) * power[h : h + 1, lanes]
            scr_ref[h * SUBS : (h + 1) * SUBS, :] = own + jnp.where(through, before, 0.0)
        half = SUBS // seqs
        msg_ref[0 : dims * seqs, lanes] = scr_ref[
            pl.ds(half - 1, dims * seqs, stride=half), :
        ].astype(BF)
        ends = lab_ref[pl.ds(length - 1, seqs, stride=length), :]
        tail = jnp.concatenate([ends, jnp.zeros((16 - seqs, TILE), F32)], axis=0)
        msg_ref[dims * seqs : dims * seqs + 16, lanes] = tail.astype(BF)


def entering(msgs, lanes, own_label, even, scr_refs, lab_scr, start, dims, seqs, power):
    half = SUBS // seqs
    gates = []
    for m, scr in zip(msgs, scr_refs):
        scr[pl.ds(start, dims * seqs, stride=half), :] = m[0 : dims * seqs, lanes].astype(F32)
        tail = m[dims * seqs : dims * seqs + 16, lanes].astype(F32)
        lab_scr[pl.ds(start, seqs, stride=half), :] = tail[0:seqs, :]
        gates.append(even & (lab_scr[...] == own_label))
    result = []
    for h in range(dims):
        total, reach = None, None
        for gate, scr in zip(gates, scr_refs):
            part = jnp.where(gate, scr[h * SUBS : (h + 1) * SUBS, :], 0.0)
            if total is None:
                total, reach = part, power[h : h + 1, :] * power[h : h + 1, :]
                far = reach
            else:
                total, far = total + part * far, far * reach
        result.append(total)
    return result


def scan_kernel(*refs, reach, dims, seqs):
    nrm_ref, lab_ref, dk_ref, pd_ref, fin_ref = refs[:5]
    msgs = refs[5 : 5 + reach]
    z_ref, mlow_ref, sp_ref = refs[5 + reach : 8 + reach]
    ent_ref, lab_scr, ys_ref = refs[8 + reach : 11 + reach]
    scr_refs = refs[11 + reach :]
    blocks, tokens, _ = nrm_ref.shape
    steps = tokens // SUBS
    half = SUBS // seqs
    first, last = chunk_labels(lab_ref, steps)
    place = lax.broadcasted_iota(jnp.int32, (SUBS, TILE), 0)
    even = place % half == 0
    inside = first == last
    joined = first == pltpu.roll(last, 1, 0)
    unroll = 4

    def block(lt, _):
        lanes = pl.ds(pl.multiple_of(lt * TILE, TILE), TILE)
        power = dk_ref[2 * dims : 3 * dims, lanes]
        arrivals = entering(msgs, lanes, first, even, scr_refs, lab_scr, 0, dims, seqs, power)
        for h in range(dims):
            e = arrivals[h]
            own = fin_ref[h * SUBS : (h + 1) * SUBS, lanes]
            onward = pltpu.roll(own + jnp.where(inside, e * power[h : h + 1, :], 0.0), 1, 0)
            ent_ref[h * SUBS : (h + 1) * SUBS, :] = jnp.where(
                even, e, jnp.where(joined, onward, 0.0)
            )
        decay = [jnp.broadcast_to(dk_ref[h : h + 1, lanes], (SUBS, TILE)) for h in range(dims)]
        weight = [
            jnp.broadcast_to(dk_ref[dims + h : dims + h + 1, lanes], (SUBS, TILE))
            for h in range(dims)
        ]

        def step(i, carry):
            before, state = carry[0], list(carry[1:])
            for u in range(unroll):
                t = i * unroll + u
                x = nrm_ref[lt, pl.ds(t, SUBS, stride=steps), :]
                l = lab_ref[pl.ds(t, SUBS, stride=steps), :]
                same = l == before
                before = l
                sums = [None] * 4
                for h in range(dims):
                    kept = jnp.where(same, state[h], 0.0)
                    if h % 2 == 0:
                        held = kept
                    else:
                        pair = jnp.concatenate([held, kept], axis=0)
                        sp_ref[lt, t, (h - 1) * SUBS : (h + 1) * SUBS, :] = pair.astype(BF)
                    state[h] = decay[h] * kept + x
                    term = weight[h] * state[h]
                    sums[h % 4] = term if sums[h % 4] is None else sums[h % 4] + term
                ys_ref[lt, pl.ds(t, SUBS, stride=steps), :] = (sums[0] + sums[1]) + (
                    sums[2] + sums[3]
                )
            return (before,) + tuple(state)

        start = tuple(ent_ref[h * SUBS : (h + 1) * SUBS, :] for h in range(dims))
        lax.fori_loop(0, steps // unroll, step, (first,) + start)
        return 0

    lax.fori_loop(0, blocks, block, 0)
    omega = pd_ref[4 * dims + 1 : 4 * dims + 2, :]

    def gate(r):
        for t in range(blocks):
            v = ys_ref[t, pl.ds(r, 128), :] + omega[:, lanes_of(t)] * nrm_ref[t, pl.ds(r, 128), :]
            z_ref[pl.ds(r, 128), lanes_of(t)] = v
            mlow_ref[pl.ds(r, 128), lanes_of(t)] = (v * sig(v)).astype(BF)

    rows_loop(tokens, 128, gate)


def load_weights(pieces, dst, sem, rows, start, cols, place):
    me = lax.axis_index("seq")
    copies = []
    for k, piece in enumerate(pieces):
        p = me ^ k
        copies.append(
            pltpu.make_async_copy(
                piece.at[pl.ds(start, rows), pl.ds(0, cols)],
                dst.at[pl.ds(pl.multiple_of(p * rows, rows), rows), pl.ds(0, cols)],
                sem.at[place, k],
            )
        )
    for c in copies:
        c.start()
    return copies


def split_sizes(width, latent, nv):
    return {"u": 0, "l": width, "r": width + latent, "e": width + latent + nv}


def front_kernel(*refs, devices):
    pieces = refs[:devices]
    nlow, mlow, pv, pm, pz, lab, seg = refs[devices : devices + 7]
    vlow, dval, upd, ext, lat, rs, ad, glow, probs, qlow, klow = refs[devices + 7 : devices + 18]
    w, res, sem = refs[devices + 18 :]
    tokens, width = nlow.shape
    nv = vlow.shape[1]
    zw = lat.shape[1]
    seqs, length = seg.shape
    rows = width // devices
    copies = load_weights(pieces, w, sem, rows, 0, w.shape[1], 0)
    for c in copies:
        c.wait()

    def value(m, n):
        v = dot(nlow[pl.ds(m, 512), :], w[:, pl.ds(n, 512)]) + pv[0:1, pl.ds(n, 512)]
        s = sig(v)
        vlow[pl.ds(m, 512), pl.ds(n, 512)] = (v * s).astype(BF)
        dval[pl.ds(m, 512), pl.ds(n, 512)] = (s * (1.0 + v * (1.0 - s))).astype(BF)

    tiles(tokens, nv, 512, 512, value)
    at = split_sizes(width, zw, nv)

    def base(m, n, start, size):
        cols = start + n
        wcols = nv + start + n
        return dot(mlow[pl.ds(m, 512), :], w[:, pl.ds(wcols, size)]) + pm[0:1, pl.ds(cols, size)]

    def update(m, n):
        upd[pl.ds(m, 512), pl.ds(n, 512)] = sig(base(m, n, at["u"], 512))

    tiles(tokens, width, 512, 512, update)

    def extra(m, n):
        ext[pl.ds(m, 512), pl.ds(n, 512)] = base(m, n, at["e"], 512)

    tiles(tokens, width, 512, 512, extra)

    def reset(m, n):
        res[pl.ds(m, 512), pl.ds(n, 512)] = base(m, n, at["r"], 512)

    tiles(tokens, nv, 512, 512, reset)

    def latent(m, n):
        v = base(m, n, at["l"], zw)
        lat[pl.ds(m, 512), :] = v
        y = v * sig(v)
        qlow[pl.ds(m, 512), :] = ((y * pz[2:3, :] + pz[4:5, :]) * zw ** (-0.5)).astype(BF)
        klow[pl.ds(m, 512), :] = (y * pz[3:4, :]).astype(BF)

    tiles(tokens, zw, 512, zw, latent)

    row = lax.broadcasted_iota(jnp.int32, (length, length), 0)
    col = lax.broadcasted_iota(jnp.int32, (length, length), 1)
    flip = jnp.where((row + col) % length == 0, 1.0, 0.0).astype(BF)
    bias = dot(pz[...].astype(BF), flip)[5:6, :]
    table = pltpu.roll(jnp.broadcast_to(bias, (length, length)), 0, 1, stride=1, stride_axis=0)
    causal = row >= col

    def attend(r):
        here = pl.ds(r, length)
        label_j = seg[pl.ds(r // length, 1), :].astype(F32)
        allowed = causal & (lab[here, :] == label_j)
        scores = dot(qlow[here, :], klow[here, :], NT) + table
        scores = jnp.where(allowed, scores, -1e30)
        weights = jnp.exp(scores - jnp.max(scores, axis=-1, keepdims=True))
        prob = weights / jnp.sum(weights, axis=-1, keepdims=True)
        probs[here, :] = prob
        plow = prob.astype(BF)
        for n in range(nv // 256):
            cols = slice(n * 256, (n + 1) * 256)
            a = dot(plow, vlow[here, cols])
            v = res[here, cols]
            s = sig(v)
            y = v * s
            rs[here, cols] = y.astype(BF)
            ad[here, cols] = (a * (s * (1.0 + v * (1.0 - s)))).astype(BF)
            glow[here, cols] = (a * y).astype(BF)

    rows_loop(tokens, length, attend)


def column_sum(ref, row, cols, values, first):
    total = jnp.sum(values, axis=0, keepdims=True)
    if isinstance(first, bool):
        ref[row : row + 1, cols] = total if first else ref[row : row + 1, cols] + total
        return

    @pl.when(first)
    def _():
        ref[row : row + 1, cols] = total

    @pl.when(jnp.logical_not(first))
    def _():
        ref[row : row + 1, cols] = ref[row : row + 1, cols] + total


def put_pieces(src, own, sib, devices, depth, rows, at, src_cols, cols):
    me = lax.axis_index("seq")
    for p in range(devices):
        k = me ^ p
        kc = k // 2

        def put(dst, p=p, kc=kc):
            for z in range(depth):
                begin = (p * depth + z) * rows
                dst[kc, z, at : at + rows, cols] = src[begin : begin + rows, src_cols].astype(BF)

        pl.when(k % 2 == 0)(partial(put, own))
        pl.when(k % 2 == 1)(partial(put, sib))


def middle_kernel(*refs, devices, depth, dims):
    pieces = refs[:devices]
    tok, cot, upd, ext, rs, ad, glow, pd, pv = refs[devices : devices + 9]
    out, gin, attg, blu, blre, v512, v1024, own, sib = refs[devices + 9 : devices + 18]
    w2, wup, proj, mid, slow, dup, hlow, clow, ulow, elow, gmid, grad, sem = refs[devices + 18 :]
    tokens, width = tok.shape
    nv = rs.shape[1]
    nf = dup.shape[1]
    rows2, rows1 = nv // devices, width // devices
    copies = load_weights(pieces, w2, sem, rows2, 0, 2 * width, 0)
    copies += load_weights(pieces, wup, sem, rows1, rows2, nf, 1)
    for c in copies:
        c.wait()
    down = pl.ds(width, width)

    def project(m, n):
        proj[pl.ds(m, 512), pl.ds(n, 512)] = dot(glow[pl.ds(m, 512), :], w2[:, pl.ds(n, 512)])

    tiles(tokens, width, 512, 512, project)
    gain = pd[4 * dims + 2 : 4 * dims + 3, :]

    def blend(r):
        here = pl.ds(r, 64)
        x = tok[here, :].astype(F32)
        pre = ext[here, :] + proj[here, :]
        s = sig(pre)
        m = x + upd[here, :] * (pre * s - x)
        mid[here, :] = m
        slow[here, :] = (m * norm_scale(m) * gain).astype(BF)

    rows_loop(tokens, 64, blend)

    def up(m, n):
        v = dot(slow[pl.ds(m, 512), :], wup[:, pl.ds(n, 512)]) + pv[1:2, pl.ds(n, 512)]
        s = sig(v)
        hlow[pl.ds(m, 512), pl.ds(n, 512)] = (v * s).astype(BF)
        dup[pl.ds(m, 512), pl.ds(n, 512)] = s * (1.0 + v * (1.0 - s))

    tiles(tokens, nf, 512, 512, up)

    def down_forward(m, n):
        at, cols = pl.ds(m, 512), pl.ds(n, 512)
        y = dot(hlow[at, :], w2[:, pl.ds(width + n, 512)])
        out[at, cols] = mid[at, cols] + y + pd[4 * dims + 3 : 4 * dims + 4, cols]
        c = cot[at, cols]
        clow[at, cols] = c.astype(BF)
        column_sum(v512, 0, cols, c, m == 0)

    tiles(tokens, width, 512, 512, down_forward)

    def up_back(m, n):
        at, cols = pl.ds(m, 512), pl.ds(n, 512)
        g = dot(clow[at, :], w2[cols, down], NT) * dup[at, cols]
        ulow[at, cols] = g.astype(BF)
        column_sum(v1024, 0, cols, g, m == 0)

    tiles(tokens, nf, 512, 512, up_back)

    def down_grad(m, n):
        grad[pl.ds(m, 512), pl.ds(width + n, 512)] = dot(
            hlow[:, pl.ds(m, 512)], clow[:, pl.ds(n, 512)], TN
        ).astype(BF)

    tiles(nf, width, 512, 512, down_grad)

    def second_back(m, n):
        gmid[pl.ds(m, 512), pl.ds(n, 512)] = dot(ulow[pl.ds(m, 512), :], wup[pl.ds(n, 512), :], NT)

    tiles(tokens, width, 512, 512, second_back)
    everything = slice(0, width)

    def middle_back(r):
        here = pl.ds(r, 64)
        start = r == 0
        m = mid[here, :]
        g = gmid[here, :]
        scale = norm_scale(m)
        n = m * scale
        column_sum(v512, 1, everything, g * n, start)
        g = g * gain
        gm = cot[here, :] + scale * (g - n * jnp.mean(g * n, axis=-1, keepdims=True))
        x = tok[here, :].astype(F32)
        pre = ext[here, :] + proj[here, :]
        s = sig(pre)
        u = upd[here, :]
        ge = gm * u * (s * (1.0 + pre * (1.0 - s)))
        gu = gm * (pre * s - x) * (u * (1.0 - u))
        gin[here, :] = gm * (1.0 - u)
        low = ge.astype(BF)
        elow[here, :] = low
        blre[here, pl.ds(nv, width)] = low
        blu[here, :] = gu.astype(BF)
        column_sum(v512, 2, everything, gu, start)
        column_sum(v512, 3, everything, ge, start)

    rows_loop(tokens, 64, middle_back)

    def gated_back(m, n):
        at, cols = pl.ds(m, 512), pl.ds(n, 512)
        g = dot(elow[at, :], w2[cols, pl.ds(0, width)], NT)
        gr = g * ad[at, cols].astype(F32)
        blre[at, cols] = gr.astype(BF)
        attg[at, cols] = (g * rs[at, cols].astype(F32)).astype(BF)
        column_sum(v1024, 1, cols, gr, m == 0)

    tiles(tokens, nv, 512, 512, gated_back)

    def attend_grad(m, n):
        grad[pl.ds(m, 512), pl.ds(n, 512)] = dot(
            glow[:, pl.ds(m, 512)], elow[:, pl.ds(n, 512)], TN
        ).astype(BF)

    tiles(nv, width, 512, 512, attend_grad)
    r2, r1 = rows2 // depth, rows1 // depth
    put_pieces(grad, own, sib, devices, depth, r2, 0, slice(0, 2 * width), slice(0, 2 * width))

    def up_grad(m, n):
        grad[pl.ds(m, 512), pl.ds(n, 512)] = dot(
            slow[:, pl.ds(m, 512)], ulow[:, pl.ds(n, 512)], TN
        ).astype(BF)

    tiles(width, nf, 512, 512, up_grad)
    put_pieces(grad, own, sib, devices, depth, r1, r2, slice(0, nf), slice(0, nf))


def back_kernel(*refs, devices, dims):
    pieces = refs[:devices]
    probs, attg, vlow, dval, qlow, klow, lat, blu, blre, z, nrm, pd, pz, dk, lab = refs[
        devices : devices + 15
    ]
    vgl, bll, gs, gnp, w512, w1024, w128, msg, ach = refs[devices + 15 : devices + 24]
    w, gq, gk, scr, sem = refs[devices + 24 :]
    tokens, width = z.shape
    nv = vlow.shape[1]
    zw = lat.shape[1]
    seqs = tokens // probs.shape[1]
    length = probs.shape[1]
    steps = tokens // SUBS
    rows = width // devices
    copies = load_weights(pieces, w, sem, rows, 0, w.shape[1], 0)
    row = lax.broadcasted_iota(jnp.int32, (length, length), 0)
    col = lax.broadcasted_iota(jnp.int32, (length, length), 1)

    def attend(r, total):
        here = pl.ds(pl.multiple_of(r * length, length), length)
        p = probs[here, :]
        plow = p.astype(BF)
        gp = dot(attg[here, :], vlow[here, :], NT)
        gsc = p * (gp - jnp.sum(p * gp, axis=-1, keepdims=True))
        low = gsc.astype(BF)
        gq[here, :] = dot(low, klow[here, :])
        gk[here, :] = dot(low, qlow[here, :], TN)
        for n in range(nv // 256):
            cols = slice(n * 256, (n + 1) * 256)
            gv = dot(plow, attg[here, cols], TN) * dval[here, cols].astype(F32)
            vgl[here, cols] = gv.astype(BF)
            column_sum(w1024, 0, cols, gv, r == 0)
        return total + gsc

    total = lax.fori_loop(0, seqs, attend, jnp.zeros((length, length), F32))
    flip = jnp.where((row + col) % length == 0, 1.0, 0.0)
    turned = lax.dot_general(
        total, flip, NN, precision=lax.Precision.HIGHEST, preferred_element_type=F32
    )
    turned = pltpu.roll(turned, 0, 1, stride=1, stride_axis=0)
    w128[...] = jnp.zeros_like(w128)
    w128[5:6, :] = jnp.sum(turned, axis=0, keepdims=True)

    def latent_back(r):
        here = pl.ds(r, 128)
        v = lat[here, :]
        s = sig(v)
        y = v * s
        q = gq[here, :] * zw ** (-0.5)
        k = gk[here, :]
        g = (q * pz[2:3, :] + k * pz[3:4, :]) * (s * (1.0 + v * (1.0 - s)))
        bll[here, :] = g.astype(BF)
        start = r == 0
        every = slice(0, zw)
        column_sum(w128, 0, every, g, start)
        column_sum(w128, 2, every, q * y, start)
        column_sum(w128, 3, every, k * y, start)
        column_sum(w128, 4, every, q, start)

    rows_loop(tokens, 128, latent_back)
    for c in copies:
        c.wait()
    at = split_sizes(width, zw, nv)

    def mixed_back(m, n):
        here, cols = pl.ds(m, 512), pl.ds(n, 512)
        g = dot(blu[here, :], w[cols, nv : nv + width], NT)
        g = g + dot(bll[here, :], w[cols, nv + at["l"] : nv + at["r"]], NT)
        g = g + dot(blre[here, :], w[cols, nv + at["r"] :], NT)
        v = z[here, cols]
        s = sig(v)
        g = g * (s * (1.0 + v * (1.0 - s)))
        t = n // TILE
        for j in range(512 // TILE):
            gs[t + j, here, :] = g[:, lanes_of(j)]
        column_sum(w512, 0, cols, g * two(nrm, t, here), m == 0)

    tiles(tokens, width, 512, 512, mixed_back)
    first, last = chunk_labels(lab, steps)
    one_way(gs, lab, first, dk, ach, dims, steps, width, True)
    power = dk[2 * dims : 3 * dims, :]
    through = (first == last) & (last == pltpu.roll(first, SUBS - 1, 0))
    for lt in range(width // TILE):
        lanes = lanes_of(lt)
        for h in range(dims):
            here = slice(h * SUBS, (h + 1) * SUBS)
            after = pltpu.roll(ach[here, lanes], SUBS - 1, 0) * power[h : h + 1, lanes]
            scr[here, :] = ach[here, lanes] + jnp.where(through, after, 0.0)
        half = SUBS // seqs
        msg[0 : dims * seqs, lanes] = scr[pl.ds(0, dims * seqs, stride=half), :].astype(BF)
        starts = lab[pl.ds(0, seqs, stride=length), :]
        tail = jnp.concatenate([starts, jnp.zeros((16 - seqs, TILE), F32)], axis=0)
        msg[dims * seqs : dims * seqs + 16, lanes] = tail.astype(BF)

    def normed_back(m, n):
        here, cols = pl.ds(m, 512), pl.ds(n, 512)
        omega = pd[4 * dims + 1 : 4 * dims + 2, cols]
        g = two(gs, n // TILE, here) * omega + dot(vgl[here, :], w[cols, 0:nv], NT)
        for j in range(512 // TILE):
            gnp[n // TILE + j, here, :] = g[:, lanes_of(j)]

    tiles(tokens, width, 512, 512, normed_back)


def two(ref, t, here):
    return jnp.concatenate([ref[t + j, here, :] for j in range(512 // TILE)], axis=1)


def weight_kernel(
    nlow, mlow, vgl, blu, bll, blre, own, sib, grad, *, devices, depth
):
    tokens, width = nlow.shape
    nv = vgl.shape[1]
    zw = bll.shape[1]
    at = split_sizes(width, zw, nv)

    def piece(lhs, rhs, start, cols):
        def fn(m, n):
            grad[pl.ds(m, 512), pl.ds(start + n, cols)] = dot(
                lhs[:, pl.ds(m, 512)], rhs[:, pl.ds(n, cols)], TN
            ).astype(BF)

        tiles(width, rhs.shape[1], 512, cols, fn)

    piece(nlow, vgl, 0, 512)
    piece(mlow, blu, nv, 512)
    piece(mlow, bll, nv + at["l"], zw)
    piece(mlow, blre, nv + at["r"], 512)
    full = slice(0, grad.shape[1])
    put_pieces(grad, own, sib, devices, depth, width // devices // depth, 0, full, full)


def last_kernel(*refs, reach, devices, dims, seqs, nm):
    sp, nrm, gs, gnp, lab, dk, ach = refs[:7]
    msgs = refs[7 : 7 + reach]
    tok, gin, pd, v512, v1024, w512, w1024, w128 = refs[7 + reach : 15 + reach]
    tg, own, sib = refs[15 + reach : 18 + reach]
    ent, lab_scr, gnb, sd, sv, sm, sums_ref = refs[18 + reach : 25 + reach]
    scr_refs = refs[25 + reach :]
    blocks, tokens, _ = nrm.shape
    width = tok.shape[1]
    steps = tokens // SUBS
    half = SUBS // seqs
    first, last = chunk_labels(lab, steps)
    place = lax.broadcasted_iota(jnp.int32, (SUBS, TILE), 0)
    odd = place % half == half - 1
    inside = first == last
    joined = last == pltpu.roll(first, SUBS - 1, 0)
    unroll = 4
    group = 8
    zero = jnp.zeros((SUBS, TILE), F32)

    def block(lt, _):
        lanes = pl.ds(pl.multiple_of(lt * TILE, TILE), TILE)
        power = dk[2 * dims : 3 * dims, lanes]
        arrivals = entering(msgs, lanes, last, odd, scr_refs, lab_scr, half - 1, dims, seqs, power)
        for h in range(dims):
            e = arrivals[h]
            here = slice(h * SUBS, (h + 1) * SUBS)
            onward = pltpu.roll(
                ach[here, lanes] + jnp.where(inside, e * power[h : h + 1, :], 0.0), SUBS - 1, 0
            )
            ent[here, :] = jnp.where(odd, e, jnp.where(joined, onward, 0.0))
        for base in range(0, dims, group):
            span = range(base, base + group)
            decay = [jnp.broadcast_to(dk[h : h + 1, lanes], (SUBS, TILE)) for h in span]
            weight = [
                jnp.broadcast_to(dk[dims + h : dims + h + 1, lanes], (SUBS, TILE)) for h in span
            ]

            def step(i, carry, base=base, decay=decay, weight=weight):
                after = carry[0]
                a, g0, g1 = (list(carry[1 + j * group : 1 + (j + 1) * group]) for j in range(3))
                for u in range(unroll):
                    t = steps - 1 - (i * unroll + u)
                    here = pl.ds(t, SUBS, stride=steps)
                    x = nrm[lt, here, :]
                    g = gs[lt, here, :]
                    l = lab[here, :]
                    same = l == after
                    after = l
                    sums = [gnp[lt, here, :] if base == 0 else gnb[lt, here, :], zero]
                    for j in range(group):
                        h = base + j
                        if j % 2 == 0:
                            pair = sp[lt, t, h * SUBS : (h + 2) * SUBS, :].astype(F32)
                        a[j] = decay[j] * jnp.where(same, a[j], 0.0) + g
                        g0[j] = g0[j] + a[j] * x
                        g1[j] = g1[j] + a[j] * pair[j % 2 * SUBS : (j % 2 + 1) * SUBS, :]
                        sums[j % 2] = sums[j % 2] + weight[j] * a[j]
                    gnb[lt, here, :] = sums[0] + sums[1]
                return (after,) + tuple(a) + tuple(g0) + tuple(g1)

            start = tuple(ent[h * SUBS : (h + 1) * SUBS, :] for h in span)
            done = lax.fori_loop(0, steps // unroll, step, (last,) + start + (zero,) * (2 * group))
            for j in range(group):
                h = base + j
                sums_ref[h : h + 1, lanes] = jnp.sum(done[1 + group + j], axis=0, keepdims=True)
                sums_ref[dims + h : dims + h + 1, lanes] = jnp.sum(
                    done[1 + 2 * group + j], axis=0, keepdims=True
                )
        return 0

    lax.fori_loop(0, blocks, block, 0)
    rate = 1.0 / (1.0 + jnp.exp(-pd[0:dims, :]))
    damping = 1.0 / (1.0 + jnp.exp(-pd[dims : 2 * dims, :]))
    beta, eta = pd[2 * dims : 3 * dims, :], pd[3 * dims : 4 * dims, :]
    g0 = sums_ref[0:dims, :]
    grad_decay = sums_ref[dims : 2 * dims, :] * eta * rate * beta
    grad_rate = g0 * eta * beta - damping * grad_decay
    sd[0:dims, :] = grad_rate * rate * (1.0 - rate)
    sd[dims : 2 * dims, :] = -grad_decay * rate * damping * (1.0 - damping)
    sd[2 * dims : 3 * dims, :] = g0 * rate * eta
    sd[3 * dims : 4 * dims, :] = g0 * rate * beta
    top = 4 * dims
    gain = pd[top : top + 1, :]
    sd[top : top + 8, :] = jnp.zeros((8, width), F32)

    def norm(r):
        here = pl.ds(r, 64)
        x = tok[here, :].astype(F32)
        q = norm_scale(x)
        m = x * q
        gn = jnp.concatenate([gnb[t, here, :] for t in range(blocks)], axis=1)
        sd[top : top + 1, :] += jnp.sum(gn * m, axis=0, keepdims=True)
        gn = gn * gain
        tg[here, :] = gin[here, :] + q * (gn - m * jnp.mean(gn * m, axis=-1, keepdims=True))

    rows_loop(tokens, 64, norm)
    sd[top + 1 : top + 2, :] = w512[0:1, :]
    sd[top + 2 : top + 3, :] = v512[1:2, :]
    sd[top + 3 : top + 4, :] = v512[0:1, :]
    nv = v1024.shape[1]
    zw = w128.shape[1]
    sv[...] = jnp.zeros_like(sv)
    sv[0:1, :] = w1024[0:1, :]
    sv[1:2, :] = v1024[0:1, :]
    at = split_sizes(width, zw, nv)
    sm[...] = jnp.zeros_like(sm)
    sm[0:1, 0:width] = v512[2:3, :]
    sm[0:1, at["l"] : at["r"]] = w128[0:1, :]
    sm[0:1, at["r"] : at["e"]] = v1024[1:2, :]
    sm[0:1, at["e"] : nm] = v512[3:4, :]
    me = lax.axis_index("seq")
    zrow = lax.broadcasted_iota(jnp.int32, (8, TILE), 0)
    zpart = jnp.where(zrow >= 2, w128[...], 0.0)
    for p in range(devices):
        k = me ^ p
        kc = k // 2

        def put(dst, p=p, kc=kc):
            dst[kc, 0:72, :] = sd[:, lanes_of(p * (width // devices) // TILE)]
            dst[kc, 72:80, :] = sv[:, lanes_of(p * (nv // devices) // TILE)] + zpart
            begin = p * (nm // devices) // TILE
            dst[kc, 80:88, :] = jnp.zeros((8, TILE), F32)
            for j in range(spread(nm // devices, devices)):
                dst[kc, 80 + j : 81 + j, :] = sm[0:1, lanes_of(begin + j)]

        pl.when(k % 2 == 0)(partial(put, own))
        pl.when(k % 2 == 1)(partial(put, sib))


def hop(x, axis, k):
    length = lax.axis_size(axis)
    return lax.ppermute(x, axis, [(i, i ^ k) for i in range(length)])


def fold_kernel(own, got, *outs):
    for k, out in enumerate(outs):
        out[...] = (own[k].astype(F32) + got[k].astype(F32)).astype(out.dtype)


def fold(own, sib, dtype):
    got = hop(sib, "seq", 1)
    outs = [struct(own.shape[1:], F32)] + [struct(own.shape[1:], dtype)] * (own.shape[0] - 1)
    return whole(fold_kernel, outs, n_in=2, name="fold")(own, got)


def across(parts):
    return [parts[0]] + [hop(part, "seq", 2 * k) for k, part in enumerate(parts) if k]


def deal_kernel(*refs, count, depth):
    ins, outs, scr = refs[:count], refs[count:-1], refs[-1]
    me = lax.axis_index("grp")
    total = ins[0][...]
    for other in ins[1:]:
        total = total + other[...].astype(F32)
    scr[...] = total
    for k in range(depth):
        outs[k][...] = scr[me ^ k].astype(outs[k].dtype)


def deal(parts, depth):
    shape = parts[0].shape
    outs = [struct(shape[1:], F32)] + [struct(shape[1:], BF)] * (depth - 1)
    body = partial(deal_kernel, count=len(parts), depth=depth)
    mine = whole(body, outs, [pltpu.VMEM(shape, F32)], n_in=len(parts), name="deal")(*parts)
    return [mine[0]] + [hop(part, "grp", k) for k, part in enumerate(mine) if k]


def join_kernel(*refs):
    total = refs[0][...]
    for other in refs[1:-1]:
        total = total + other[...].astype(F32)
    refs[-1][...] = total.astype(BF)


def join(parts):
    depth = len(parts)
    mine = whole(join_kernel, struct(parts[0].shape, BF), n_in=depth, name="join")(*parts)
    return [mine] + [hop(mine, "grp", k) for k in range(1, depth)]


def spread_a_kernel(*refs, depth, r2, width):
    ins, (attend, down, up, scr) = refs[:depth], refs[depth:]
    me = lax.axis_index("grp")
    for k in range(depth):
        scr[me ^ k] = ins[k][...].astype(F32)
    r1 = up.shape[0] // depth
    for z in range(depth):
        attend[z * r2 : (z + 1) * r2, :] = scr[z, 0:r2, 0:width]
        down[z * r2 : (z + 1) * r2, :] = scr[z, 0:r2, width:]
        up[z * r1 : (z + 1) * r1, :] = scr[z, r2:, :]


def spread_b_kernel(*refs, depth):
    ins, (value, mix, scr) = refs[:depth], refs[depth:]
    me = lax.axis_index("grp")
    for k in range(depth):
        scr[me ^ k] = ins[k][...].astype(F32)
    r = value.shape[0] // depth
    nv = value.shape[1]
    for z in range(depth):
        value[z * r : (z + 1) * r, :] = scr[z, :, 0:nv]
        mix[z * r : (z + 1) * r, :] = scr[z, :, nv:]


def final_kernel(*refs, depth, plan, held, dims):
    ins, decs = refs[:depth], refs[depth : depth + 4]
    vectors, scr = refs[depth + 4 : -1], refs[-1]
    grp, me = lax.axis_index("grp"), lax.axis_index("seq")
    for k in range(depth):
        scr[grp ^ k] = ins[k][...]
    total = scr[0]
    for z in range(1, depth):
        total = total + scr[z]
    pick = pick_lanes(me, held, TILE)
    for j, dec in enumerate(decs):
        dec[...] = lax.dot_general(
            total[j * dims : (j + 1) * dims, :], pick, NT,
            precision=lax.Precision.HIGHEST, preferred_element_type=F32,
        )
    for out, (at, count, n, nt) in zip(vectors, plan):
        lanes = nt * TILE
        for i in range(count):
            values = [total[at + i + j : at + i + j + 1, :] for j in range(nt)]
            values = values[0] if nt == 1 else jnp.concatenate(values, axis=1)
            values = jnp.broadcast_to(values, (SUBS, lanes))
            moved = pltpu.roll(values, (lanes - (me * n) % TILE) % lanes, 1)
            if count == 1:
                out[...] = moved[0:1, 0:n].reshape(n)
            else:
                out[i : i + 1, :] = moved[0:1, 0:n]


def total_kernel(*refs):
    total = refs[0][...]
    for other in refs[1:-1]:
        total = total + other[...]
    refs[-1][...] = total


def near_pieces(x, devices):
    return [x] + [hop(x, "seq", 2 * k) for k in range(1, devices // 2)]


def far_pieces(near):
    return [hop(part, "seq", 1) for part in near]


def woven(near, far):
    return [part for pair in zip(near, far) for part in pair]


def gather_pieces(x, devices):
    near = near_pieces(x, devices)
    return woven(near, far_pieces(near))


def after(x, *first):
    return lax.optimization_barrier((x, first))[0]


def per_device(
    tokens, segments, cotangent, first_gain, value_weight, value_bias, decay_alpha, decay_delta,
    decay_beta, decay_eta, skip_omega, mix_weight, mix_bias, latent_gains, query_offset,
    position_bias, attend_weight, second_gain, up_weight, up_bias, down_weight, down_bias,
):
    devices = lax.axis_size("seq")
    depth = lax.axis_size("grp")
    seqs, length, width = tokens.shape
    count = seqs * length
    steps = count // SUBS
    dims = decay_alpha.shape[1]
    nv = value_weight.shape[1]
    nf = up_weight.shape[1]
    nm = mix_weight.shape[1]
    zw = query_offset.shape[0] * devices
    reach = max(1, devices // 4)
    held = width // devices

    vectors = [
        (72, value_bias), (73, up_bias), (80, mix_bias), (64, first_gain), (65, skip_omega),
        (66, second_gain), (67, down_bias), (74, latent_gains), (76, query_offset),
        (77, position_bias),
    ]
    plan = []
    for at, v in vectors:
        n = v.shape[-1]
        plan.append((at, v.ndim, n, spread(n, devices)))
    decs = [d.T for d in (decay_alpha, decay_delta, decay_beta, decay_eta)]
    placed = whole(
        partial(place_kernel, plan=plan), struct((ROWS_SMALL, TILE), F32),
        n_in=4 + len(vectors), name="place", vmem=60,
    )(*decs, *[v for _, v in vectors])
    small = gather_pieces(placed, devices)

    w1, w2 = whole(
        pack_kernel,
        [struct((held, nv + nm), BF), struct((nv // devices + held, 2 * width), BF)],
        n_in=5,
        name="pack",
        vmem=60,
    )(*lax.optimization_barrier(
        (value_weight, mix_weight, attend_weight, down_weight, up_weight, small)
    )[:5])
    w1 = near_pieces(w1, devices)

    tok = tokens.reshape(count, width)
    cot = cotangent.reshape(count, width)
    blocks = width // TILE
    msg_rows = dims * seqs + 16
    pd, pv, pz, pm, dk, nrm, nlow, lab, fin, msg = whole(
        partial(head_kernel, devices=devices, dims=dims, nv=nv, nm=nm),
        [
            struct((72, width), F32), struct((8, nv), F32), struct((8, TILE), F32),
            struct((8, nm), F32), struct((3 * dims, width), F32), struct((blocks, count, TILE), F32),
            struct((count, width), BF), struct((count, TILE), F32),
            struct((dims * SUBS, width), F32), struct((msg_rows, width), BF),
        ],
        [pltpu.VMEM((dims * SUBS, TILE), F32), pltpu.VMEM((devices, ROWS_SMALL, TILE), F32)],
        n_in=devices + 2,
        name="head",
        micros=6,
    )(*small, tok, segments)

    w2 = near_pieces(after(w2, msg), devices)
    onward = [
        lax.ppermute(msg, "seq", [(i, i + k) for i in range(devices - k)])
        for k in range(1, reach + 1)
    ]

    arrivals = [pltpu.VMEM((dims * SUBS, TILE), F32)] * reach
    z, mlow, sp = whole(
        partial(scan_kernel, reach=reach, dims=dims, seqs=seqs),
        [
            struct((count, width), F32), struct((count, width), BF),
            struct((blocks, steps, dims * SUBS, TILE), BF),
        ],
        [
            pltpu.VMEM((dims * SUBS, TILE), F32), pltpu.VMEM((SUBS, TILE), F32),
            pltpu.VMEM((blocks, count, TILE), F32),
        ] + arrivals,
        n_in=5 + reach,
        name="scan",
        micros=8,
    )(nrm, lab, dk, pd, fin, *onward)

    early, late = w1[:-1], w1[-1:]
    w1 = woven(w1, far_pieces(after(early, onward)) + far_pieces(after(late, z)))

    def sems(n):
        return pltpu.SemaphoreType.DMA((n, devices))

    vlow, dval, upd, ext, lat, rs, ad, glow, probs, qlow, klow = whole(
        partial(front_kernel, devices=devices),
        [
            struct((count, nv), BF), struct((count, nv), BF), struct((count, width), F32),
            struct((count, width), F32), struct((count, zw), F32), struct((count, nv), BF),
            struct((count, nv), BF), struct((count, nv), BF), struct((count, length), F32),
            struct((count, zw), BF), struct((count, zw), BF),
        ],
        [pltpu.VMEM((width, nv + nm), BF), pltpu.VMEM((count, nv), F32), sems(1)],
        in_specs=[HB] * devices + [VM] * 7,
        name="front",
        micros=11,
    )(*w1, nlow, mlow, pv, pm, pz, lab, segments)

    w2 = woven(w2, far_pieces(after(w2, glow)))
    half = devices // 2
    rows2, rows1 = nv // devices // depth, held // depth
    piece_a = struct((half, depth, rows2 + rows1, 2 * width), BF)
    out, gin, attg, blu, blre, v512, v1024, own_a, sib_a = whole(
        partial(middle_kernel, devices=devices, depth=depth, dims=dims),
        [
            struct((count, width), F32), struct((count, width), F32), struct((count, nv), BF),
            struct((count, width), BF), struct((count, nv + width), BF), struct((8, width), F32),
            struct((8, nv), F32), piece_a, piece_a,
        ],
        [
            pltpu.VMEM((nv, 2 * width), BF), pltpu.VMEM((width, nf), BF),
            pltpu.VMEM((count, width), F32), pltpu.VMEM((count, width), F32),
            pltpu.VMEM((count, width), BF), pltpu.VMEM((count, nf), F32),
            pltpu.VMEM((count, nf), BF), pltpu.VMEM((count, width), BF),
            pltpu.VMEM((count, nf), BF), pltpu.VMEM((count, width), BF),
            pltpu.VMEM((count, width), F32), pltpu.VMEM((nv, 2 * width), BF), sems(2),
        ],
        in_specs=[HB] * devices + [VM] * 9,
        name="middle",
        micros=19,
    )(*w2, tok, cot, upd, ext, rs, ad, glow, pd, pv)

    vgl, bll, gs, gnp, w512, w1024, w128, back_msg, ach = whole(
        partial(back_kernel, devices=devices, dims=dims),
        [
            struct((count, nv), BF), struct((count, zw), BF), struct((blocks, count, TILE), F32),
            struct((blocks, count, TILE), F32), struct((8, width), F32), struct((8, nv), F32),
            struct((8, TILE), F32), struct((msg_rows, width), BF),
            struct((dims * SUBS, width), F32),
        ],
        [
            pltpu.VMEM((width, nv + nm), BF), pltpu.VMEM((count, zw), F32),
            pltpu.VMEM((count, zw), F32), pltpu.VMEM((dims * SUBS, TILE), F32), sems(1),
        ],
        in_specs=[HB] * devices + [VM] * 15,
        name="back",
        micros=15,
    )(*w1, probs, attg, vlow, dval, qlow, klow, lat, blu, blre, z, nrm, pd, pz, dk, lab)

    backward = [
        lax.ppermute(back_msg, "seq", [(i + k, i) for i in range(devices - k)])
        for k in range(1, reach + 1)
    ]

    piece_b = struct((half, depth, rows1, nv + nm), BF)
    own_b, sib_b = whole(
        partial(weight_kernel, devices=devices, depth=depth),
        [piece_b, piece_b],
        [pltpu.VMEM((width, nv + nm), BF)],
        n_in=6,
        name="weights",
        micros=6,
    )(nlow, mlow, vgl, blu, bll, blre)

    piece_c = struct((half, ROWS_SMALL, TILE), F32)
    wide = ceil_div(nm, TILE) + 2
    tokens_grad, own_c, sib_c = whole(
        partial(last_kernel, reach=reach, devices=devices, dims=dims, seqs=seqs, nm=nm),
        [struct((count, width), F32), piece_c, piece_c],
        [
            pltpu.VMEM((dims * SUBS, TILE), F32), pltpu.VMEM((SUBS, TILE), F32),
            pltpu.VMEM((blocks, count, TILE), F32), pltpu.VMEM((72, width), F32),
            pltpu.VMEM((8, nv), F32), pltpu.VMEM((8, wide * TILE), F32),
            pltpu.VMEM((2 * dims, width), F32),
        ] + arrivals,
        n_in=15 + reach,
        name="last",
        micros=12,
    )(sp, nrm, gs, gnp, lab, dk, ach, *backward, tok, gin, pd, v512, v1024, w512, w1024, w128)

    sum_a = join(deal(across(fold(own_a, sib_a, BF)), depth))
    attend_grad, down_grad, up_grad = whole(
        partial(spread_a_kernel, depth=depth, r2=rows2, width=width),
        [
            struct((nv // devices, width), F32), struct((nf // devices, width), F32),
            struct((held, nf), F32),
        ],
        [pltpu.VMEM((depth,) + piece_a.shape[2:], F32)],
        n_in=depth,
        name="spread_a",
    )(*sum_a)
    sum_b = join(deal(across(fold(own_b, sib_b, BF)), depth))
    value_grad, mix_grad = whole(
        partial(spread_b_kernel, depth=depth),
        [struct((held, nv), F32), struct((held, nm), F32)],
        [pltpu.VMEM((depth,) + piece_b.shape[2:], F32)],
        n_in=depth,
        name="spread_b",
    )(*sum_b)
    parts_c = across(fold(own_c, sib_c, F32))
    shard_c = whole(total_kernel, struct(piece_c.shape[1:], F32), n_in=half, name="total")(*parts_c)
    all_c = [shard_c] + [hop(shard_c, "grp", k) for k in range(1, depth)]
    alpha_g, delta_g, beta_g, eta_g, value_b, up_b, mix_b, first_g, omega, second_g, down_b, gains_g, qoff, posb = whole(
        partial(final_kernel, depth=depth, plan=plan, held=held, dims=dims),
        [struct((dims, held), F32)] * 4 + [struct(v.shape, F32) for _, v in vectors],
        [pltpu.VMEM((depth,) + piece_c.shape[1:], F32)],
        n_in=depth,
        name="final",
    )(*all_c)
    return (
        out.reshape(tokens.shape),
        tokens_grad.reshape(tokens.shape),
        first_g,
        value_grad,
        value_b,
        alpha_g.T,
        delta_g.T,
        beta_g.T,
        eta_g.T,
        omega,
        mix_grad,
        mix_b,
        gains_g,
        qoff,
        posb,
        attend_grad,
        second_g,
        up_grad,
        up_b,
        down_grad,
        down_b,
    )


def solution(mesh):
    vec, mat = P("seq"), P("seq", None)
    data = P("grp", "seq", None)
    params = (
        vec, mat, vec, mat, mat, mat, mat, vec, mat, vec, P(None, "seq"), vec, vec, mat, vec, mat,
        vec, mat, vec,
    )
    return jax.shard_map(
        per_device,
        mesh=mesh,
        in_specs=(data, P("grp", "seq"), data) + params,
        out_specs=(data, data) + params,
        check_vma=False,
    )
```

```python
from functools import partial

import jax
import jax.numpy as jnp
from jax import lax
from jax.experimental import pallas as pl
from jax.experimental.pallas import tpu as pltpu
from jax.sharding import PartitionSpec as P

EPSILON = 1e-06
F32 = jnp.float32
BF = jnp.bfloat16
TILE = 128
SUBS = 8
ROWS_SMALL = 88
NN = (((1,), (0,)), ((), ()))
NT = (((1,), (1,)), ((), ()))
TN = (((0,), (0,)), ((), ()))


def dot(a, b, dims=NN):
    return lax.dot_general(a, b, dims, preferred_element_type=F32)


def sig(v):
    return 0.5 * jnp.tanh(0.5 * v) + 0.5


def struct(shape, dtype):
    return jax.ShapeDtypeStruct(shape, dtype)


VM = pl.BlockSpec(memory_space=pltpu.VMEM)
HB = pl.BlockSpec(memory_space=pl.ANY)


def cost(micros):
    return pl.CostEstimate(flops=0, transcendentals=0, bytes_accessed=int(micros * 3.69e6))


def whole(body, outs, scratch=(), in_specs=None, n_in=None, name=None, micros=2, vmem=26):
    return pl.pallas_call(
        body,
        out_shape=outs,
        in_specs=in_specs if in_specs is not None else [VM] * n_in,
        out_specs=jax.tree.map(lambda _: VM, outs),
        scratch_shapes=list(scratch),
        compiler_params=pltpu.CompilerParams(vmem_limit_bytes=vmem << 20),
        cost_estimate=cost(micros),
        name=name,
    )


def tiles(m_size, n_size, tm, tn, fn):
    for n in range(0, n_size, tn):
        for m in range(0, m_size, tm):
            fn(m, n)


def rows_loop(total, step, fn):
    def body(i, _):
        fn(pl.multiple_of(i * step, step))
        return 0

    lax.fori_loop(0, total // step, body, 0)


def ceil_div(a, b):
    return -(-a // b)


def spread(n, devices):
    return max(ceil_div((d * n) % TILE + n, TILE) for d in range(devices))


def place_kernel(*refs, plan):
    me = lax.axis_index("seq")
    decs, vectors, out_ref = refs[:4], refs[4:-1], refs[-1]
    out_ref[...] = jnp.zeros_like(out_ref)
    dims, held = decs[0].shape
    pick = pick_lanes(me, held, TILE)
    for j, dec in enumerate(decs):
        out_ref[j * dims : (j + 1) * dims, :] = dot(dec[...], pick.astype(BF))
    source = 0
    for at, count, n, nt in plan:
        values = vectors[source][...].astype(F32)
        source += 1
        if count == 1:
            values = values.reshape(1, n)
        values = jnp.broadcast_to(values, (SUBS, n)) if count == 1 else values
        moved = dot(values.astype(BF), pick_lanes(me, n, nt * TILE).astype(BF))
        for i in range(count):
            for j in range(nt):
                out_ref[at + i + j : at + i + j + 1, :] = moved[i : i + 1, j * TILE : (j + 1) * TILE]


def pick_lanes(me, n, lanes):
    row = lax.broadcasted_iota(jnp.int32, (n, lanes), 0)
    lane = lax.broadcasted_iota(jnp.int32, (n, lanes), 1)
    return jnp.where(lane == row + (me * n) % TILE, 1.0, 0.0)


def pack_kernel(value, mix, attend, down, up, w1, w2):
    nv = value.shape[1]
    w1[:, 0:nv] = value[...]
    w1[:, nv:] = mix[...]
    rows, width = attend.shape
    w2[0:rows, 0:width] = attend[...]
    w2[0:rows, width:] = down[...]
    w2[rows:, :] = up[...]


def assemble(src, low, high, n, total, devices):
    parts = [None] * ceil_div(total, TILE)
    for d in range(devices):
        t = d * n // TILE
        block = src[d, low:high, :]
        parts[t] = block if parts[t] is None else parts[t] + block
    return parts


def chunk_labels(lab_ref, steps):
    return lab_ref[pl.ds(0, SUBS, stride=steps), :], lab_ref[pl.ds(steps - 1, SUBS, stride=steps), :]


def lanes_of(t):
    return slice(t * TILE, (t + 1) * TILE)


def padded(steps):
    return pltpu.VMEM((SUBS * (steps + 1), TILE), F32)


def stage(src, dst, steps):
    for c in range(SUBS):
        dst[c * (steps + 1) : c * (steps + 1) + steps, :] = src[pl.ds(c * steps, steps), :]


def unstage(src, dst, steps):
    for c in range(SUBS):
        dst[pl.ds(c * steps, steps), :] = src[c * (steps + 1) : c * (steps + 1) + steps, :]


def rows_at(t, steps):
    return pl.ds(t, SUBS, stride=steps + 1)


def one_way(
    src_ref, lab_ref, ref_label, dk_ref, out_ref, pads, dims, steps, width, reverse, unroll=8
):
    src_pad, lab_pad = pads
    stage(lab_ref, lab_pad, steps)
    for lt in range(width // TILE):
        lanes = lanes_of(lt)
        decay = [jnp.broadcast_to(dk_ref[h : h + 1, lanes], (SUBS, TILE)) for h in range(dims)]

        stage(src_ref.at[lt], src_pad, steps)

        def step(i, state, decay=decay):
            state = list(state)
            for u in range(unroll):
                t = i * unroll + u
                if reverse:
                    t = steps - 1 - t
                x = src_pad[rows_at(t, steps), :]
                l = lab_pad[rows_at(t, steps), :]
                x = jnp.where(l == ref_label, x, 0.0)
                state = [decay[h] * state[h] + x for h in range(dims)]
            return tuple(state)

        zero = jnp.zeros((SUBS, TILE), F32)
        final = lax.fori_loop(0, steps // unroll, step, (zero,) * dims)
        for h in range(dims):
            out_ref[h * SUBS : (h + 1) * SUBS, lanes] = final[h]


def norm_scale(x):
    return lax.rsqrt(jnp.mean(x * x, axis=-1, keepdims=True) + EPSILON)


def head_kernel(*refs, devices, dims, nv, nm):
    (
        tok_ref, seg_ref, pd_ref, pv_ref, pz_ref, pm_ref, dk_ref, nrm_ref, low_ref, lab_ref,
        fin_ref, msg_ref, scr_ref, small_ref, *pads
    ) = refs[2:]
    me = lax.axis_index("seq")
    for k in range(devices):
        small_ref[me ^ k] = refs[k % 2][k // 2]
    tokens, width = tok_ref.shape
    seqs, length = seg_ref.shape
    steps = tokens // SUBS
    for t, part in enumerate(assemble(small_ref, 0, 72, width // devices, width, devices)):
        pd_ref[:, lanes_of(t)] = part
    for t, part in enumerate(assemble(small_ref, 72, 80, nv // devices, nv, devices)):
        pv_ref[:, lanes_of(t)] = part
    z = small_ref[0, 72:80, :]
    for d in range(1, devices):
        z = z + small_ref[d, 72:80, :]
    pz_ref[...] = z
    n = nm // devices
    cells = [None] * (nm // TILE)
    for d in range(devices):
        first, lane = divmod(d * n, TILE)
        for j in range(ceil_div(lane + n, TILE)):
            piece = small_ref[d, 80 + j : 81 + j, :]
            cells[first + j] = piece if cells[first + j] is None else cells[first + j] + piece
    for t, piece in enumerate(cells):
        pm_ref[:, lanes_of(t)] = jnp.broadcast_to(piece, (SUBS, TILE))

    rate = 1.0 / (1.0 + jnp.exp(-pd_ref[0:dims, :]))
    damping = 1.0 / (1.0 + jnp.exp(-pd_ref[dims : 2 * dims, :]))
    decay = 1.0 - rate * damping
    dk_ref[0:dims, :] = decay
    dk_ref[dims : 2 * dims, :] = pd_ref[3 * dims : 4 * dims, :] * rate * pd_ref[2 * dims : 3 * dims, :]
    power, k = decay, 1
    while k < steps:
        power, k = power * power, k * 2
    dk_ref[2 * dims : 3 * dims, :] = power

    gain = pd_ref[4 * dims : 4 * dims + 1, :]

    def norm(r):
        x = tok_ref[pl.ds(r, 64), :].astype(F32)
        y = x * norm_scale(x) * gain
        for t in range(width // TILE):
            nrm_ref[t, pl.ds(r, 64), :] = y[:, lanes_of(t)]
        low_ref[pl.ds(r, 64), :] = y.astype(BF)

    rows_loop(tokens, 64, norm)

    labels = seg_ref[...].astype(F32)
    row = lax.broadcasted_iota(jnp.int32, (length, length), 0)
    col = lax.broadcasted_iota(jnp.int32, (length, length), 1)
    for s in range(seqs):
        diagonal = jnp.where(row == col, labels[s : s + 1, :], 0.0).astype(BF)
        lab_ref[s * length : (s + 1) * length, :] = dot(diagonal, jnp.ones((length, TILE), BF))

    first, last = chunk_labels(lab_ref, steps)
    one_way(nrm_ref, lab_ref, last, dk_ref, fin_ref, pads, dims, steps, width, False)
    through = (first == last) & (first == pltpu.roll(last, 1, 0))
    for lt in range(width // TILE):
        lanes = lanes_of(lt)
        for h in range(dims):
            own = fin_ref[h * SUBS : (h + 1) * SUBS, lanes]
            before = pltpu.roll(own, 1, 0) * power[h : h + 1, lanes]
            scr_ref[h * SUBS : (h + 1) * SUBS, :] = own + jnp.where(through, before, 0.0)
        half = SUBS // seqs
        msg_ref[0 : dims * seqs, lanes] = scr_ref[
            pl.ds(half - 1, dims * seqs, stride=half), :
        ].astype(BF)
        ends = lab_ref[pl.ds(length - 1, seqs, stride=length), :]
        tail = jnp.concatenate([ends, jnp.zeros((16 - seqs, TILE), F32)], axis=0)
        msg_ref[dims * seqs : dims * seqs + 16, lanes] = tail.astype(BF)


def entering(msgs, lanes, own_label, even, scr_refs, lab_scr, start, dims, seqs, power):
    half = SUBS // seqs
    gates = []
    for m, scr in zip(msgs, scr_refs):
        scr[pl.ds(start, dims * seqs, stride=half), :] = m[0 : dims * seqs, lanes].astype(F32)
        tail = m[dims * seqs : dims * seqs + 16, lanes].astype(F32)
        lab_scr[pl.ds(start, seqs, stride=half), :] = tail[0:seqs, :]
        gates.append(even & (lab_scr[...] == own_label))
    result = []
    for h in range(dims):
        total, reach = None, None
        for gate, scr in zip(gates, scr_refs):
            part = jnp.where(gate, scr[h * SUBS : (h + 1) * SUBS, :], 0.0)
            if total is None:
                total, reach = part, power[h : h + 1, :] * power[h : h + 1, :]
                far = reach
            else:
                total, far = total + part * far, far * reach
        result.append(total)
    return result


def scan_kernel(*refs, reach, dims, seqs):
    nrm_ref, lab_ref, dk_ref, pd_ref, fin_ref = refs[:5]
    msgs = refs[5 : 5 + reach]
    z_ref, mlow_ref, sp_ref = refs[5 + reach : 8 + reach]
    ent_ref, lab_scr, ys_ref, x_pad, lab_pad, y_pad = refs[8 + reach : 14 + reach]
    scr_refs = refs[14 + reach :]
    blocks, tokens, _ = nrm_ref.shape
    steps = tokens // SUBS
    half = SUBS // seqs
    first, last = chunk_labels(lab_ref, steps)
    place = lax.broadcasted_iota(jnp.int32, (SUBS, TILE), 0)
    even = place % half == 0
    inside = first == last
    joined = first == pltpu.roll(last, 1, 0)
    unroll = 4
    stage(lab_ref, lab_pad, steps)

    def block(lt, _):
        stage(nrm_ref.at[lt], x_pad, steps)
        lanes = pl.ds(pl.multiple_of(lt * TILE, TILE), TILE)
        power = dk_ref[2 * dims : 3 * dims, lanes]
        arrivals = entering(msgs, lanes, first, even, scr_refs, lab_scr, 0, dims, seqs, power)
        for h in range(dims):
            e = arrivals[h]
            own = fin_ref[h * SUBS : (h + 1) * SUBS, lanes]
            onward = pltpu.roll(own + jnp.where(inside, e * power[h : h + 1, :], 0.0), 1, 0)
            ent_ref[h * SUBS : (h + 1) * SUBS, :] = jnp.where(
                even, e, jnp.where(joined, onward, 0.0)
            )
        decay = [jnp.broadcast_to(dk_ref[h : h + 1, lanes], (SUBS, TILE)) for h in range(dims)]
        weight = [
            jnp.broadcast_to(dk_ref[dims + h : dims + h + 1, lanes], (SUBS, TILE))
            for h in range(dims)
        ]

        def step(i, carry):
            before, state = carry[0], list(carry[1:])
            for u in range(unroll):
                t = i * unroll + u
                x = x_pad[rows_at(t, steps), :]
                l = lab_pad[rows_at(t, steps), :]
                same = l == before
                before = l
                sums = [None] * 4
                for h in range(dims):
                    kept = jnp.where(same, state[h], 0.0)
                    if h % 2 == 0:
                        held = kept
                    else:
                        pair = jnp.concatenate([held, kept], axis=0)
                        sp_ref[lt, t, (h - 1) * SUBS : (h + 1) * SUBS, :] = pair.astype(BF)
                    state[h] = decay[h] * kept + x
                    term = weight[h] * state[h]
                    sums[h % 4] = term if sums[h % 4] is None else sums[h % 4] + term
                y_pad[rows_at(t, steps), :] = (sums[0] + sums[1]) + (
                    sums[2] + sums[3]
                )
            return (before,) + tuple(state)

        start = tuple(ent_ref[h * SUBS : (h + 1) * SUBS, :] for h in range(dims))
        lax.fori_loop(0, steps // unroll, step, (first,) + start)
        unstage(y_pad, ys_ref.at[lt], steps)
        return 0

    lax.fori_loop(0, blocks, block, 0)
    omega = pd_ref[4 * dims + 1 : 4 * dims + 2, :]

    def gate(r):
        for t in range(blocks):
            v = ys_ref[t, pl.ds(r, 128), :] + omega[:, lanes_of(t)] * nrm_ref[t, pl.ds(r, 128), :]
            z_ref[pl.ds(r, 128), lanes_of(t)] = v
            mlow_ref[pl.ds(r, 128), lanes_of(t)] = (v * sig(v)).astype(BF)

    rows_loop(tokens, 128, gate)


def load_weights(pieces, dst, sem, rows, start, cols, place):
    me = lax.axis_index("seq")
    copies = []
    for k in range(2 * pieces[0].shape[0]):
        p = me ^ k
        piece = pieces[k % 2].at[k // 2]
        copies.append(
            pltpu.make_async_copy(
                piece.at[pl.ds(start, rows), pl.ds(0, cols)],
                dst.at[pl.ds(pl.multiple_of(p * rows, rows), rows), pl.ds(0, cols)],
                sem.at[place, k],
            )
        )
    for c in copies:
        c.start()
    return copies


def split_sizes(width, latent, nv):
    return {"u": 0, "l": width, "r": width + latent, "e": width + latent + nv}


def front_kernel(*refs, devices):
    n = 2
    pieces = refs[:n]
    nlow, mlow, pv, pm, pz, lab, seg = refs[n : n + 7]
    vlow, dval, upd, ext, lat, rs, ad, glow, probs, qlow, klow = refs[n + 7 : n + 18]
    w, res, sem = refs[n + 18 :]
    tokens, width = nlow.shape
    nv = vlow.shape[1]
    zw = lat.shape[1]
    seqs, length = seg.shape
    rows = width // devices
    copies = load_weights(pieces, w, sem, rows, 0, w.shape[1], 0)
    for c in copies:
        c.wait()

    def value(m, n):
        v = dot(nlow[pl.ds(m, 512), :], w[:, pl.ds(n, 512)]) + pv[0:1, pl.ds(n, 512)]
        s = sig(v)
        vlow[pl.ds(m, 512), pl.ds(n, 512)] = (v * s).astype(BF)
        dval[pl.ds(m, 512), pl.ds(n, 512)] = (s * (1.0 + v * (1.0 - s))).astype(BF)

    tiles(tokens, nv, 512, 512, value)
    at = split_sizes(width, zw, nv)

    def base(m, n, start, size):
        cols = start + n
        wcols = nv + start + n
        return dot(mlow[pl.ds(m, 512), :], w[:, pl.ds(wcols, size)]) + pm[0:1, pl.ds(cols, size)]

    def update(m, n):
        upd[pl.ds(m, 512), pl.ds(n, 512)] = sig(base(m, n, at["u"], 512))

    tiles(tokens, width, 512, 512, update)

    def extra(m, n):
        ext[pl.ds(m, 512), pl.ds(n, 512)] = base(m, n, at["e"], 512)

    tiles(tokens, width, 512, 512, extra)

    def reset(m, n):
        res[pl.ds(m, 512), pl.ds(n, 512)] = base(m, n, at["r"], 512)

    tiles(tokens, nv, 512, 512, reset)

    def latent(m, n):
        v = base(m, n, at["l"], zw)
        lat[pl.ds(m, 512), :] = v
        y = v * sig(v)
        qlow[pl.ds(m, 512), :] = ((y * pz[2:3, :] + pz[4:5, :]) * zw ** (-0.5)).astype(BF)
        klow[pl.ds(m, 512), :] = (y * pz[3:4, :]).astype(BF)

    tiles(tokens, zw, 512, zw, latent)

    row = lax.broadcasted_iota(jnp.int32, (length, length), 0)
    col = lax.broadcasted_iota(jnp.int32, (length, length), 1)
    flip = jnp.where((row + col) % length == 0, 1.0, 0.0).astype(BF)
    bias = dot(pz[...].astype(BF), flip)[5:6, :]
    table = pltpu.roll(jnp.broadcast_to(bias, (length, length)), 0, 1, stride=1, stride_axis=0)
    causal = row >= col

    def attend(r):
        here = pl.ds(r, length)
        label_j = seg[pl.ds(r // length, 1), :].astype(F32)
        allowed = causal & (lab[here, :] == label_j)
        scores = dot(qlow[here, :], klow[here, :], NT) + table
        scores = jnp.where(allowed, scores, -1e30)
        weights = jnp.exp(scores - jnp.max(scores, axis=-1, keepdims=True))
        prob = weights / jnp.sum(weights, axis=-1, keepdims=True)
        probs[here, :] = prob
        plow = prob.astype(BF)
        for n in range(nv // 256):
            cols = slice(n * 256, (n + 1) * 256)
            a = dot(plow, vlow[here, cols])
            v = res[here, cols]
            s = sig(v)
            y = v * s
            rs[here, cols] = y.astype(BF)
            ad[here, cols] = (a * (s * (1.0 + v * (1.0 - s)))).astype(BF)
            glow[here, cols] = (a * y).astype(BF)

    rows_loop(tokens, length, attend)


def column_sum(ref, row, cols, values, first):
    total = jnp.sum(values, axis=0, keepdims=True)
    if isinstance(first, bool):
        ref[row : row + 1, cols] = total if first else ref[row : row + 1, cols] + total
        return

    @pl.when(first)
    def _():
        ref[row : row + 1, cols] = total

    @pl.when(jnp.logical_not(first))
    def _():
        ref[row : row + 1, cols] = ref[row : row + 1, cols] + total


def put_pieces(src, own, sib, devices, depth, rows, at, src_cols, cols):
    me = lax.axis_index("seq")
    for p in range(devices):
        k = me ^ p
        kc = k // 2

        def put(dst, p=p, kc=kc):
            for z in range(depth):
                begin = (p * depth + z) * rows
                dst[kc, z, at : at + rows, cols] = src[begin : begin + rows, src_cols].astype(BF)

        pl.when(k % 2 == 0)(partial(put, own))
        pl.when(k % 2 == 1)(partial(put, sib))


def middle_kernel(*refs, devices, depth, dims):
    n = 2
    pieces = refs[:n]
    tok, cot, upd, ext, rs, ad, glow, pd, pv = refs[n : n + 9]
    out, gin, attg, blu, blre, v512, v1024, own, sib = refs[n + 9 : n + 18]
    w2, wup, proj, mid, slow, dup, hlow, clow, ulow, elow, gmid, grad, sem = refs[n + 18 :]
    tokens, width = tok.shape
    nv = rs.shape[1]
    nf = dup.shape[1]
    rows2, rows1 = nv // devices, width // devices
    copies = load_weights(pieces, w2, sem, rows2, 0, 2 * width, 0)
    copies += load_weights(pieces, wup, sem, rows1, rows2, nf, 1)
    for c in copies:
        c.wait()
    down = pl.ds(width, width)

    def project(m, n):
        proj[pl.ds(m, 512), pl.ds(n, 512)] = dot(glow[pl.ds(m, 512), :], w2[:, pl.ds(n, 512)])

    tiles(tokens, width, 512, 512, project)
    gain = pd[4 * dims + 2 : 4 * dims + 3, :]

    def blend(r):
        here = pl.ds(r, 64)
        x = tok[here, :].astype(F32)
        pre = ext[here, :] + proj[here, :]
        s = sig(pre)
        m = x + upd[here, :] * (pre * s - x)
        mid[here, :] = m
        slow[here, :] = (m * norm_scale(m) * gain).astype(BF)

    rows_loop(tokens, 64, blend)

    def up(m, n):
        v = dot(slow[pl.ds(m, 512), :], wup[:, pl.ds(n, 512)]) + pv[1:2, pl.ds(n, 512)]
        s = sig(v)
        hlow[pl.ds(m, 512), pl.ds(n, 512)] = (v * s).astype(BF)
        dup[pl.ds(m, 512), pl.ds(n, 512)] = s * (1.0 + v * (1.0 - s))

    tiles(tokens, nf, 512, 512, up)

    def down_forward(m, n):
        at, cols = pl.ds(m, 512), pl.ds(n, 512)
        y = dot(hlow[at, :], w2[:, pl.ds(width + n, 512)])
        out[at, cols] = mid[at, cols] + y + pd[4 * dims + 3 : 4 * dims + 4, cols]
        c = cot[at, cols]
        clow[at, cols] = c.astype(BF)
        column_sum(v512, 0, cols, c, m == 0)

    tiles(tokens, width, 512, 512, down_forward)

    def up_back(m, n):
        at, cols = pl.ds(m, 512), pl.ds(n, 512)
        g = dot(clow[at, :], w2[cols, down], NT) * dup[at, cols]
        ulow[at, cols] = g.astype(BF)
        column_sum(v1024, 0, cols, g, m == 0)

    tiles(tokens, nf, 512, 512, up_back)

    def down_grad(m, n):
        grad[pl.ds(m, 512), pl.ds(width + n, 512)] = dot(
            hlow[:, pl.ds(m, 512)], clow[:, pl.ds(n, 512)], TN
        ).astype(BF)

    tiles(nf, width, 512, 512, down_grad)

    def second_back(m, n):
        gmid[pl.ds(m, 512), pl.ds(n, 512)] = dot(ulow[pl.ds(m, 512), :], wup[pl.ds(n, 512), :], NT)

    tiles(tokens, width, 512, 512, second_back)
    everything = slice(0, width)

    def middle_back(r):
        here = pl.ds(r, 64)
        start = r == 0
        m = mid[here, :]
        g = gmid[here, :]
        scale = norm_scale(m)
        n = m * scale
        column_sum(v512, 1, everything, g * n, start)
        g = g * gain
        gm = cot[here, :] + scale * (g - n * jnp.mean(g * n, axis=-1, keepdims=True))
        x = tok[here, :].astype(F32)
        pre = ext[here, :] + proj[here, :]
        s = sig(pre)
        u = upd[here, :]
        ge = gm * u * (s * (1.0 + pre * (1.0 - s)))
        gu = gm * (pre * s - x) * (u * (1.0 - u))
        gin[here, :] = gm * (1.0 - u)
        low = ge.astype(BF)
        elow[here, :] = low
        blre[here, pl.ds(nv, width)] = low
        blu[here, :] = gu.astype(BF)
        column_sum(v512, 2, everything, gu, start)
        column_sum(v512, 3, everything, ge, start)

    rows_loop(tokens, 64, middle_back)

    def gated_back(m, n):
        at, cols = pl.ds(m, 512), pl.ds(n, 512)
        g = dot(elow[at, :], w2[cols, pl.ds(0, width)], NT)
        gr = g * ad[at, cols].astype(F32)
        blre[at, cols] = gr.astype(BF)
        attg[at, cols] = (g * rs[at, cols].astype(F32)).astype(BF)
        column_sum(v1024, 1, cols, gr, m == 0)

    tiles(tokens, nv, 512, 512, gated_back)

    def attend_grad(m, n):
        grad[pl.ds(m, 512), pl.ds(n, 512)] = dot(
            glow[:, pl.ds(m, 512)], elow[:, pl.ds(n, 512)], TN
        ).astype(BF)

    tiles(nv, width, 512, 512, attend_grad)
    r2, r1 = rows2 // depth, rows1 // depth
    put_pieces(grad, own, sib, devices, depth, r2, 0, slice(0, 2 * width), slice(0, 2 * width))

    def up_grad(m, n):
        grad[pl.ds(m, 512), pl.ds(n, 512)] = dot(
            slow[:, pl.ds(m, 512)], ulow[:, pl.ds(n, 512)], TN
        ).astype(BF)

    tiles(width, nf, 512, 512, up_grad)
    put_pieces(grad, own, sib, devices, depth, r1, r2, slice(0, nf), slice(0, nf))


def back_kernel(*refs, devices, dims):
    n = 2
    pieces = refs[:n]
    probs, attg, vlow, dval, qlow, klow, lat, blu, blre, z, nrm, pd, pz, dk, lab = refs[
        n : n + 15
    ]
    vgl, bll, gs, gnp, w512, w1024, w128, msg, ach = refs[n + 15 : n + 24]
    w, gq, gk, scr, sem, *pads = refs[n + 24 :]
    tokens, width = z.shape
    nv = vlow.shape[1]
    zw = lat.shape[1]
    seqs = tokens // probs.shape[1]
    length = probs.shape[1]
    steps = tokens // SUBS
    rows = width // devices
    copies = load_weights(pieces, w, sem, rows, 0, w.shape[1], 0)
    row = lax.broadcasted_iota(jnp.int32, (length, length), 0)
    col = lax.broadcasted_iota(jnp.int32, (length, length), 1)

    def attend(r, total):
        here = pl.ds(pl.multiple_of(r * length, length), length)
        p = probs[here, :]
        plow = p.astype(BF)
        gp = dot(attg[here, :], vlow[here, :], NT)
        gsc = p * (gp - jnp.sum(p * gp, axis=-1, keepdims=True))
        low = gsc.astype(BF)
        gq[here, :] = dot(low, klow[here, :])
        gk[here, :] = dot(low, qlow[here, :], TN)
        for n in range(nv // 256):
            cols = slice(n * 256, (n + 1) * 256)
            gv = dot(plow, attg[here, cols], TN) * dval[here, cols].astype(F32)
            vgl[here, cols] = gv.astype(BF)
            column_sum(w1024, 0, cols, gv, r == 0)
        return total + gsc

    total = lax.fori_loop(0, seqs, attend, jnp.zeros((length, length), F32))
    flip = jnp.where((row + col) % length == 0, 1.0, 0.0)
    turned = lax.dot_general(
        total, flip, NN, precision=lax.Precision.HIGHEST, preferred_element_type=F32
    )
    turned = pltpu.roll(turned, 0, 1, stride=1, stride_axis=0)
    w128[...] = jnp.zeros_like(w128)
    w128[5:6, :] = jnp.sum(turned, axis=0, keepdims=True)

    def latent_back(r):
        here = pl.ds(r, 128)
        v = lat[here, :]
        s = sig(v)
        y = v * s
        q = gq[here, :] * zw ** (-0.5)
        k = gk[here, :]
        g = (q * pz[2:3, :] + k * pz[3:4, :]) * (s * (1.0 + v * (1.0 - s)))
        bll[here, :] = g.astype(BF)
        start = r == 0
        every = slice(0, zw)
        column_sum(w128, 0, every, g, start)
        column_sum(w128, 2, every, q * y, start)
        column_sum(w128, 3, every, k * y, start)
        column_sum(w128, 4, every, q, start)

    rows_loop(tokens, 128, latent_back)
    for c in copies:
        c.wait()
    at = split_sizes(width, zw, nv)

    def mixed_back(m, n):
        here, cols = pl.ds(m, 512), pl.ds(n, 512)
        g = dot(blu[here, :], w[cols, nv : nv + width], NT)
        g = g + dot(bll[here, :], w[cols, nv + at["l"] : nv + at["r"]], NT)
        g = g + dot(blre[here, :], w[cols, nv + at["r"] :], NT)
        v = z[here, cols]
        s = sig(v)
        g = g * (s * (1.0 + v * (1.0 - s)))
        t = n // TILE
        for j in range(512 // TILE):
            gs[t + j, here, :] = g[:, lanes_of(j)]
        column_sum(w512, 0, cols, g * two(nrm, t, here), m == 0)

    tiles(tokens, width, 512, 512, mixed_back)
    first, last = chunk_labels(lab, steps)
    one_way(gs, lab, first, dk, ach, pads, dims, steps, width, True)
    power = dk[2 * dims : 3 * dims, :]
    through = (first == last) & (last == pltpu.roll(first, SUBS - 1, 0))
    for lt in range(width // TILE):
        lanes = lanes_of(lt)
        for h in range(dims):
            here = slice(h * SUBS, (h + 1) * SUBS)
            after = pltpu.roll(ach[here, lanes], SUBS - 1, 0) * power[h : h + 1, lanes]
            scr[here, :] = ach[here, lanes] + jnp.where(through, after, 0.0)
        half = SUBS // seqs
        msg[0 : dims * seqs, lanes] = scr[pl.ds(0, dims * seqs, stride=half), :].astype(BF)
        starts = lab[pl.ds(0, seqs, stride=length), :]
        tail = jnp.concatenate([starts, jnp.zeros((16 - seqs, TILE), F32)], axis=0)
        msg[dims * seqs : dims * seqs + 16, lanes] = tail.astype(BF)

    def normed_back(m, n):
        here, cols = pl.ds(m, 512), pl.ds(n, 512)
        omega = pd[4 * dims + 1 : 4 * dims + 2, cols]
        g = two(gs, n // TILE, here) * omega + dot(vgl[here, :], w[cols, 0:nv], NT)
        for j in range(512 // TILE):
            gnp[n // TILE + j, here, :] = g[:, lanes_of(j)]

    tiles(tokens, width, 512, 512, normed_back)


def two(ref, t, here):
    return jnp.concatenate([ref[t + j, here, :] for j in range(512 // TILE)], axis=1)


def weight_kernel(
    nlow, mlow, vgl, blu, bll, blre, own, sib, grad, *, devices, depth
):
    tokens, width = nlow.shape
    nv = vgl.shape[1]
    zw = bll.shape[1]
    at = split_sizes(width, zw, nv)

    def piece(lhs, rhs, start, cols):
        def fn(m, n):
            grad[pl.ds(m, 512), pl.ds(start + n, cols)] = dot(
                lhs[:, pl.ds(m, 512)], rhs[:, pl.ds(n, cols)], TN
            ).astype(BF)

        tiles(width, rhs.shape[1], 512, cols, fn)

    piece(nlow, vgl, 0, 512)
    piece(mlow, blu, nv, 512)
    piece(mlow, bll, nv + at["l"], zw)
    piece(mlow, blre, nv + at["r"], 512)
    full = slice(0, grad.shape[1])
    put_pieces(grad, own, sib, devices, depth, width // devices // depth, 0, full, full)


def last_kernel(*refs, reach, devices, dims, seqs, nm):
    sp, nrm, gs, gnp, lab, dk, ach = refs[:7]
    msgs = refs[7 : 7 + reach]
    tok, gin, pd, v512, v1024, w512, w1024, w128 = refs[7 + reach : 15 + reach]
    tg, own, sib = refs[15 + reach : 18 + reach]
    ent, lab_scr, gnb, sd, sv, sm, sums_ref = refs[18 + reach : 25 + reach]
    lab_pad, x_pad, g_pad, n_pad = refs[25 + reach : 29 + reach]
    scr_refs = refs[29 + reach :]
    blocks, tokens, _ = nrm.shape
    width = tok.shape[1]
    steps = tokens // SUBS
    half = SUBS // seqs
    first, last = chunk_labels(lab, steps)
    place = lax.broadcasted_iota(jnp.int32, (SUBS, TILE), 0)
    odd = place % half == half - 1
    inside = first == last
    joined = last == pltpu.roll(first, SUBS - 1, 0)
    unroll = 4
    group = 8
    zero = jnp.zeros((SUBS, TILE), F32)
    stage(lab, lab_pad, steps)

    def block(lt, _):
        stage(nrm.at[lt], x_pad, steps)
        stage(gs.at[lt], g_pad, steps)
        stage(gnp.at[lt], n_pad, steps)
        lanes = pl.ds(pl.multiple_of(lt * TILE, TILE), TILE)
        power = dk[2 * dims : 3 * dims, lanes]
        arrivals = entering(msgs, lanes, last, odd, scr_refs, lab_scr, half - 1, dims, seqs, power)
        for h in range(dims):
            e = arrivals[h]
            here = slice(h * SUBS, (h + 1) * SUBS)
            onward = pltpu.roll(
                ach[here, lanes] + jnp.where(inside, e * power[h : h + 1, :], 0.0), SUBS - 1, 0
            )
            ent[here, :] = jnp.where(odd, e, jnp.where(joined, onward, 0.0))
        for base in range(0, dims, group):
            span = range(base, base + group)
            decay = [jnp.broadcast_to(dk[h : h + 1, lanes], (SUBS, TILE)) for h in span]
            weight = [
                jnp.broadcast_to(dk[dims + h : dims + h + 1, lanes], (SUBS, TILE)) for h in span
            ]

            def step(i, carry, base=base, decay=decay, weight=weight):
                after = carry[0]
                a, g0, g1 = (list(carry[1 + j * group : 1 + (j + 1) * group]) for j in range(3))
                for u in range(unroll):
                    t = steps - 1 - (i * unroll + u)
                    here = rows_at(t, steps)
                    x = x_pad[here, :]
                    g = g_pad[here, :]
                    l = lab_pad[here, :]
                    same = l == after
                    after = l
                    sums = [n_pad[here, :], zero]
                    for j in range(group):
                        h = base + j
                        if j % 2 == 0:
                            pair = sp[lt, t, h * SUBS : (h + 2) * SUBS, :].astype(F32)
                        a[j] = decay[j] * jnp.where(same, a[j], 0.0) + g
                        g0[j] = g0[j] + a[j] * x
                        g1[j] = g1[j] + a[j] * pair[j % 2 * SUBS : (j % 2 + 1) * SUBS, :]
                        sums[j % 2] = sums[j % 2] + weight[j] * a[j]
                    n_pad[here, :] = sums[0] + sums[1]
                return (after,) + tuple(a) + tuple(g0) + tuple(g1)

            start = tuple(ent[h * SUBS : (h + 1) * SUBS, :] for h in span)
            done = lax.fori_loop(0, steps // unroll, step, (last,) + start + (zero,) * (2 * group))
            for j in range(group):
                h = base + j
                sums_ref[h : h + 1, lanes] = jnp.sum(done[1 + group + j], axis=0, keepdims=True)
                sums_ref[dims + h : dims + h + 1, lanes] = jnp.sum(
                    done[1 + 2 * group + j], axis=0, keepdims=True
                )
        unstage(n_pad, gnb.at[lt], steps)
        return 0

    lax.fori_loop(0, blocks, block, 0)
    rate = 1.0 / (1.0 + jnp.exp(-pd[0:dims, :]))
    damping = 1.0 / (1.0 + jnp.exp(-pd[dims : 2 * dims, :]))
    beta, eta = pd[2 * dims : 3 * dims, :], pd[3 * dims : 4 * dims, :]
    g0 = sums_ref[0:dims, :]
    grad_decay = sums_ref[dims : 2 * dims, :] * eta * rate * beta
    grad_rate = g0 * eta * beta - damping * grad_decay
    sd[0:dims, :] = grad_rate * rate * (1.0 - rate)
    sd[dims : 2 * dims, :] = -grad_decay * rate * damping * (1.0 - damping)
    sd[2 * dims : 3 * dims, :] = g0 * rate * eta
    sd[3 * dims : 4 * dims, :] = g0 * rate * beta
    top = 4 * dims
    gain = pd[top : top + 1, :]
    sd[top : top + 8, :] = jnp.zeros((8, width), F32)

    def norm(r):
        here = pl.ds(r, 64)
        x = tok[here, :].astype(F32)
        q = norm_scale(x)
        m = x * q
        gn = jnp.concatenate([gnb[t, here, :] for t in range(blocks)], axis=1)
        sd[top : top + 1, :] += jnp.sum(gn * m, axis=0, keepdims=True)
        gn = gn * gain
        tg[here, :] = gin[here, :] + q * (gn - m * jnp.mean(gn * m, axis=-1, keepdims=True))

    rows_loop(tokens, 64, norm)
    sd[top + 1 : top + 2, :] = w512[0:1, :]
    sd[top + 2 : top + 3, :] = v512[1:2, :]
    sd[top + 3 : top + 4, :] = v512[0:1, :]
    nv = v1024.shape[1]
    zw = w128.shape[1]
    sv[...] = jnp.zeros_like(sv)
    sv[0:1, :] = w1024[0:1, :]
    sv[1:2, :] = v1024[0:1, :]
    at = split_sizes(width, zw, nv)
    sm[...] = jnp.zeros_like(sm)
    sm[0:1, 0:width] = v512[2:3, :]
    sm[0:1, at["l"] : at["r"]] = w128[0:1, :]
    sm[0:1, at["r"] : at["e"]] = v1024[1:2, :]
    sm[0:1, at["e"] : nm] = v512[3:4, :]
    me = lax.axis_index("seq")
    zrow = lax.broadcasted_iota(jnp.int32, (8, TILE), 0)
    zpart = jnp.where(zrow >= 2, w128[...], 0.0)
    for p in range(devices):
        k = me ^ p
        kc = k // 2

        def put(dst, p=p, kc=kc):
            dst[kc, 0:72, :] = sd[:, lanes_of(p * (width // devices) // TILE)]
            dst[kc, 72:80, :] = sv[:, lanes_of(p * (nv // devices) // TILE)] + zpart
            begin = p * (nm // devices) // TILE
            dst[kc, 80:88, :] = jnp.zeros((8, TILE), F32)
            for j in range(spread(nm // devices, devices)):
                dst[kc, 80 + j : 81 + j, :] = sm[0:1, lanes_of(begin + j)]

        pl.when(k % 2 == 0)(partial(put, own))
        pl.when(k % 2 == 1)(partial(put, sib))


def hop(x, axis, k):
    length = lax.axis_size(axis)
    return lax.ppermute(x, axis, [(i, i ^ k) for i in range(length)])


def fold_kernel(own, got, *outs):
    for k, out in enumerate(outs):
        out[...] = (own[k].astype(F32) + got[k].astype(F32)).astype(out.dtype)


def fold(own, sib, dtype):
    got = hop(sib, "seq", 1)
    outs = [struct(own.shape[1:], F32)] + [struct(own.shape[1:], dtype)] * (own.shape[0] - 1)
    return whole(fold_kernel, outs, n_in=2, name="fold")(own, got)


def across(parts):
    return [parts[0]] + [hop(part, "seq", 2 * k) for k, part in enumerate(parts) if k]


def split_kernel(own, got, kept, to_x, to_y, later_x, later_y):
    h = own.shape[1] // 2
    top, low = slice(0, h), slice(h, None)

    def piece(k, part):
        return own[k, part].astype(F32) + got[k, part].astype(F32)

    kept[...] = own[0].astype(F32) + got[0].astype(F32)
    to_x[top] = piece(1, top).astype(BF)
    to_x[low] = piece(3, top).astype(BF)
    to_y[top] = piece(2, low).astype(BF)
    to_y[low] = piece(3, low).astype(BF)
    later_x[...] = piece(1, low)
    later_y[...] = piece(2, top)


def split(own, sib):
    got = hop(sib, "seq", 1)
    shape = own.shape[1:]
    half = (shape[0] // 2,) + shape[1:]
    return whole(
        split_kernel,
        [struct(shape, F32), struct(shape, BF), struct(shape, BF), struct(half, F32), struct(half, F32)],
        n_in=2,
        name="split",
    )(own, got)


def turn_kernel(from_x, from_y, later_x, later_y, to_x, to_y):
    h = later_x.shape[0]
    to_x[...] = (later_x[...] + from_y[h:].astype(F32)).astype(BF)
    to_y[...] = (later_y[...] + from_x[h:].astype(F32)).astype(BF)


def spread_sums(own, sib, devices, tie):
    if devices != 8:
        parts = across(fold(own, sib, BF))
        return parts[:1], parts[:1], lambda *first: parts
    kept, to_x, to_y, later_x, later_y = split(own, sib)
    from_x, from_y = hop(to_x, "seq", 2), hop(to_y, "seq", 4)

    def finish(*first):
        fx, fy = after((from_x, from_y), *first)
        half = struct(later_x.shape, BF)
        qx, qy = whole(turn_kernel, [half, half], n_in=4, name="turn")(fx, fy, later_x, later_y)
        return [kept, fx, fy, hop(qx, "seq", 2), hop(qy, "seq", 4)]

    return [kept], [from_x, from_y], finish


def deal_kernel(*refs, count, depth, halves):
    ins, outs, scr = refs[:count], refs[count:-1], refs[-1]
    me = lax.axis_index("grp")
    if halves:
        kept, from_x, from_y, last_x, last_y = ins
        h = depth // 2
        scr[0:h] = kept[0:h] + from_x[0:h].astype(F32) + last_y[...].astype(F32)
        scr[h:] = kept[h:] + from_y[0:h].astype(F32) + last_x[...].astype(F32)
    else:
        total = ins[0][...]
        for other in ins[1:]:
            total = total + other[...].astype(F32)
        scr[...] = total
    for k in range(depth):
        outs[k][...] = scr[me ^ k].astype(outs[k].dtype)


def deal(parts, depth, devices):
    shape = parts[0].shape
    outs = [struct(shape[1:], F32)] + [struct(shape[1:], BF)] * (depth - 1)
    body = partial(deal_kernel, count=len(parts), depth=depth, halves=devices == 8)
    mine = whole(body, outs, [pltpu.VMEM(shape, F32)], n_in=len(parts), name="deal")(*parts)
    return [mine[0]] + [hop(part, "grp", k) for k, part in enumerate(mine) if k]


def join_kernel(*refs, depth, half):
    part_a, part_b = refs[:depth], refs[depth : 2 * depth]
    part_c, out, c_scr = refs[2 * depth : 2 * depth + half], refs[-2], refs[-1]
    a, b = part_a[0][...], part_b[0][...]
    for k in range(1, depth):
        a, b = a + part_a[k][...].astype(F32), b + part_b[k][...].astype(F32)
    c = part_c[0][...]
    for other in part_c[1:]:
        c = c + other[...]
    rows, lanes = out.shape[0], a.shape[1]
    for j in range(a.shape[0] // rows):
        out[:, j * lanes : (j + 1) * lanes] = a[j * rows : (j + 1) * rows, :].astype(BF)
    at = a.shape[0] // rows * lanes
    out[:, at : at + b.shape[1]] = b.astype(BF)
    at += b.shape[1]
    c_scr[...] = jnp.zeros_like(c_scr)
    c_scr[0 : c.shape[0], :] = c
    for j in range(c_scr.shape[0] // rows):
        out[:, at + j * TILE : at + (j + 1) * TILE] = c_scr[j * rows : (j + 1) * rows, :].astype(BF)


def join(sum_a, sum_b, parts_c):
    depth, rows = len(sum_a), sum_b[0].shape[0]
    blocks_c = ceil_div(ROWS_SMALL, rows)
    wide = sum_a[0].shape[0] // rows * sum_a[0].shape[1] + sum_b[0].shape[1] + blocks_c * TILE
    mine = whole(
        partial(join_kernel, depth=depth, half=len(parts_c)), struct((rows, wide), BF),
        [pltpu.VMEM((blocks_c * rows, TILE), F32)],
        n_in=2 * depth + len(parts_c), name="join",
    )(*sum_a, *sum_b, *parts_c)
    return [mine] + [hop(mine, "grp", k) for k in range(1, depth)]


def final_kernel(*refs, depth, plan, held, dims):
    ins, (attend, down, up, value, mix) = refs[:depth], refs[depth : depth + 5]
    decs, vectors = refs[depth + 5 : depth + 9], refs[depth + 9 : -2]
    scr, c_scr = refs[-2:]
    grp, me = lax.axis_index("grp"), lax.axis_index("seq")
    for k in range(depth):
        scr[grp ^ k] = ins[k][...].astype(F32)
    rows, width = scr.shape[1], attend.shape[1]
    wide, nv = 2 * width, value.shape[1]
    folds = attend.shape[0] // depth // rows
    for z in range(depth):
        for j in range(folds):
            at = (z * folds + j) * rows
            attend[at : at + rows, :] = scr[z, :, j * wide : j * wide + width]
            down[at : at + rows, :] = scr[z, :, j * wide + width : (j + 1) * wide]
        at = folds * wide
        here = slice(z * rows, (z + 1) * rows)
        up[here, :] = scr[z, :, at : at + wide]
        at += wide
        value[here, :] = scr[z, :, at : at + nv]
        mix[here, :] = scr[z, :, at + nv : at + nv + mix.shape[1]]
    at = (folds + 1) * wide + nv + mix.shape[1]
    for j in range(c_scr.shape[0] // rows):
        cols = slice(at + j * TILE, at + (j + 1) * TILE)
        block = scr[0, :, cols]
        for z in range(1, depth):
            block = block + scr[z, :, cols]
        c_scr[j * rows : (j + 1) * rows, :] = block
    total = c_scr[...]
    pick = pick_lanes(me, held, TILE)
    for j, dec in enumerate(decs):
        dec[...] = lax.dot_general(
            total[j * dims : (j + 1) * dims, :], pick, NT,
            precision=lax.Precision.HIGHEST, preferred_element_type=F32,
        )
    for out, (at, count, n, nt) in zip(vectors, plan):
        lanes = nt * TILE
        for i in range(count):
            values = [total[at + i + j : at + i + j + 1, :] for j in range(nt)]
            values = values[0] if nt == 1 else jnp.concatenate(values, axis=1)
            values = jnp.broadcast_to(values, (SUBS, lanes))
            moved = pltpu.roll(values, (lanes - (me * n) % TILE) % lanes, 1)
            if count == 1:
                out[...] = moved[0:1, 0:n].reshape(n)
            else:
                out[i : i + 1, :] = moved[0:1, 0:n]


def near_pieces(x, devices):
    return [x] + [hop(x, "seq", 2 * k) for k in range(1, devices // 2)]


def bundle_kernel(*refs, halves):
    ins, out = refs[:-1], refs[-1]
    for k, ref in enumerate(ins[: out.shape[0] - halves]):
        out[k] = ref[...]
    if halves:
        rows = out.shape[1] // 2
        out[out.shape[0] - 1, 0:rows, :] = ins[-2][...]
        out[out.shape[0] - 1, rows:, :] = ins[-1][...]


def bundle(parts, halves=0):
    shape = (len(parts) - halves,) + parts[0].shape
    return whole(
        partial(bundle_kernel, halves=halves), struct(shape, parts[0].dtype), n_in=len(parts),
        name="bundle",
    )(*parts)


def with_far(both):
    return [both, hop(both, "seq", 1)]


def relay_kernel(x, y, top, bottom):
    rows = top.shape[0]
    top[...] = x[0:rows, :]
    bottom[...] = y[rows:, :]


def relay(x, y):
    half = struct((x.shape[0] // 2, x.shape[1]), x.dtype)
    top, bottom = whole(relay_kernel, [half, half], n_in=2, name="relay")(x, y)
    return [hop(top, "seq", 4), hop(bottom, "seq", 2)]


def first_pieces(x, devices):
    near = 3 if devices == 8 else devices // 2
    return [x] + [hop(x, "seq", 2 * k) for k in range(1, near)]


def more_pieces(parts, devices, *first):
    if devices != 8:
        return parts
    x, y = after(parts[1:3], *first)
    return parts + relay(x, y)


def after(x, *first):
    return lax.optimization_barrier((x, first))[0]


def per_device(
    tokens, segments, cotangent, first_gain, value_weight, value_bias, decay_alpha, decay_delta,
    decay_beta, decay_eta, skip_omega, mix_weight, mix_bias, latent_gains, query_offset,
    position_bias, attend_weight, second_gain, up_weight, up_bias, down_weight, down_bias,
):
    devices = lax.axis_size("seq")
    depth = lax.axis_size("grp")
    seqs, length, width = tokens.shape
    count = seqs * length
    steps = count // SUBS
    dims = decay_alpha.shape[1]
    nv = value_weight.shape[1]
    nf = up_weight.shape[1]
    nm = mix_weight.shape[1]
    zw = query_offset.shape[0] * devices
    reach = max(1, devices // 4)
    held = width // devices

    vectors = [
        (72, value_bias), (73, up_bias), (80, mix_bias), (64, first_gain), (65, skip_omega),
        (66, second_gain), (67, down_bias), (74, latent_gains), (76, query_offset),
        (77, position_bias),
    ]
    plan = []
    for at, v in vectors:
        n = v.shape[-1]
        plan.append((at, v.ndim, n, spread(n, devices)))
    decs = [d.T for d in (decay_alpha, decay_delta, decay_beta, decay_eta)]
    placed = whole(
        partial(place_kernel, plan=plan), struct((ROWS_SMALL, TILE), F32),
        n_in=4 + len(vectors), name="place", vmem=60,
    )(*decs, *[v for _, v in vectors])
    near = near_pieces(placed, devices)
    small = with_far(bundle(near))

    w1, w2 = whole(
        pack_kernel,
        [struct((held, nv + nm), BF), struct((nv // devices + held, 2 * width), BF)],
        n_in=5,
        name="pack",
        vmem=60,
    )(*lax.optimization_barrier(
        (value_weight, mix_weight, attend_weight, down_weight, up_weight, placed)
    )[:5])
    w1 = first_pieces(after(w1, near[1:]), devices)

    tok = tokens.reshape(count, width)
    cot = cotangent.reshape(count, width)
    blocks = width // TILE
    msg_rows = dims * seqs + 16
    pd, pv, pz, pm, dk, nrm, nlow, lab, fin, msg = whole(
        partial(head_kernel, devices=devices, dims=dims, nv=nv, nm=nm),
        [
            struct((72, width), F32), struct((8, nv), F32), struct((8, TILE), F32),
            struct((8, nm), F32), struct((3 * dims, width), F32), struct((blocks, count, TILE), F32),
            struct((count, width), BF), struct((count, TILE), F32),
            struct((dims * SUBS, width), F32), struct((msg_rows, width), BF),
        ],
        [pltpu.VMEM((dims * SUBS, TILE), F32), pltpu.VMEM((devices, ROWS_SMALL, TILE), F32)]
        + [padded(steps)] * 2,
        n_in=4,
        name="head",
        micros=6,
    )(*small, tok, segments)

    onward = [
        lax.ppermute(msg, "seq", [(i, i + k) for i in range(devices - k)])
        for k in range(1, reach + 1)
    ]

    halves = 1 if devices == 8 else 0
    w1 = more_pieces(w1, devices, msg)
    w1 = with_far(bundle(after(w1, onward), halves))
    w2 = first_pieces(after(w2, w1[0]), devices)
    nrm = after(nrm, w1[0])
    arrivals = [pltpu.VMEM((dims * SUBS, TILE), F32)] * reach
    z, mlow, sp = whole(
        partial(scan_kernel, reach=reach, dims=dims, seqs=seqs),
        [
            struct((count, width), F32), struct((count, width), BF),
            struct((blocks, steps, dims * SUBS, TILE), BF),
        ],
        [
            pltpu.VMEM((dims * SUBS, TILE), F32), pltpu.VMEM((SUBS, TILE), F32),
            pltpu.VMEM((blocks, count, TILE), F32),
        ] + [padded(steps)] * 3 + arrivals,
        n_in=5 + reach,
        name="scan",
        micros=8,
    )(nrm, lab, dk, pd, fin, *onward)

    w2 = more_pieces(w2, devices, z)

    def sems(n):
        return pltpu.SemaphoreType.DMA((n, devices))

    vlow, dval, upd, ext, lat, rs, ad, glow, probs, qlow, klow = whole(
        partial(front_kernel, devices=devices),
        [
            struct((count, nv), BF), struct((count, nv), BF), struct((count, width), F32),
            struct((count, width), F32), struct((count, zw), F32), struct((count, nv), BF),
            struct((count, nv), BF), struct((count, nv), BF), struct((count, length), F32),
            struct((count, zw), BF), struct((count, zw), BF),
        ],
        [pltpu.VMEM((width, nv + nm), BF), pltpu.VMEM((count, nv), F32), sems(1)],
        in_specs=[HB] * 2 + [VM] * 7,
        name="front",
        micros=11,
    )(*w1, nlow, mlow, pv, pm, pz, lab, segments)

    w2 = with_far(bundle(after(w2, glow), halves))
    half = devices // 2
    rows2, rows1 = nv // devices // depth, held // depth
    piece_a = struct((half, depth, rows2 + rows1, 2 * width), BF)
    out, gin, attg, blu, blre, v512, v1024, own_a, sib_a = whole(
        partial(middle_kernel, devices=devices, depth=depth, dims=dims),
        [
            struct((count, width), F32), struct((count, width), F32), struct((count, nv), BF),
            struct((count, width), BF), struct((count, nv + width), BF), struct((8, width), F32),
            struct((8, nv), F32), piece_a, piece_a,
        ],
        [
            pltpu.VMEM((nv, 2 * width), BF), pltpu.VMEM((width, nf), BF),
            pltpu.VMEM((count, width), F32), pltpu.VMEM((count, width), F32),
            pltpu.VMEM((count, width), BF), pltpu.VMEM((count, nf), F32),
            pltpu.VMEM((count, nf), BF), pltpu.VMEM((count, width), BF),
            pltpu.VMEM((count, nf), BF), pltpu.VMEM((count, width), BF),
            pltpu.VMEM((count, width), F32), pltpu.VMEM((nv, 2 * width), BF), sems(2),
        ],
        in_specs=[HB] * 2 + [VM] * 9,
        name="middle",
        micros=19,
    )(*w2, tok, cot, upd, ext, rs, ad, glow, pd, pv)

    vgl, bll, gs, gnp, w512, w1024, w128, back_msg, ach = whole(
        partial(back_kernel, devices=devices, dims=dims),
        [
            struct((count, nv), BF), struct((count, zw), BF), struct((blocks, count, TILE), F32),
            struct((blocks, count, TILE), F32), struct((8, width), F32), struct((8, nv), F32),
            struct((8, TILE), F32), struct((msg_rows, width), BF),
            struct((dims * SUBS, width), F32),
        ],
        [
            pltpu.VMEM((width, nv + nm), BF), pltpu.VMEM((count, zw), F32),
            pltpu.VMEM((count, zw), F32), pltpu.VMEM((dims * SUBS, TILE), F32), sems(1),
            padded(steps), padded(steps),
        ],
        in_specs=[HB] * 2 + [VM] * 15,
        name="back",
        micros=15,
    )(*w1, probs, attg, vlow, dval, qlow, klow, lat, blu, blre, z, nrm, pd, pz, dk, lab)

    backward = [
        lax.ppermute(back_msg, "seq", [(i + k, i) for i in range(devices - k)])
        for k in range(1, reach + 1)
    ]

    piece_b = struct((half, depth, rows1, nv + nm), BF)
    own_b, sib_b = whole(
        partial(weight_kernel, devices=devices, depth=depth),
        [piece_b, piece_b],
        [pltpu.VMEM((width, nv + nm), BF)],
        n_in=6,
        name="weights",
        micros=6,
    )(nlow, mlow, vgl, blu, bll, blre)

    _, _, finish_a = spread_sums(after(own_a, backward), sib_a, devices, None)
    tie_b, _, finish_b = spread_sums(own_b, sib_b, devices, None)
    nrm = after(nrm, tie_b)
    piece_c = struct((half, ROWS_SMALL, TILE), F32)
    wide = ceil_div(nm, TILE) + 2
    tokens_grad, own_c, sib_c = whole(
        partial(last_kernel, reach=reach, devices=devices, dims=dims, seqs=seqs, nm=nm),
        [struct((count, width), F32), piece_c, piece_c],
        [
            pltpu.VMEM((dims * SUBS, TILE), F32), pltpu.VMEM((SUBS, TILE), F32),
            pltpu.VMEM((blocks, count, TILE), F32), pltpu.VMEM((72, width), F32),
            pltpu.VMEM((8, nv), F32), pltpu.VMEM((8, wide * TILE), F32),
            pltpu.VMEM((2 * dims, width), F32),
        ] + [padded(steps)] * 4 + arrivals,
        n_in=15 + reach,
        name="last",
        micros=12,
    )(sp, nrm, gs, gnp, lab, dk, ach, *backward, tok, gin, pd, v512, v1024, w512, w1024, w128)

    sum_a = deal(finish_a(own_c), depth, devices)
    sum_b = deal(finish_b(own_c), depth, devices)
    parts_c = across(fold(own_c, sib_c, F32))
    everything = join(sum_a, sum_b, parts_c)
    grads = whole(
        partial(final_kernel, depth=depth, plan=plan, held=held, dims=dims),
        [
            struct((nv // devices, width), F32), struct((nf // devices, width), F32),
            struct((held, nf), F32), struct((held, nv), F32), struct((held, nm), F32),
        ] + [struct((dims, held), F32)] * 4 + [struct(v.shape, F32) for _, v in vectors],
        [
            pltpu.VMEM((depth,) + everything[0].shape, F32),
            pltpu.VMEM((ceil_div(ROWS_SMALL, rows1) * rows1, TILE), F32),
        ],
        n_in=depth,
        name="final",
    )(*everything)
    attend_grad, down_grad, up_grad, value_grad, mix_grad = grads[:5]
    alpha_g, delta_g, beta_g, eta_g = grads[5:9]
    value_b, up_b, mix_b, first_g, omega, second_g, down_b, gains_g, qoff, posb = grads[9:]
    return (
        out.reshape(tokens.shape),
        tokens_grad.reshape(tokens.shape),
        first_g,
        value_grad,
        value_b,
        alpha_g.T,
        delta_g.T,
        beta_g.T,
        eta_g.T,
        omega,
        mix_grad,
        mix_b,
        gains_g,
        qoff,
        posb,
        attend_grad,
        second_g,
        up_grad,
        up_b,
        down_grad,
        down_b,
    )


def solution(mesh):
    vec, mat = P("seq"), P("seq", None)
    data = P("grp", "seq", None)
    params = (
        vec, mat, vec, mat, mat, mat, mat, vec, mat, vec, P(None, "seq"), vec, vec, mat, vec, mat,
        vec, mat, vec,
    )
    return jax.shard_map(
        per_device,
        mesh=mesh,
        in_specs=(data, P("grp", "seq"), data) + params,
        out_specs=(data, data) + params,
        check_vma=False,
    )
```

```python
from functools import partial

import jax
import jax.numpy as jnp
from jax import lax
from jax.experimental import pallas as pl
from jax.experimental.pallas import tpu as pltpu
from jax.sharding import PartitionSpec as P

EPSILON = 1e-06
F32 = jnp.float32
BF = jnp.bfloat16
TILE = 128
SUBS = 8
ROWS_SMALL = 88
NN = (((1,), (0,)), ((), ()))
NT = (((1,), (1,)), ((), ()))
TN = (((0,), (0,)), ((), ()))


def dot(a, b, dims=NN):
    return lax.dot_general(a, b, dims, preferred_element_type=F32)


def sig(v):
    return 0.5 * jnp.tanh(0.5 * v) + 0.5


def struct(shape, dtype):
    return jax.ShapeDtypeStruct(shape, dtype)


VM = pl.BlockSpec(memory_space=pltpu.VMEM)
HB = pl.BlockSpec(memory_space=pl.ANY)


def cost(micros):
    return pl.CostEstimate(flops=0, transcendentals=0, bytes_accessed=int(micros * 3.69e6))


def whole(body, outs, scratch=(), in_specs=None, n_in=None, name=None, micros=2, vmem=26):
    return pl.pallas_call(
        body,
        out_shape=outs,
        in_specs=in_specs if in_specs is not None else [VM] * n_in,
        out_specs=jax.tree.map(lambda _: VM, outs),
        scratch_shapes=list(scratch),
        compiler_params=pltpu.CompilerParams(vmem_limit_bytes=vmem << 20),
        cost_estimate=cost(micros),
        name=name,
    )


def tiles(m_size, n_size, tm, tn, fn):
    for n in range(0, n_size, tn):
        for m in range(0, m_size, tm):
            fn(m, n)


def rows_loop(total, step, fn):
    def body(i, _):
        fn(pl.multiple_of(i * step, step))
        return 0

    lax.fori_loop(0, total // step, body, 0)


def ceil_div(a, b):
    return -(-a // b)


def spread(n, devices):
    return max(ceil_div((d * n) % TILE + n, TILE) for d in range(devices))


def place_kernel(*refs, plan):
    me = lax.axis_index("seq")
    decs, vectors, out_ref = refs[:4], refs[4:-1], refs[-1]
    out_ref[...] = jnp.zeros_like(out_ref)
    dims, held = decs[0].shape
    pick = pick_lanes(me, held, TILE)
    for j, dec in enumerate(decs):
        out_ref[j * dims : (j + 1) * dims, :] = dot(dec[...], pick.astype(BF))
    source = 0
    for at, count, n, nt in plan:
        values = vectors[source][...].astype(F32)
        source += 1
        if count == 1:
            values = values.reshape(1, n)
        values = jnp.broadcast_to(values, (SUBS, n)) if count == 1 else values
        moved = dot(values.astype(BF), pick_lanes(me, n, nt * TILE).astype(BF))
        for i in range(count):
            for j in range(nt):
                out_ref[at + i + j : at + i + j + 1, :] = moved[i : i + 1, j * TILE : (j + 1) * TILE]


def pick_lanes(me, n, lanes):
    row = lax.broadcasted_iota(jnp.int32, (n, lanes), 0)
    lane = lax.broadcasted_iota(jnp.int32, (n, lanes), 1)
    return jnp.where(lane == row + (me * n) % TILE, 1.0, 0.0)


def pack_kernel(value, mix, attend, down, up, w1, w2):
    nv = value.shape[1]
    w1[:, 0:nv] = value[...]
    w1[:, nv:] = mix[...]
    rows, width = attend.shape
    w2[0:rows, 0:width] = attend[...]
    w2[0:rows, width:] = down[...]
    w2[rows:, :] = up[...]


def assemble(src, low, high, n, total, devices):
    parts = [None] * ceil_div(total, TILE)
    for d in range(devices):
        t = d * n // TILE
        block = src[d, low:high, :]
        parts[t] = block if parts[t] is None else parts[t] + block
    return parts


def chunk_labels(lab_ref, steps):
    return lab_ref[pl.ds(0, SUBS, stride=steps), :], lab_ref[pl.ds(steps - 1, SUBS, stride=steps), :]


def lanes_of(t):
    return slice(t * TILE, (t + 1) * TILE)


def padded(steps):
    return pltpu.VMEM((SUBS * (steps + 1), TILE), F32)


def stage(src, dst, steps):
    for c in range(SUBS):
        dst[c * (steps + 1) : c * (steps + 1) + steps, :] = src[pl.ds(c * steps, steps), :]


def unstage(src, dst, steps):
    for c in range(SUBS):
        dst[pl.ds(c * steps, steps), :] = src[c * (steps + 1) : c * (steps + 1) + steps, :]


def rows_at(t, steps):
    return pl.ds(t, SUBS, stride=steps + 1)


def one_way(
    src_ref, lab_ref, ref_label, dk_ref, out_ref, pads, dims, steps, width, reverse, unroll=8
):
    src_pad, lab_pad = pads
    stage(lab_ref, lab_pad, steps)
    for lt in range(width // TILE):
        lanes = lanes_of(lt)
        decay = [jnp.broadcast_to(dk_ref[h : h + 1, lanes], (SUBS, TILE)) for h in range(dims)]

        stage(src_ref.at[lt], src_pad, steps)

        def step(i, state, decay=decay):
            state = list(state)
            for u in range(unroll):
                t = i * unroll + u
                if reverse:
                    t = steps - 1 - t
                x = src_pad[rows_at(t, steps), :]
                l = lab_pad[rows_at(t, steps), :]
                x = jnp.where(l == ref_label, x, 0.0)
                state = [decay[h] * state[h] + x for h in range(dims)]
            return tuple(state)

        zero = jnp.zeros((SUBS, TILE), F32)
        final = lax.fori_loop(0, steps // unroll, step, (zero,) * dims)
        for h in range(dims):
            out_ref[h * SUBS : (h + 1) * SUBS, lanes] = final[h]


def norm_scale(x):
    return lax.rsqrt(jnp.mean(x * x, axis=-1, keepdims=True) + EPSILON)


def head_kernel(*refs, devices, dims, nv, nm):
    (
        tok_ref, seg_ref, pd_ref, pv_ref, pz_ref, pm_ref, dk_ref, nrm_ref, low_ref, lab_ref,
        fin_ref, msg_ref, scr_ref, small_ref, *pads
    ) = refs[2:]
    me = lax.axis_index("seq")
    for k in range(devices):
        small_ref[me ^ k] = refs[k % 2][k // 2]
    tokens, width = tok_ref.shape
    seqs, length = seg_ref.shape
    steps = tokens // SUBS
    for t, part in enumerate(assemble(small_ref, 0, 72, width // devices, width, devices)):
        pd_ref[:, lanes_of(t)] = part
    for t, part in enumerate(assemble(small_ref, 72, 80, nv // devices, nv, devices)):
        pv_ref[:, lanes_of(t)] = part
    z = small_ref[0, 72:80, :]
    for d in range(1, devices):
        z = z + small_ref[d, 72:80, :]
    pz_ref[...] = z
    n = nm // devices
    cells = [None] * (nm // TILE)
    for d in range(devices):
        first, lane = divmod(d * n, TILE)
        for j in range(ceil_div(lane + n, TILE)):
            piece = small_ref[d, 80 + j : 81 + j, :]
            cells[first + j] = piece if cells[first + j] is None else cells[first + j] + piece
    for t, piece in enumerate(cells):
        pm_ref[:, lanes_of(t)] = jnp.broadcast_to(piece, (SUBS, TILE))

    rate = 1.0 / (1.0 + jnp.exp(-pd_ref[0:dims, :]))
    damping = 1.0 / (1.0 + jnp.exp(-pd_ref[dims : 2 * dims, :]))
    decay = 1.0 - rate * damping
    dk_ref[0:dims, :] = decay
    dk_ref[dims : 2 * dims, :] = pd_ref[3 * dims : 4 * dims, :] * rate * pd_ref[2 * dims : 3 * dims, :]
    power, k = decay, 1
    while k < steps:
        power, k = power * power, k * 2
    dk_ref[2 * dims : 3 * dims, :] = power

    gain = pd_ref[4 * dims : 4 * dims + 1, :]

    def norm(r):
        x = tok_ref[pl.ds(r, 64), :].astype(F32)
        y = x * norm_scale(x) * gain
        for t in range(width // TILE):
            nrm_ref[t, pl.ds(r, 64), :] = y[:, lanes_of(t)]
        low_ref[pl.ds(r, 64), :] = y.astype(BF)

    rows_loop(tokens, 64, norm)

    labels = seg_ref[...].astype(F32)
    row = lax.broadcasted_iota(jnp.int32, (length, length), 0)
    col = lax.broadcasted_iota(jnp.int32, (length, length), 1)
    for s in range(seqs):
        diagonal = jnp.where(row == col, labels[s : s + 1, :], 0.0).astype(BF)
        lab_ref[s * length : (s + 1) * length, :] = dot(diagonal, jnp.ones((length, TILE), BF))

    first, last = chunk_labels(lab_ref, steps)
    one_way(nrm_ref, lab_ref, last, dk_ref, fin_ref, pads, dims, steps, width, False)
    through = (first == last) & (first == pltpu.roll(last, 1, 0))
    for lt in range(width // TILE):
        lanes = lanes_of(lt)
        for h in range(dims):
            own = fin_ref[h * SUBS : (h + 1) * SUBS, lanes]
            before = pltpu.roll(own, 1, 0) * power[h : h + 1, lanes]
            scr_ref[h * SUBS : (h + 1) * SUBS, :] = own + jnp.where(through, before, 0.0)
        half = SUBS // seqs
        msg_ref[0 : dims * seqs, lanes] = scr_ref[
            pl.ds(half - 1, dims * seqs, stride=half), :
        ].astype(BF)
        ends = lab_ref[pl.ds(length - 1, seqs, stride=length), :]
        tail = jnp.concatenate([ends, jnp.zeros((16 - seqs, TILE), F32)], axis=0)
        msg_ref[dims * seqs : dims * seqs + 16, lanes] = tail.astype(BF)


def entering(msgs, lanes, own_label, even, scr_refs, lab_scr, start, dims, seqs, power):
    half = SUBS // seqs
    gates = []
    for m, scr in zip(msgs, scr_refs):
        scr[pl.ds(start, dims * seqs, stride=half), :] = m[0 : dims * seqs, lanes].astype(F32)
        tail = m[dims * seqs : dims * seqs + 16, lanes].astype(F32)
        lab_scr[pl.ds(start, seqs, stride=half), :] = tail[0:seqs, :]
        gates.append(even & (lab_scr[...] == own_label))
    result = []
    for h in range(dims):
        total, reach = None, None
        for gate, scr in zip(gates, scr_refs):
            part = jnp.where(gate, scr[h * SUBS : (h + 1) * SUBS, :], 0.0)
            if total is None:
                total, reach = part, power[h : h + 1, :] * power[h : h + 1, :]
                far = reach
            else:
                total, far = total + part * far, far * reach
        result.append(total)
    return result


def scan_kernel(*refs, reach, dims, seqs):
    nrm_ref, lab_ref, dk_ref, pd_ref, fin_ref = refs[:5]
    msgs = refs[5 : 5 + reach]
    z_ref, mlow_ref, sp_ref = refs[5 + reach : 8 + reach]
    ent_ref, lab_scr, ys_ref, x_pad, lab_pad, y_pad = refs[8 + reach : 14 + reach]
    scr_refs = refs[14 + reach :]
    blocks, tokens, _ = nrm_ref.shape
    steps = tokens // SUBS
    half = SUBS // seqs
    first, last = chunk_labels(lab_ref, steps)
    place = lax.broadcasted_iota(jnp.int32, (SUBS, TILE), 0)
    even = place % half == 0
    inside = first == last
    joined = first == pltpu.roll(last, 1, 0)
    unroll = 4
    stage(lab_ref, lab_pad, steps)

    def block(lt, _):
        stage(nrm_ref.at[lt], x_pad, steps)
        lanes = pl.ds(pl.multiple_of(lt * TILE, TILE), TILE)
        power = dk_ref[2 * dims : 3 * dims, lanes]
        arrivals = entering(msgs, lanes, first, even, scr_refs, lab_scr, 0, dims, seqs, power)
        for h in range(dims):
            e = arrivals[h]
            own = fin_ref[h * SUBS : (h + 1) * SUBS, lanes]
            onward = pltpu.roll(own + jnp.where(inside, e * power[h : h + 1, :], 0.0), 1, 0)
            ent_ref[h * SUBS : (h + 1) * SUBS, :] = jnp.where(
                even, e, jnp.where(joined, onward, 0.0)
            )
        decay = [jnp.broadcast_to(dk_ref[h : h + 1, lanes], (SUBS, TILE)) for h in range(dims)]
        weight = [
            jnp.broadcast_to(dk_ref[dims + h : dims + h + 1, lanes], (SUBS, TILE))
            for h in range(dims)
        ]

        def step(i, carry):
            before, state = carry[0], list(carry[1:])
            for u in range(unroll):
                t = i * unroll + u
                x = x_pad[rows_at(t, steps), :]
                l = lab_pad[rows_at(t, steps), :]
                same = l == before
                before = l
                sums = [None] * 4
                for h in range(dims):
                    kept = jnp.where(same, state[h], 0.0)
                    if h % 2 == 0:
                        held = kept
                    else:
                        pair = jnp.concatenate([held, kept], axis=0)
                        sp_ref[lt, t, (h - 1) * SUBS : (h + 1) * SUBS, :] = pair.astype(BF)
                    state[h] = decay[h] * kept + x
                    term = weight[h] * state[h]
                    sums[h % 4] = term if sums[h % 4] is None else sums[h % 4] + term
                y_pad[rows_at(t, steps), :] = (sums[0] + sums[1]) + (
                    sums[2] + sums[3]
                )
            return (before,) + tuple(state)

        start = tuple(ent_ref[h * SUBS : (h + 1) * SUBS, :] for h in range(dims))
        lax.fori_loop(0, steps // unroll, step, (first,) + start)
        unstage(y_pad, ys_ref.at[lt], steps)
        return 0

    lax.fori_loop(0, blocks, block, 0)
    omega = pd_ref[4 * dims + 1 : 4 * dims + 2, :]

    def gate(r):
        for t in range(blocks):
            v = ys_ref[t, pl.ds(r, 128), :] + omega[:, lanes_of(t)] * nrm_ref[t, pl.ds(r, 128), :]
            z_ref[pl.ds(r, 128), lanes_of(t)] = v
            mlow_ref[pl.ds(r, 128), lanes_of(t)] = (v * sig(v)).astype(BF)

    rows_loop(tokens, 128, gate)


def load_weights(pieces, dst, sem, rows, start, cols, place):
    me = lax.axis_index("seq")
    copies = []
    for k in range(2 * pieces[0].shape[0]):
        p = me ^ k
        piece = pieces[k % 2].at[k // 2]
        copies.append(
            pltpu.make_async_copy(
                piece.at[pl.ds(start, rows), pl.ds(0, cols)],
                dst.at[pl.ds(pl.multiple_of(p * rows, rows), rows), pl.ds(0, cols)],
                sem.at[place, k],
            )
        )
    for c in copies:
        c.start()
    return copies


def split_sizes(width, latent, nv):
    return {"u": 0, "l": width, "r": width + latent, "e": width + latent + nv}


def front_kernel(*refs, devices):
    n = 2
    pieces = refs[:n]
    nlow, mlow, pv, pm, pz, lab, seg = refs[n : n + 7]
    vlow, dval, upd, ext, lat, rs, ad, glow, probs, qlow, klow = refs[n + 7 : n + 18]
    w, res, sem = refs[n + 18 :]
    tokens, width = nlow.shape
    nv = vlow.shape[1]
    zw = lat.shape[1]
    seqs, length = seg.shape
    rows = width // devices
    copies = load_weights(pieces, w, sem, rows, 0, w.shape[1], 0)
    for c in copies:
        c.wait()

    def value(m, n):
        v = dot(nlow[pl.ds(m, 512), :], w[:, pl.ds(n, 512)]) + pv[0:1, pl.ds(n, 512)]
        s = sig(v)
        vlow[pl.ds(m, 512), pl.ds(n, 512)] = (v * s).astype(BF)
        dval[pl.ds(m, 512), pl.ds(n, 512)] = (s * (1.0 + v * (1.0 - s))).astype(BF)

    tiles(tokens, nv, 512, 512, value)
    at = split_sizes(width, zw, nv)

    def base(m, n, start, size):
        cols = start + n
        wcols = nv + start + n
        return dot(mlow[pl.ds(m, 512), :], w[:, pl.ds(wcols, size)]) + pm[0:1, pl.ds(cols, size)]

    def update(m, n):
        upd[pl.ds(m, 512), pl.ds(n, 512)] = sig(base(m, n, at["u"], 512))

    tiles(tokens, width, 512, 512, update)

    def extra(m, n):
        ext[pl.ds(m, 512), pl.ds(n, 512)] = base(m, n, at["e"], 512)

    tiles(tokens, width, 512, 512, extra)

    def reset(m, n):
        res[pl.ds(m, 512), pl.ds(n, 512)] = base(m, n, at["r"], 512)

    tiles(tokens, nv, 512, 512, reset)

    def latent(m, n):
        v = base(m, n, at["l"], zw)
        lat[pl.ds(m, 512), :] = v
        y = v * sig(v)
        qlow[pl.ds(m, 512), :] = ((y * pz[2:3, :] + pz[4:5, :]) * zw ** (-0.5)).astype(BF)
        klow[pl.ds(m, 512), :] = (y * pz[3:4, :]).astype(BF)

    tiles(tokens, zw, 512, zw, latent)

    row = lax.broadcasted_iota(jnp.int32, (length, length), 0)
    col = lax.broadcasted_iota(jnp.int32, (length, length), 1)
    flip = jnp.where((row + col) % length == 0, 1.0, 0.0).astype(BF)
    bias = dot(pz[...].astype(BF), flip)[5:6, :]
    table = pltpu.roll(jnp.broadcast_to(bias, (length, length)), 0, 1, stride=1, stride_axis=0)
    causal = row >= col

    def attend(r):
        here = pl.ds(r, length)
        label_j = seg[pl.ds(r // length, 1), :].astype(F32)
        allowed = causal & (lab[here, :] == label_j)
        scores = dot(qlow[here, :], klow[here, :], NT) + table
        scores = jnp.where(allowed, scores, -1e30)
        weights = jnp.exp(scores - jnp.max(scores, axis=-1, keepdims=True))
        prob = weights / jnp.sum(weights, axis=-1, keepdims=True)
        probs[here, :] = prob
        plow = prob.astype(BF)
        for n in range(nv // 256):
            cols = slice(n * 256, (n + 1) * 256)
            a = dot(plow, vlow[here, cols])
            v = res[here, cols]
            s = sig(v)
            y = v * s
            rs[here, cols] = y.astype(BF)
            ad[here, cols] = (a * (s * (1.0 + v * (1.0 - s)))).astype(BF)
            glow[here, cols] = (a * y).astype(BF)

    rows_loop(tokens, length, attend)


def column_sum(ref, row, cols, values, first):
    total = jnp.sum(values, axis=0, keepdims=True)
    if isinstance(first, bool):
        ref[row : row + 1, cols] = total if first else ref[row : row + 1, cols] + total
        return

    @pl.when(first)
    def _():
        ref[row : row + 1, cols] = total

    @pl.when(jnp.logical_not(first))
    def _():
        ref[row : row + 1, cols] = ref[row : row + 1, cols] + total


def put_pieces(src, own, sib, devices, depth, rows, at, src_cols, cols):
    me = lax.axis_index("seq")
    for p in range(devices):
        k = me ^ p
        kc = k // 2

        def put(dst, p=p, kc=kc):
            for z in range(depth):
                begin = (p * depth + z) * rows
                dst[kc, z, at : at + rows, cols] = src[begin : begin + rows, src_cols].astype(BF)

        pl.when(k % 2 == 0)(partial(put, own))
        pl.when(k % 2 == 1)(partial(put, sib))


def middle_kernel(*refs, devices, depth, dims):
    n = 2
    pieces = refs[:n]
    tok, cot, upd, ext, rs, ad, glow, pd, pv = refs[n : n + 9]
    out, gin, attg, blu, blre, v512, v1024, own, sib = refs[n + 9 : n + 18]
    w2, wup, proj, mid, slow, dup, hlow, clow, ulow, elow, gmid, grad, sem = refs[n + 18 :]
    tokens, width = tok.shape
    nv = rs.shape[1]
    nf = dup.shape[1]
    rows2, rows1 = nv // devices, width // devices
    copies = load_weights(pieces, w2, sem, rows2, 0, 2 * width, 0)
    copies += load_weights(pieces, wup, sem, rows1, rows2, nf, 1)
    for c in copies:
        c.wait()
    down = pl.ds(width, width)

    def project(m, n):
        proj[pl.ds(m, 512), pl.ds(n, 512)] = dot(glow[pl.ds(m, 512), :], w2[:, pl.ds(n, 512)])

    tiles(tokens, width, 512, 512, project)
    gain = pd[4 * dims + 2 : 4 * dims + 3, :]

    def blend(r):
        here = pl.ds(r, 64)
        x = tok[here, :].astype(F32)
        pre = ext[here, :] + proj[here, :]
        s = sig(pre)
        m = x + upd[here, :] * (pre * s - x)
        mid[here, :] = m
        slow[here, :] = (m * norm_scale(m) * gain).astype(BF)

    rows_loop(tokens, 64, blend)

    def up(m, n):
        v = dot(slow[pl.ds(m, 512), :], wup[:, pl.ds(n, 512)]) + pv[1:2, pl.ds(n, 512)]
        s = sig(v)
        hlow[pl.ds(m, 512), pl.ds(n, 512)] = (v * s).astype(BF)
        dup[pl.ds(m, 512), pl.ds(n, 512)] = s * (1.0 + v * (1.0 - s))

    tiles(tokens, nf, 512, 512, up)

    def down_forward(m, n):
        at, cols = pl.ds(m, 512), pl.ds(n, 512)
        y = dot(hlow[at, :], w2[:, pl.ds(width + n, 512)])
        out[at, cols] = mid[at, cols] + y + pd[4 * dims + 3 : 4 * dims + 4, cols]
        c = cot[at, cols]
        clow[at, cols] = c.astype(BF)
        column_sum(v512, 0, cols, c, m == 0)

    tiles(tokens, width, 512, 512, down_forward)

    def up_back(m, n):
        at, cols = pl.ds(m, 512), pl.ds(n, 512)
        g = dot(clow[at, :], w2[cols, down], NT) * dup[at, cols]
        ulow[at, cols] = g.astype(BF)
        column_sum(v1024, 0, cols, g, m == 0)

    tiles(tokens, nf, 512, 512, up_back)

    def down_grad(m, n):
        grad[pl.ds(m, 512), pl.ds(width + n, 512)] = dot(
            hlow[:, pl.ds(m, 512)], clow[:, pl.ds(n, 512)], TN
        ).astype(BF)

    tiles(nf, width, 512, 512, down_grad)

    def second_back(m, n):
        gmid[pl.ds(m, 512), pl.ds(n, 512)] = dot(ulow[pl.ds(m, 512), :], wup[pl.ds(n, 512), :], NT)

    tiles(tokens, width, 512, 512, second_back)
    everything = slice(0, width)

    def middle_back(r):
        here = pl.ds(r, 64)
        start = r == 0
        m = mid[here, :]
        g = gmid[here, :]
        scale = norm_scale(m)
        n = m * scale
        column_sum(v512, 1, everything, g * n, start)
        g = g * gain
        gm = cot[here, :] + scale * (g - n * jnp.mean(g * n, axis=-1, keepdims=True))
        x = tok[here, :].astype(F32)
        pre = ext[here, :] + proj[here, :]
        s = sig(pre)
        u = upd[here, :]
        ge = gm * u * (s * (1.0 + pre * (1.0 - s)))
        gu = gm * (pre * s - x) * (u * (1.0 - u))
        gin[here, :] = gm * (1.0 - u)
        low = ge.astype(BF)
        elow[here, :] = low
        blre[here, pl.ds(nv, width)] = low
        blu[here, :] = gu.astype(BF)
        column_sum(v512, 2, everything, gu, start)
        column_sum(v512, 3, everything, ge, start)

    rows_loop(tokens, 64, middle_back)

    def gated_back(m, n):
        at, cols = pl.ds(m, 512), pl.ds(n, 512)
        g = dot(elow[at, :], w2[cols, pl.ds(0, width)], NT)
        gr = g * ad[at, cols].astype(F32)
        blre[at, cols] = gr.astype(BF)
        attg[at, cols] = (g * rs[at, cols].astype(F32)).astype(BF)
        column_sum(v1024, 1, cols, gr, m == 0)

    tiles(tokens, nv, 512, 512, gated_back)

    def attend_grad(m, n):
        grad[pl.ds(m, 512), pl.ds(n, 512)] = dot(
            glow[:, pl.ds(m, 512)], elow[:, pl.ds(n, 512)], TN
        ).astype(BF)

    tiles(nv, width, 512, 512, attend_grad)
    r2, r1 = rows2 // depth, rows1 // depth
    put_pieces(grad, own, sib, devices, depth, r2, 0, slice(0, 2 * width), slice(0, 2 * width))

    def up_grad(m, n):
        grad[pl.ds(m, 512), pl.ds(n, 512)] = dot(
            slow[:, pl.ds(m, 512)], ulow[:, pl.ds(n, 512)], TN
        ).astype(BF)

    tiles(width, nf, 512, 512, up_grad)
    put_pieces(grad, own, sib, devices, depth, r1, r2, slice(0, nf), slice(0, nf))


def back_kernel(*refs, devices, dims):
    n = 2
    pieces = refs[:n]
    probs, attg, vlow, dval, qlow, klow, lat, blu, blre, z, nrm, pd, pz, dk, lab = refs[
        n : n + 15
    ]
    vgl, bll, gs, gnp, w512, w1024, w128, msg, ach = refs[n + 15 : n + 24]
    w, gq, gk, scr, sem, *pads = refs[n + 24 :]
    tokens, width = z.shape
    nv = vlow.shape[1]
    zw = lat.shape[1]
    seqs = tokens // probs.shape[1]
    length = probs.shape[1]
    steps = tokens // SUBS
    rows = width // devices
    copies = load_weights(pieces, w, sem, rows, 0, w.shape[1], 0)
    row = lax.broadcasted_iota(jnp.int32, (length, length), 0)
    col = lax.broadcasted_iota(jnp.int32, (length, length), 1)

    def attend(r, total):
        here = pl.ds(pl.multiple_of(r * length, length), length)
        p = probs[here, :]
        plow = p.astype(BF)
        gp = dot(attg[here, :], vlow[here, :], NT)
        gsc = p * (gp - jnp.sum(p * gp, axis=-1, keepdims=True))
        low = gsc.astype(BF)
        gq[here, :] = dot(low, klow[here, :])
        gk[here, :] = dot(low, qlow[here, :], TN)
        for n in range(nv // 256):
            cols = slice(n * 256, (n + 1) * 256)
            gv = dot(plow, attg[here, cols], TN) * dval[here, cols].astype(F32)
            vgl[here, cols] = gv.astype(BF)
            column_sum(w1024, 0, cols, gv, r == 0)
        return total + gsc

    total = lax.fori_loop(0, seqs, attend, jnp.zeros((length, length), F32))
    flip = jnp.where((row + col) % length == 0, 1.0, 0.0)
    turned = lax.dot_general(
        total, flip, NN, precision=lax.Precision.HIGHEST, preferred_element_type=F32
    )
    turned = pltpu.roll(turned, 0, 1, stride=1, stride_axis=0)
    w128[...] = jnp.zeros_like(w128)
    w128[5:6, :] = jnp.sum(turned, axis=0, keepdims=True)

    def latent_back(r):
        here = pl.ds(r, 128)
        v = lat[here, :]
        s = sig(v)
        y = v * s
        q = gq[here, :] * zw ** (-0.5)
        k = gk[here, :]
        g = (q * pz[2:3, :] + k * pz[3:4, :]) * (s * (1.0 + v * (1.0 - s)))
        bll[here, :] = g.astype(BF)
        start = r == 0
        every = slice(0, zw)
        column_sum(w128, 0, every, g, start)
        column_sum(w128, 2, every, q * y, start)
        column_sum(w128, 3, every, k * y, start)
        column_sum(w128, 4, every, q, start)

    rows_loop(tokens, 128, latent_back)
    for c in copies:
        c.wait()
    at = split_sizes(width, zw, nv)

    def mixed_back(m, n):
        here, cols = pl.ds(m, 512), pl.ds(n, 512)
        g = dot(blu[here, :], w[cols, nv : nv + width], NT)
        g = g + dot(bll[here, :], w[cols, nv + at["l"] : nv + at["r"]], NT)
        g = g + dot(blre[here, :], w[cols, nv + at["r"] :], NT)
        v = z[here, cols]
        s = sig(v)
        g = g * (s * (1.0 + v * (1.0 - s)))
        t = n // TILE
        for j in range(512 // TILE):
            gs[t + j, here, :] = g[:, lanes_of(j)]
        column_sum(w512, 0, cols, g * two(nrm, t, here), m == 0)

    tiles(tokens, width, 512, 512, mixed_back)
    first, last = chunk_labels(lab, steps)
    one_way(gs, lab, first, dk, ach, pads, dims, steps, width, True)
    power = dk[2 * dims : 3 * dims, :]
    through = (first == last) & (last == pltpu.roll(first, SUBS - 1, 0))
    for lt in range(width // TILE):
        lanes = lanes_of(lt)
        for h in range(dims):
            here = slice(h * SUBS, (h + 1) * SUBS)
            after = pltpu.roll(ach[here, lanes], SUBS - 1, 0) * power[h : h + 1, lanes]
            scr[here, :] = ach[here, lanes] + jnp.where(through, after, 0.0)
        half = SUBS // seqs
        msg[0 : dims * seqs, lanes] = scr[pl.ds(0, dims * seqs, stride=half), :].astype(BF)
        starts = lab[pl.ds(0, seqs, stride=length), :]
        tail = jnp.concatenate([starts, jnp.zeros((16 - seqs, TILE), F32)], axis=0)
        msg[dims * seqs : dims * seqs + 16, lanes] = tail.astype(BF)

    def normed_back(m, n):
        here, cols = pl.ds(m, 512), pl.ds(n, 512)
        omega = pd[4 * dims + 1 : 4 * dims + 2, cols]
        g = two(gs, n // TILE, here) * omega + dot(vgl[here, :], w[cols, 0:nv], NT)
        for j in range(512 // TILE):
            gnp[n // TILE + j, here, :] = g[:, lanes_of(j)]

    tiles(tokens, width, 512, 512, normed_back)


def two(ref, t, here):
    return jnp.concatenate([ref[t + j, here, :] for j in range(512 // TILE)], axis=1)


def weight_kernel(
    nlow, mlow, vgl, blu, bll, blre, own, sib, grad, *, devices, depth
):
    tokens, width = nlow.shape
    nv = vgl.shape[1]
    zw = bll.shape[1]
    at = split_sizes(width, zw, nv)

    def piece(lhs, rhs, start, cols):
        def fn(m, n):
            grad[pl.ds(m, 512), pl.ds(start + n, cols)] = dot(
                lhs[:, pl.ds(m, 512)], rhs[:, pl.ds(n, cols)], TN
            ).astype(BF)

        tiles(width, rhs.shape[1], 512, cols, fn)

    piece(nlow, vgl, 0, 512)
    piece(mlow, blu, nv, 512)
    piece(mlow, bll, nv + at["l"], zw)
    piece(mlow, blre, nv + at["r"], 512)
    full = slice(0, grad.shape[1])
    put_pieces(grad, own, sib, devices, depth, width // devices // depth, 0, full, full)


def last_kernel(*refs, reach, devices, dims, seqs, nm):
    sp, nrm, gs, gnp, lab, dk, ach = refs[:7]
    msgs = refs[7 : 7 + reach]
    tok, gin, pd, v512, v1024, w512, w1024, w128 = refs[7 + reach : 15 + reach]
    tg, own, sib = refs[15 + reach : 18 + reach]
    ent, lab_scr, gnb, sd, sv, sm, sums_ref = refs[18 + reach : 25 + reach]
    lab_pad, x_pad, g_pad, n_pad = refs[25 + reach : 29 + reach]
    scr_refs = refs[29 + reach :]
    blocks, tokens, _ = nrm.shape
    width = tok.shape[1]
    steps = tokens // SUBS
    half = SUBS // seqs
    first, last = chunk_labels(lab, steps)
    place = lax.broadcasted_iota(jnp.int32, (SUBS, TILE), 0)
    odd = place % half == half - 1
    inside = first == last
    joined = last == pltpu.roll(first, SUBS - 1, 0)
    unroll = 4
    group = 8
    zero = jnp.zeros((SUBS, TILE), F32)
    stage(lab, lab_pad, steps)

    def block(lt, _):
        stage(nrm.at[lt], x_pad, steps)
        stage(gs.at[lt], g_pad, steps)
        stage(gnp.at[lt], n_pad, steps)
        lanes = pl.ds(pl.multiple_of(lt * TILE, TILE), TILE)
        power = dk[2 * dims : 3 * dims, lanes]
        arrivals = entering(msgs, lanes, last, odd, scr_refs, lab_scr, half - 1, dims, seqs, power)
        for h in range(dims):
            e = arrivals[h]
            here = slice(h * SUBS, (h + 1) * SUBS)
            onward = pltpu.roll(
                ach[here, lanes] + jnp.where(inside, e * power[h : h + 1, :], 0.0), SUBS - 1, 0
            )
            ent[here, :] = jnp.where(odd, e, jnp.where(joined, onward, 0.0))
        for base in range(0, dims, group):
            span = range(base, base + group)
            decay = [jnp.broadcast_to(dk[h : h + 1, lanes], (SUBS, TILE)) for h in span]
            weight = [
                jnp.broadcast_to(dk[dims + h : dims + h + 1, lanes], (SUBS, TILE)) for h in span
            ]

            def step(i, carry, base=base, decay=decay, weight=weight):
                after = carry[0]
                a, g0, g1 = (list(carry[1 + j * group : 1 + (j + 1) * group]) for j in range(3))
                for u in range(unroll):
                    t = steps - 1 - (i * unroll + u)
                    here = rows_at(t, steps)
                    x = x_pad[here, :]
                    g = g_pad[here, :]
                    l = lab_pad[here, :]
                    same = l == after
                    after = l
                    sums = [n_pad[here, :], zero]
                    for j in range(group):
                        h = base + j
                        if j % 2 == 0:
                            pair = sp[lt, t, h * SUBS : (h + 2) * SUBS, :].astype(F32)
                        a[j] = decay[j] * jnp.where(same, a[j], 0.0) + g
                        g0[j] = g0[j] + a[j] * x
                        g1[j] = g1[j] + a[j] * pair[j % 2 * SUBS : (j % 2 + 1) * SUBS, :]
                        sums[j % 2] = sums[j % 2] + weight[j] * a[j]
                    n_pad[here, :] = sums[0] + sums[1]
                return (after,) + tuple(a) + tuple(g0) + tuple(g1)

            start = tuple(ent[h * SUBS : (h + 1) * SUBS, :] for h in span)
            done = lax.fori_loop(0, steps // unroll, step, (last,) + start + (zero,) * (2 * group))
            for j in range(group):
                h = base + j
                sums_ref[h : h + 1, lanes] = jnp.sum(done[1 + group + j], axis=0, keepdims=True)
                sums_ref[dims + h : dims + h + 1, lanes] = jnp.sum(
                    done[1 + 2 * group + j], axis=0, keepdims=True
                )
        unstage(n_pad, gnb.at[lt], steps)
        return 0

    lax.fori_loop(0, blocks, block, 0)
    rate = 1.0 / (1.0 + jnp.exp(-pd[0:dims, :]))
    damping = 1.0 / (1.0 + jnp.exp(-pd[dims : 2 * dims, :]))
    beta, eta = pd[2 * dims : 3 * dims, :], pd[3 * dims : 4 * dims, :]
    g0 = sums_ref[0:dims, :]
    grad_decay = sums_ref[dims : 2 * dims, :] * eta * rate * beta
    grad_rate = g0 * eta * beta - damping * grad_decay
    sd[0:dims, :] = grad_rate * rate * (1.0 - rate)
    sd[dims : 2 * dims, :] = -grad_decay * rate * damping * (1.0 - damping)
    sd[2 * dims : 3 * dims, :] = g0 * rate * eta
    sd[3 * dims : 4 * dims, :] = g0 * rate * beta
    top = 4 * dims
    gain = pd[top : top + 1, :]
    sd[top : top + 8, :] = jnp.zeros((8, width), F32)

    def norm(r):
        here = pl.ds(r, 64)
        x = tok[here, :].astype(F32)
        q = norm_scale(x)
        m = x * q
        gn = jnp.concatenate([gnb[t, here, :] for t in range(blocks)], axis=1)
        sd[top : top + 1, :] += jnp.sum(gn * m, axis=0, keepdims=True)
        gn = gn * gain
        tg[here, :] = gin[here, :] + q * (gn - m * jnp.mean(gn * m, axis=-1, keepdims=True))

    rows_loop(tokens, 64, norm)
    sd[top + 1 : top + 2, :] = w512[0:1, :]
    sd[top + 2 : top + 3, :] = v512[1:2, :]
    sd[top + 3 : top + 4, :] = v512[0:1, :]
    nv = v1024.shape[1]
    zw = w128.shape[1]
    sv[...] = jnp.zeros_like(sv)
    sv[0:1, :] = w1024[0:1, :]
    sv[1:2, :] = v1024[0:1, :]
    at = split_sizes(width, zw, nv)
    sm[...] = jnp.zeros_like(sm)
    sm[0:1, 0:width] = v512[2:3, :]
    sm[0:1, at["l"] : at["r"]] = w128[0:1, :]
    sm[0:1, at["r"] : at["e"]] = v1024[1:2, :]
    sm[0:1, at["e"] : nm] = v512[3:4, :]
    me = lax.axis_index("seq")
    zrow = lax.broadcasted_iota(jnp.int32, (8, TILE), 0)
    zpart = jnp.where(zrow >= 2, w128[...], 0.0)
    for p in range(devices):
        k = me ^ p
        kc = k // 2

        def put(dst, p=p, kc=kc):
            dst[kc, 0:72, :] = sd[:, lanes_of(p * (width // devices) // TILE)]
            dst[kc, 72:80, :] = sv[:, lanes_of(p * (nv // devices) // TILE)] + zpart
            begin = p * (nm // devices) // TILE
            dst[kc, 80:88, :] = jnp.zeros((8, TILE), F32)
            for j in range(spread(nm // devices, devices)):
                dst[kc, 80 + j : 81 + j, :] = sm[0:1, lanes_of(begin + j)]

        pl.when(k % 2 == 0)(partial(put, own))
        pl.when(k % 2 == 1)(partial(put, sib))


def hop(x, axis, k):
    length = lax.axis_size(axis)
    return lax.ppermute(x, axis, [(i, i ^ k) for i in range(length)])


def fold_kernel(own, got, *outs):
    for k, out in enumerate(outs):
        out[...] = (own[k].astype(F32) + got[k].astype(F32)).astype(out.dtype)


def fold(own, got, dtype):
    outs = [struct(own.shape[1:], F32)] + [struct(own.shape[1:], dtype)] * (own.shape[0] - 1)
    return whole(fold_kernel, outs, n_in=2, name="fold")(own, got)


def across(parts):
    return [parts[0]] + [hop(part, "seq", 2 * k) for k, part in enumerate(parts) if k]


def split_kernel(own, got, kept, to_x, to_y, later_x, later_y):
    h = own.shape[1] // 2
    top, low = slice(0, h), slice(h, None)

    def piece(k, part):
        return own[k, part].astype(F32) + got[k, part].astype(F32)

    kept[...] = own[0].astype(F32) + got[0].astype(F32)
    to_x[top] = piece(1, top).astype(BF)
    to_x[low] = piece(3, top).astype(BF)
    to_y[top] = piece(2, low).astype(BF)
    to_y[low] = piece(3, low).astype(BF)
    later_x[...] = piece(1, low)
    later_y[...] = piece(2, top)


def split(own, got):
    shape = own.shape[1:]
    half = (shape[0] // 2,) + shape[1:]
    return whole(
        split_kernel,
        [struct(shape, F32), struct(shape, BF), struct(shape, BF), struct(half, F32), struct(half, F32)],
        n_in=2,
        name="split",
    )(own, got)


def turn_kernel(from_x, from_y, later_x, later_y, to_x, to_y):
    h = later_x.shape[0]
    to_x[...] = (later_x[...] + from_y[h:].astype(F32)).astype(BF)
    to_y[...] = (later_y[...] + from_x[h:].astype(F32)).astype(BF)


def spread_sums(own, got, devices):
    if devices != 8:
        parts = across(fold(own, got, BF))
        return parts[:1], parts[:1], lambda *first: parts
    kept, to_x, to_y, later_x, later_y = split(own, got)
    from_x, from_y = hop(to_x, "seq", 2), hop(to_y, "seq", 4)

    def finish(*first):
        fx, fy = after((from_x, from_y), *first)
        half = struct(later_x.shape, BF)
        qx, qy = whole(turn_kernel, [half, half], n_in=4, name="turn")(fx, fy, later_x, later_y)
        return [kept, fx, fy, hop(qx, "seq", 2), hop(qy, "seq", 4)]

    return [kept], [from_x, from_y], finish


def deal_kernel(*refs, count, depth, halves):
    ins, outs, scr = refs[:count], refs[count:-1], refs[-1]
    me = lax.axis_index("grp")
    if halves:
        kept, from_x, from_y, last_x, last_y = ins
        h = depth // 2
        scr[0:h] = kept[0:h] + from_x[0:h].astype(F32) + last_y[...].astype(F32)
        scr[h:] = kept[h:] + from_y[0:h].astype(F32) + last_x[...].astype(F32)
    else:
        total = ins[0][...]
        for other in ins[1:]:
            total = total + other[...].astype(F32)
        scr[...] = total
    for k in range(depth):
        outs[k][...] = scr[me ^ k].astype(outs[k].dtype)


def deal(parts, depth, devices):
    shape = parts[0].shape
    outs = [struct(shape[1:], F32)] + [struct(shape[1:], BF)] * (depth - 1)
    body = partial(deal_kernel, count=len(parts), depth=depth, halves=devices == 8)
    mine = whole(body, outs, [pltpu.VMEM(shape, F32)], n_in=len(parts), name="deal")(*parts)
    return [mine[0]] + [hop(part, "grp", k) for k, part in enumerate(mine) if k]


def join_kernel(*refs, depth, half):
    part_a, part_b = refs[:depth], refs[depth : 2 * depth]
    part_c, out, c_scr = refs[2 * depth : 2 * depth + half], refs[-2], refs[-1]
    a, b = part_a[0][...], part_b[0][...]
    for k in range(1, depth):
        a, b = a + part_a[k][...].astype(F32), b + part_b[k][...].astype(F32)
    c = part_c[0][...]
    for other in part_c[1:]:
        c = c + other[...]
    rows, lanes = out.shape[0], a.shape[1]
    for j in range(a.shape[0] // rows):
        out[:, j * lanes : (j + 1) * lanes] = a[j * rows : (j + 1) * rows, :].astype(BF)
    at = a.shape[0] // rows * lanes
    out[:, at : at + b.shape[1]] = b.astype(BF)
    at += b.shape[1]
    c_scr[...] = jnp.zeros_like(c_scr)
    c_scr[0 : c.shape[0], :] = c
    for j in range(c_scr.shape[0] // rows):
        out[:, at + j * TILE : at + (j + 1) * TILE] = c_scr[j * rows : (j + 1) * rows, :].astype(BF)


def join(sum_a, sum_b, parts_c):
    depth, rows = len(sum_a), sum_b[0].shape[0]
    blocks_c = ceil_div(ROWS_SMALL, rows)
    wide = sum_a[0].shape[0] // rows * sum_a[0].shape[1] + sum_b[0].shape[1] + blocks_c * TILE
    mine = whole(
        partial(join_kernel, depth=depth, half=len(parts_c)), struct((rows, wide), BF),
        [pltpu.VMEM((blocks_c * rows, TILE), F32)],
        n_in=2 * depth + len(parts_c), name="join",
    )(*sum_a, *sum_b, *parts_c)
    return [mine] + [hop(mine, "grp", k) for k in range(1, depth)]


def final_kernel(*refs, depth, plan, held, dims):
    ins, (attend, down, up, value, mix) = refs[:depth], refs[depth : depth + 5]
    decs, vectors = refs[depth + 5 : depth + 9], refs[depth + 9 : -2]
    scr, c_scr = refs[-2:]
    grp, me = lax.axis_index("grp"), lax.axis_index("seq")
    for k in range(depth):
        scr[grp ^ k] = ins[k][...].astype(F32)
    rows, width = scr.shape[1], attend.shape[1]
    wide, nv = 2 * width, value.shape[1]
    folds = attend.shape[0] // depth // rows
    for z in range(depth):
        for j in range(folds):
            at = (z * folds + j) * rows
            attend[at : at + rows, :] = scr[z, :, j * wide : j * wide + width]
            down[at : at + rows, :] = scr[z, :, j * wide + width : (j + 1) * wide]
        at = folds * wide
        here = slice(z * rows, (z + 1) * rows)
        up[here, :] = scr[z, :, at : at + wide]
        at += wide
        value[here, :] = scr[z, :, at : at + nv]
        mix[here, :] = scr[z, :, at + nv : at + nv + mix.shape[1]]
    at = (folds + 1) * wide + nv + mix.shape[1]
    for j in range(c_scr.shape[0] // rows):
        cols = slice(at + j * TILE, at + (j + 1) * TILE)
        block = scr[0, :, cols]
        for z in range(1, depth):
            block = block + scr[z, :, cols]
        c_scr[j * rows : (j + 1) * rows, :] = block
    total = c_scr[...]
    pick = pick_lanes(me, held, TILE)
    for j, dec in enumerate(decs):
        dec[...] = lax.dot_general(
            total[j * dims : (j + 1) * dims, :], pick, NT,
            precision=lax.Precision.HIGHEST, preferred_element_type=F32,
        )
    for out, (at, count, n, nt) in zip(vectors, plan):
        lanes = nt * TILE
        for i in range(count):
            values = [total[at + i + j : at + i + j + 1, :] for j in range(nt)]
            values = values[0] if nt == 1 else jnp.concatenate(values, axis=1)
            values = jnp.broadcast_to(values, (SUBS, lanes))
            moved = pltpu.roll(values, (lanes - (me * n) % TILE) % lanes, 1)
            if count == 1:
                out[...] = moved[0:1, 0:n].reshape(n)
            else:
                out[i : i + 1, :] = moved[0:1, 0:n]


def near_pieces(x, devices):
    return [x] + [hop(x, "seq", 2 * k) for k in range(1, devices // 2)]


def bundle_kernel(*refs, halves):
    ins, out = refs[:-1], refs[-1]
    for k, ref in enumerate(ins[: out.shape[0] - halves]):
        out[k] = ref[...]
    if halves:
        rows = out.shape[1] // 2
        out[out.shape[0] - 1, 0:rows, :] = ins[-2][...]
        out[out.shape[0] - 1, rows:, :] = ins[-1][...]


def bundle(parts, halves=0):
    shape = (len(parts) - halves,) + parts[0].shape
    return whole(
        partial(bundle_kernel, halves=halves), struct(shape, parts[0].dtype), n_in=len(parts),
        name="bundle",
    )(*parts)


def with_far(both):
    return [both, hop(both, "seq", 1)]


def relay_kernel(x, y, top, bottom):
    rows = top.shape[0]
    top[...] = x[0:rows, :]
    bottom[...] = y[rows:, :]


def relay(x, y):
    half = struct((x.shape[0] // 2, x.shape[1]), x.dtype)
    top, bottom = whole(relay_kernel, [half, half], n_in=2, name="relay")(x, y)
    return [hop(top, "seq", 4), hop(bottom, "seq", 2)]


def first_pieces(x, devices):
    near = 3 if devices == 8 else devices // 2
    return [x] + [hop(x, "seq", 2 * k) for k in range(1, near)]


def more_pieces(parts, devices, *first):
    if devices != 8:
        return parts
    x, y = after(parts[1:3], *first)
    return parts + relay(x, y)


def after(x, *first):
    return lax.optimization_barrier((x, first))[0]


def per_device(
    tokens, segments, cotangent, first_gain, value_weight, value_bias, decay_alpha, decay_delta,
    decay_beta, decay_eta, skip_omega, mix_weight, mix_bias, latent_gains, query_offset,
    position_bias, attend_weight, second_gain, up_weight, up_bias, down_weight, down_bias,
):
    devices = lax.axis_size("seq")
    depth = lax.axis_size("grp")
    seqs, length, width = tokens.shape
    count = seqs * length
    steps = count // SUBS
    dims = decay_alpha.shape[1]
    nv = value_weight.shape[1]
    nf = up_weight.shape[1]
    nm = mix_weight.shape[1]
    zw = query_offset.shape[0] * devices
    reach = max(1, devices // 4)
    held = width // devices

    vectors = [
        (72, value_bias), (73, up_bias), (80, mix_bias), (64, first_gain), (65, skip_omega),
        (66, second_gain), (67, down_bias), (74, latent_gains), (76, query_offset),
        (77, position_bias),
    ]
    plan = []
    for at, v in vectors:
        n = v.shape[-1]
        plan.append((at, v.ndim, n, spread(n, devices)))
    decs = [d.T for d in (decay_alpha, decay_delta, decay_beta, decay_eta)]
    placed = whole(
        partial(place_kernel, plan=plan), struct((ROWS_SMALL, TILE), F32),
        n_in=4 + len(vectors), name="place", vmem=60,
    )(*decs, *[v for _, v in vectors])
    near = near_pieces(placed, devices)
    small = with_far(bundle(near))

    w1, w2 = whole(
        pack_kernel,
        [struct((held, nv + nm), BF), struct((nv // devices + held, 2 * width), BF)],
        n_in=5,
        name="pack",
        vmem=60,
    )(*lax.optimization_barrier(
        (value_weight, mix_weight, attend_weight, down_weight, up_weight, placed)
    )[:5])
    w1 = first_pieces(after(w1, near[1:]), devices)

    tok = tokens.reshape(count, width)
    cot = cotangent.reshape(count, width)
    blocks = width // TILE
    msg_rows = dims * seqs + 16
    pd, pv, pz, pm, dk, nrm, nlow, lab, fin, msg = whole(
        partial(head_kernel, devices=devices, dims=dims, nv=nv, nm=nm),
        [
            struct((72, width), F32), struct((8, nv), F32), struct((8, TILE), F32),
            struct((8, nm), F32), struct((3 * dims, width), F32), struct((blocks, count, TILE), F32),
            struct((count, width), BF), struct((count, TILE), F32),
            struct((dims * SUBS, width), F32), struct((msg_rows, width), BF),
        ],
        [pltpu.VMEM((dims * SUBS, TILE), F32), pltpu.VMEM((devices, ROWS_SMALL, TILE), F32)]
        + [padded(steps)] * 2,
        n_in=4,
        name="head",
        micros=6,
    )(*small, tok, segments)

    onward = [
        lax.ppermute(msg, "seq", [(i, i + k) for i in range(devices - k)])
        for k in range(1, reach + 1)
    ]

    halves = 1 if devices == 8 else 0
    w1 = more_pieces(w1, devices, msg)
    w1 = with_far(bundle(after(w1, onward), halves))
    w2 = first_pieces(after(w2, w1[0]), devices)
    nrm = after(nrm, w1[0])
    arrivals = [pltpu.VMEM((dims * SUBS, TILE), F32)] * reach
    z, mlow, sp = whole(
        partial(scan_kernel, reach=reach, dims=dims, seqs=seqs),
        [
            struct((count, width), F32), struct((count, width), BF),
            struct((blocks, steps, dims * SUBS, TILE), BF),
        ],
        [
            pltpu.VMEM((dims * SUBS, TILE), F32), pltpu.VMEM((SUBS, TILE), F32),
            pltpu.VMEM((blocks, count, TILE), F32),
        ] + [padded(steps)] * 3 + arrivals,
        n_in=5 + reach,
        name="scan",
        micros=8,
    )(nrm, lab, dk, pd, fin, *onward)

    w2 = more_pieces(w2, devices, z)

    def sems(n):
        return pltpu.SemaphoreType.DMA((n, devices))

    vlow, dval, upd, ext, lat, rs, ad, glow, probs, qlow, klow = whole(
        partial(front_kernel, devices=devices),
        [
            struct((count, nv), BF), struct((count, nv), BF), struct((count, width), F32),
            struct((count, width), F32), struct((count, zw), F32), struct((count, nv), BF),
            struct((count, nv), BF), struct((count, nv), BF), struct((count, length), F32),
            struct((count, zw), BF), struct((count, zw), BF),
        ],
        [pltpu.VMEM((width, nv + nm), BF), pltpu.VMEM((count, nv), F32), sems(1)],
        in_specs=[HB] * 2 + [VM] * 7,
        name="front",
        micros=11,
    )(*w1, nlow, mlow, pv, pm, pz, lab, segments)

    w2 = with_far(bundle(after(w2, glow), halves))
    half = devices // 2
    rows2, rows1 = nv // devices // depth, held // depth
    piece_a = struct((half, depth, rows2 + rows1, 2 * width), BF)
    out, gin, attg, blu, blre, v512, v1024, own_a, sib_a = whole(
        partial(middle_kernel, devices=devices, depth=depth, dims=dims),
        [
            struct((count, width), F32), struct((count, width), F32), struct((count, nv), BF),
            struct((count, width), BF), struct((count, nv + width), BF), struct((8, width), F32),
            struct((8, nv), F32), piece_a, piece_a,
        ],
        [
            pltpu.VMEM((nv, 2 * width), BF), pltpu.VMEM((width, nf), BF),
            pltpu.VMEM((count, width), F32), pltpu.VMEM((count, width), F32),
            pltpu.VMEM((count, width), BF), pltpu.VMEM((count, nf), F32),
            pltpu.VMEM((count, nf), BF), pltpu.VMEM((count, width), BF),
            pltpu.VMEM((count, nf), BF), pltpu.VMEM((count, width), BF),
            pltpu.VMEM((count, width), F32), pltpu.VMEM((nv, 2 * width), BF), sems(2),
        ],
        in_specs=[HB] * 2 + [VM] * 9,
        name="middle",
        micros=19,
    )(*w2, tok, cot, upd, ext, rs, ad, glow, pd, pv)

    vgl, bll, gs, gnp, w512, w1024, w128, back_msg, ach = whole(
        partial(back_kernel, devices=devices, dims=dims),
        [
            struct((count, nv), BF), struct((count, zw), BF), struct((blocks, count, TILE), F32),
            struct((blocks, count, TILE), F32), struct((8, width), F32), struct((8, nv), F32),
            struct((8, TILE), F32), struct((msg_rows, width), BF),
            struct((dims * SUBS, width), F32),
        ],
        [
            pltpu.VMEM((width, nv + nm), BF), pltpu.VMEM((count, zw), F32),
            pltpu.VMEM((count, zw), F32), pltpu.VMEM((dims * SUBS, TILE), F32), sems(1),
            padded(steps), padded(steps),
        ],
        in_specs=[HB] * 2 + [VM] * 15,
        name="back",
        micros=15,
    )(*w1, probs, attg, vlow, dval, qlow, klow, lat, blu, blre, z, nrm, pd, pz, dk, lab)

    got_a = hop(sib_a, "seq", 1)
    back_msg = after(back_msg, got_a)
    backward = [
        lax.ppermute(back_msg, "seq", [(i + k, i) for i in range(devices - k)])
        for k in range(1, reach + 1)
    ]

    piece_b = struct((half, depth, rows1, nv + nm), BF)
    own_b, sib_b = whole(
        partial(weight_kernel, devices=devices, depth=depth),
        [piece_b, piece_b],
        [pltpu.VMEM((width, nv + nm), BF)],
        n_in=6,
        name="weights",
        micros=6,
    )(nlow, mlow, vgl, blu, bll, blre)

    _, _, finish_a = spread_sums(after(own_a, backward), got_a, devices)
    tie_b, _, finish_b = spread_sums(own_b, hop(after(sib_b, backward), "seq", 1), devices)
    nrm = after(nrm, tie_b)
    piece_c = struct((half, ROWS_SMALL, TILE), F32)
    wide = ceil_div(nm, TILE) + 2
    tokens_grad, own_c, sib_c = whole(
        partial(last_kernel, reach=reach, devices=devices, dims=dims, seqs=seqs, nm=nm),
        [struct((count, width), F32), piece_c, piece_c],
        [
            pltpu.VMEM((dims * SUBS, TILE), F32), pltpu.VMEM((SUBS, TILE), F32),
            pltpu.VMEM((blocks, count, TILE), F32), pltpu.VMEM((72, width), F32),
            pltpu.VMEM((8, nv), F32), pltpu.VMEM((8, wide * TILE), F32),
            pltpu.VMEM((2 * dims, width), F32),
        ] + [padded(steps)] * 4 + arrivals,
        n_in=15 + reach,
        name="last",
        micros=12,
    )(sp, nrm, gs, gnp, lab, dk, ach, *backward, tok, gin, pd, v512, v1024, w512, w1024, w128)

    sum_a = deal(finish_a(own_c), depth, devices)
    sum_b = deal(finish_b(own_c), depth, devices)
    parts_c = across(fold(after(own_c, sum_b[0]), hop(sib_c, "seq", 1), F32))
    everything = join(sum_a, sum_b, parts_c)
    grads = whole(
        partial(final_kernel, depth=depth, plan=plan, held=held, dims=dims),
        [
            struct((nv // devices, width), F32), struct((nf // devices, width), F32),
            struct((held, nf), F32), struct((held, nv), F32), struct((held, nm), F32),
        ] + [struct((dims, held), F32)] * 4 + [struct(v.shape, F32) for _, v in vectors],
        [
            pltpu.VMEM((depth,) + everything[0].shape, F32),
            pltpu.VMEM((ceil_div(ROWS_SMALL, rows1) * rows1, TILE), F32),
        ],
        n_in=depth,
        name="final",
    )(*everything)
    attend_grad, down_grad, up_grad, value_grad, mix_grad = grads[:5]
    alpha_g, delta_g, beta_g, eta_g = grads[5:9]
    value_b, up_b, mix_b, first_g, omega, second_g, down_b, gains_g, qoff, posb = grads[9:]
    return (
        out.reshape(tokens.shape),
        tokens_grad.reshape(tokens.shape),
        first_g,
        value_grad,
        value_b,
        alpha_g.T,
        delta_g.T,
        beta_g.T,
        eta_g.T,
        omega,
        mix_grad,
        mix_b,
        gains_g,
        qoff,
        posb,
        attend_grad,
        second_g,
        up_grad,
        up_b,
        down_grad,
        down_b,
    )


def solution(mesh):
    vec, mat = P("seq"), P("seq", None)
    data = P("grp", "seq", None)
    params = (
        vec, mat, vec, mat, mat, mat, mat, vec, mat, vec, P(None, "seq"), vec, vec, mat, vec, mat,
        vec, mat, vec,
    )
    return jax.shard_map(
        per_device,
        mesh=mesh,
        in_specs=(data, P("grp", "seq"), data) + params,
        out_specs=(data, data) + params,
        check_vma=False,
    )
```
